32 devices in a mesh: groups: 2 (over y), wide: 8 (over z, x), narrow: 2 (over core).
Axes of the slice: x: 2, y: 2, z: 4, core: 2. Of those that a mesh axis runs over, the one named last changes fastest.
Arguments:
- features: bfloat16 [1024, 128, 128], P(('groups', 'wide'), 'narrow'), parts along dimension 0, may hold values from -6 to 6
- cotangent: bfloat16 [1024, 128, 128], P(('groups', 'wide'), 'narrow'), parts along dimension 0, may hold values from -6 to 6
- down_weight: bfloat16 [3, 3, 128, 128], replicated, may hold values from -0.1875 to 0.1875
- down_bias: float32 [128], replicated, may hold values from -3 to 3
- up_weight: bfloat16 [3, 3, 128, 128], replicated, may hold values from -0.1875 to 0.1875
Outputs:
- feature_grad: bfloat16 [1024, 128, 128], P(('groups', 'wide'), 'narrow'), parts along dimension 0
- down_grad: float32 [6, 3, 128, 128], P('groups'), parts along dimension 0
- up_grad: float32 [6, 3, 128, 128], P('groups'), parts along dimension 0
- bias_grad: float32 [256], P('groups'), parts along dimension 0
The draws below stay inside these ranges and needn't reach their ends.
There are 2 independent parts, one for each index of `groups`. The reference program is written for one: setup_inputs(seed, part) draws one part's arguments, and reference() takes and returns one part's arrays. A program takes and returns all parts, laid end to end along the dimension named above; an argument that names none is the same for every part. Nothing has to cross between parts.
All inputs are finite; a program needn't handle non-finite values.
Results may differ from the reference program's by a relative error of at most 0.0055.
Values may be sent and summed in bfloat16 or wider, within the bound.
No kernel may reach another device: no remote copies, remote signals or barrier semaphores. Data moves between devices by JAX's collectives and lax.ppermute only.
A program may use at most 64 MiB of HBM per device.

```python
import jax
import jax.numpy as jnp
from jax import lax

C = 128
H = 512
W = 128


def steps_of(key, dims, shards, smallest, high):
    factor_of, own = 1.0, jax.random.fold_in(key, 6)
    for position, shards_of in shards:
        draws = jnp.exp(jax.random.uniform(jax.random.fold_in(own, position), (shards_of,), jnp.float32, smallest / len(shards), high / len(shards)))
        factor_of = factor_of * jnp.repeat(draws, dims[position] // shards_of).reshape([-1 if axis == position else 1 for axis in range(len(dims))])
    return factor_of


def normal_values(stream_key, extent, width, reach, split=(), held_as=jnp.bfloat16):
    level = steps_of(stream_key, extent, split, -0.22, 0.18) if split else 1.0
    result = jax.random.normal(stream_key, extent, jnp.float32) * width * level
    return jnp.minimum(jnp.maximum(result, -reach), reach).astype(held_as)


def setup_inputs(seed: int = 0, part: int = 0) -> dict:
    keys = jax.random.split(jax.random.key(seed), 6)
    own_keys = jax.random.split(jax.random.fold_in(keys[5], part), 6)
    return {
        "features": normal_values(own_keys[0], (H, W, C), 1.0, 6.0, ((0, 8), (1, 2))),
        "cotangent": normal_values(own_keys[1], (H, W, C), 1.0, 6.0, ((0, 8), (1, 2))),
        "down_weight": normal_values(keys[2], (3, 3, C, C), (9 * C) ** -0.5, 0.1875),
        "down_bias": normal_values(keys[3], (C,), 0.5, 3.0, (), jnp.float32),
        "up_weight": normal_values(keys[4], (3, 3, C, C), (9 * C) ** -0.5, 0.1875),
    }


def patches(extended, half_rows, half_cols):
    pieces = [extended[row_off:row_off + 2 * half_rows:2, col_off:col_off + 2 * half_cols:2] for row_off in range(3) for col_off in range(3)]
    channels = extended.shape[2]
    return jnp.concatenate(pieces, axis=2).reshape(half_rows * half_cols, 9 * channels)

def spread(terms, half_rows, half_cols, channels):
    terms = terms.reshape(half_rows, half_cols, 9, channels)
    row_parts = []
    for row_par in range(2):
        col_parts = []
        for col_par in range(2):
            summed = jnp.zeros((half_rows + 1, half_cols + 1, channels), jnp.float32)
            for row_off in range(3):
                for col_off in range(3):
                    if row_off % 2 == row_par and col_off % 2 == col_par:
                        summed = summed + jnp.pad(terms[:, :, row_off * 3 + col_off], ((row_off // 2, 1 - row_off // 2), (col_off // 2, 1 - col_off // 2), (0, 0)))
            col_parts.append(summed)
        row_parts.append(jnp.stack(col_parts, axis=2))
    spread_out = jnp.stack(row_parts, axis=1).reshape(2 * half_rows + 2, 2 * half_cols + 2, channels)
    return spread_out[:2 * half_rows + 1, :2 * half_cols + 1]

def reference(features, cotangent, down_weight, down_bias, up_weight):
    total_rows, total_cols, channels = features.shape
    half_rows = total_rows // 2
    half_cols = total_cols // 2
    feat_ext = jnp.pad(features, ((1, 0), (1, 0), (0, 0)))
    cot_ext = jnp.pad(cotangent, ((1, 0), (1, 0), (0, 0)))
    feat_patch = patches(feat_ext, half_rows, half_cols)
    cot_patch = patches(cot_ext, half_rows, half_cols)
    pre_act = jnp.dot(feat_patch, down_weight.reshape(9 * channels, channels), preferred_element_type=jnp.float32) + down_bias
    activated = jax.nn.silu(pre_act).astype(jnp.bfloat16)
    up_trans = up_weight.reshape(9, channels, channels).transpose(0, 2, 1).reshape(9 * channels, channels)
    act_grad = jnp.dot(cot_patch, up_trans, preferred_element_type=jnp.float32)
    sigm = jax.nn.sigmoid(pre_act)
    pre_grad = (act_grad * sigm * (1.0 + pre_act * (1.0 - sigm))).astype(jnp.bfloat16)
    raw_up = lax.dot_general(activated, cot_patch, (((0,), (0,)), ((), ())), preferred_element_type=jnp.float32)
    raw_up = raw_up.reshape(channels, 9, channels).transpose(1, 0, 2).reshape(3, 3, channels, channels)
    raw_down = lax.dot_general(feat_patch, pre_grad, (((0,), (0,)), ((), ())), preferred_element_type=jnp.float32)
    raw_down = raw_down.reshape(3, 3, channels, channels)
    raw_bias = lax.optimization_barrier(jnp.sum(pre_grad.astype(jnp.float32), axis=0))
    down_trans = down_weight.reshape(9, channels, channels).transpose(2, 0, 1).reshape(channels, 9 * channels)
    terms = jnp.dot(pre_grad, down_trans, preferred_element_type=jnp.float32)
    spread_out = spread(terms, half_rows, half_cols, channels)
    feature_grad = (cotangent.astype(jnp.float32) + spread_out[1:, 1:]).astype(jnp.bfloat16)
    square_sum = jnp.sum(raw_down * raw_down) + jnp.sum(raw_up * raw_up) + jnp.sum(raw_bias * raw_bias)
    clip_level = 0.5 * jnp.sqrt(jnp.float32(18 * channels * channels + channels))
    factor = jnp.minimum(1.0, clip_level / jnp.sqrt(square_sum))
    return (feature_grad, raw_down * factor, raw_up * factor, raw_bias * factor)
```

```python
import functools

import jax
import jax.numpy as jnp
from jax import lax
from jax.experimental import pallas as pl
from jax.experimental.pallas import tpu as pltpu
from jax.sharding import PartitionSpec as P

F32 = jnp.float32
BF16 = jnp.bfloat16
VM = pl.BlockSpec(memory_space=pltpu.VMEM)
ANY = pl.BlockSpec(memory_space=pl.ANY)
SIDE = 16


def call(body, out_shape, scratch=(), in_specs=None, n_in=0, flops=0, nbytes=0, name=None):
    return pl.pallas_call(
        body,
        out_shape=out_shape,
        in_specs=in_specs if in_specs is not None else [VM] * n_in,
        out_specs=jax.tree.map(lambda _: VM, out_shape),
        scratch_shapes=list(scratch),
        name=name,
        cost_estimate=pl.CostEstimate(flops=flops, transcendentals=0, bytes_accessed=nbytes),
    )


def sds(shape, dtype):
    return jax.ShapeDtypeStruct(shape, dtype)


def edge_body(feat, cot, rows, cols, strip, wide_strip, sems):
    tile_rows, tile_cols, _ = feat.shape
    copies = []
    for which, ref in enumerate((feat, cot)):
        copies.append(
            pltpu.make_async_copy(ref.at[tile_rows - 1], rows.at[which], sems.at[2 * which])
        )
        copies.append(
            pltpu.make_async_copy(
                ref.at[:, pl.ds(tile_cols - 16, 16), :], strip.at[which], sems.at[2 * which + 1]
            )
        )
    for copy in copies:
        copy.start()
    for copy in copies:
        copy.wait()
    for which in range(2):
        wide_strip[...] = strip[which].astype(F32).reshape(wide_strip.shape)
        cols[which] = wide_strip[pl.ds(15, tile_rows, stride=16), :].astype(BF16)


def phase_body(tile, out, wide):
    rows, cols, channels = tile.shape
    wide[:, 0:8, :] = jnp.zeros((rows, 8, channels), F32)
    wide[:, 8:, :] = tile[...].astype(F32)
    for col_off in range(3):
        out[col_off] = wide[:, pl.ds(7 + col_off, cols // 2, stride=2), :].astype(BF16)


def fill_patches(phases, top, left, patch, line, column):
    _, rows, half_cols, channels = phases.shape
    half_rows = rows // 2
    line[0:8, :] = jnp.broadcast_to(left[0:1, :].astype(F32), (8, channels))
    line[8:, :] = top[...].astype(F32)
    column[...] = left[...].astype(F32)
    first = lax.broadcasted_iota(jnp.int32, (half_rows, half_cols, channels), 1) == 0
    paired = phases.reshape(3, half_rows, 2, half_cols, channels)
    for col_off in range(3):
        lanes = [pl.ds((3 * row_off + col_off) * channels, channels) for row_off in range(3)]
        even = paired[col_off, :, 0].astype(F32) if col_off == 0 else paired[col_off, :, 0]
        odd = paired[col_off, :, 1].astype(F32) if col_off == 0 else paired[col_off, :, 1]
        if col_off == 0:
            rim = [
                column[pl.ds(off, half_rows, stride=2), :].reshape(half_rows, 1, channels)
                for off in (1, 2)
            ]
            even = jnp.where(first, rim[0], even).astype(BF16)
            odd = jnp.where(first, rim[1], odd).astype(BF16)
        patch[:, :, lanes[1]] = even
        patch[:, :, lanes[2]] = odd
        patch[1:, :, lanes[0]] = odd[:-1]
        patch[0, :, lanes[0]] = line[pl.ds(7 + col_off, half_cols, stride=2), :].astype(BF16)


def main_body(
    feat_phases, cot_phases, top, left, down_weight, down_bias, up_weight,
    grads, first_row, first_col, mine, other, bias_part,
    feat_patch, cot_patch, up_mat, act, wide_grads, line, column,
):
    _, rows, half_cols, channels = feat_phases.shape
    half_rows = rows // 2
    pixels = half_rows * half_cols
    taps = 9 * channels
    fill_patches(feat_phases, top.at[0], left.at[0], feat_patch, line, column)
    fill_patches(cot_phases, top.at[1], left.at[1], cot_patch, line, column)
    for tap in range(9):
        up_mat[:, pl.ds(tap * channels, channels)] = up_weight[tap // 3, tap % 3]
    down_mat = down_weight[...].reshape(taps, channels)
    bias_row = down_bias[...].reshape(1, channels)
    step = 8
    for start in range(0, half_rows, step):
        span = pl.ds(start * half_cols, step * half_cols)
        feat_rows = feat_patch[start : start + step].reshape(step * half_cols, taps)
        cot_rows = cot_patch[start : start + step].reshape(step * half_cols, taps)
        pre = jnp.dot(feat_rows, down_mat, preferred_element_type=F32) + bias_row
        act_grad = lax.dot_general(
            cot_rows, up_mat[...], (((1,), (1,)), ((), ())), preferred_element_type=F32
        )
        sigm = 1.0 / (1.0 + jnp.exp(-pre))
        act[span, :] = (pre * sigm).astype(BF16)
        pre_grad = (act_grad * sigm * (1.0 + pre * (1.0 - sigm))).astype(BF16)
        grads[span, :] = pre_grad
        wide_grads[span, :] = pre_grad.astype(F32)
    first_row[...] = grads[0:half_cols, :]
    first_col[...] = wide_grads[pl.ds(0, half_rows, stride=half_cols), :].astype(BF16)
    raw_bias = jnp.sum(wide_grads[...], axis=0, keepdims=True)
    coarse = raw_bias.astype(BF16)
    fine = (raw_bias - coarse.astype(F32)).astype(BF16)
    bias_part[...] = jnp.broadcast_to(coarse.astype(F32) + fine.astype(F32), bias_part.shape)
    put_side(other, taps, coarse, fine)
    raw_up = lax.dot_general(
        act[...], cot_patch[...].reshape(pixels, taps), (((0,), (0,)), ((), ())),
        preferred_element_type=F32,
    )
    raw_down = lax.dot_general(
        feat_patch[...].reshape(pixels, taps), grads[...], (((0,), (0,)), ((), ())),
        preferred_element_type=F32,
    )
    core = lax.axis_index("narrow")

    @pl.when(core == 0)
    def _():
        mine[...] = raw_down
        for tap in range(9):
            span = pl.ds(tap * channels, channels)
            other[span, :] = raw_up[:, tap * channels : (tap + 1) * channels].astype(BF16)

    @pl.when(core != 0)
    def _():
        other[0:taps, :] = raw_down.astype(BF16)
        for tap in range(9):
            span = pl.ds(tap * channels, channels)
            mine[span, :] = raw_up[:, tap * channels : (tap + 1) * channels]


def put_side(out, at, coarse, fine):
    channels = out.shape[1]
    row = lax.broadcasted_iota(jnp.int32, (SIDE, channels), 0)
    block = jnp.where(row == 0, coarse.astype(F32), jnp.where(row == 1, fine.astype(F32), 0.0))
    out[at : at + SIDE, :] = block.astype(BF16)


def take_side(ref, at):
    block = ref[at : at + SIDE, :].astype(F32)
    return block[0:1] + block[1:2]


def bit_of(position):
    low, high = position
    at = lax.axis_index("wide")
    shift = jnp.where(lax.axis_index("narrow") == 0, low, high)
    return lax.rem(lax.shift_right_logical(at, shift.astype(at.dtype)), 2)


def joined_bias(bias_in, got, size, out, sent, at):
    total = bias_in[0:1, :] + take_side(got, size)
    coarse = total.astype(BF16)
    fine = (total - coarse.astype(F32)).astype(BF16)
    out[...] = jnp.broadcast_to(coarse.astype(F32) + fine.astype(F32), out.shape)
    if sent is not None:
        put_side(sent, at, coarse, fine)


def halve_body(position, held, got, bias_in, keep, send, bias_out):
    size = held.shape[0]
    half = size // 2
    bit = bit_of(position)
    near = pl.ds(pl.multiple_of(bit * half, 16), half)
    away = pl.ds(pl.multiple_of((1 - bit) * half, 16), half)
    send[0:half, :] = (held[away, :] + got[away, :].astype(F32)).astype(BF16)
    keep[...] = held[near, :] + got[near, :].astype(F32)
    joined_bias(bias_in, got, size, bias_out, send, half)


def whole_body(held, got, bias_in, send, bias_out):
    size = got.shape[0] - SIDE
    send[0:size, :] = (held[0:size, :].astype(F32) + got[0:size, :].astype(F32)).astype(BF16)
    joined_bias(bias_in, got, size, bias_out, send, size)


def last_body(held, got, bias_in, total, bias_out):
    size = got.shape[0] - SIDE
    total[...] = (held[0:size, :].astype(F32) + got[0:size, :].astype(F32)).astype(BF16)
    joined_bias(bias_in, got, size, bias_out, None, 0)


def place_body(position, held, got, out):
    size = held.shape[0]
    bit = bit_of(position)
    out[pl.ds(pl.multiple_of(bit * size, 16), size), :] = held[...]
    out[pl.ds(pl.multiple_of((1 - bit) * size, 16), size), :] = got[...]


def final_body(held, got, bias_in, down, up, bias_out):
    channels = held.shape[1]
    core = lax.axis_index("narrow")
    squares = jnp.zeros((channels, channels), F32)
    for ref in (held, got):
        part = jnp.zeros((channels, channels), F32)
        for tap in range(9):
            block = ref[tap * channels : (tap + 1) * channels, :].astype(F32)
            part = part + block * block
        squares = squares + part
    bias = bias_in[0:1, :]
    total = jnp.sum(jnp.sum(squares, axis=0, keepdims=True) + bias * bias, axis=1, keepdims=True)
    clip_level = 0.5 * float(18 * channels * channels + channels) ** 0.5
    factor = jnp.minimum(1.0, clip_level / jnp.sqrt(total))
    factor = jnp.broadcast_to(factor, (1, channels))
    bias_out[...] = bias * factor

    def write(down_ref, up_ref):
        for tap in range(9):
            rows = slice(tap * channels, (tap + 1) * channels)
            down[tap] = down_ref[rows, :].astype(F32) * factor
            up[tap] = up_ref[rows, :].astype(F32) * factor

    @pl.when(core == 0)
    def _():
        write(held, got)

    @pl.when(core != 0)
    def _():
        write(got, held)


def feature_body(grads, right, below, cot, down_weight, out, wide, pairs, near_mat, low_mat, woven):
    tile_rows, tile_cols, channels = cot.shape
    half_rows, half_cols = tile_rows // 2, tile_cols // 2
    wide[0:half_rows, 0:half_cols, :] = grads[...].astype(F32).reshape(
        half_rows, half_cols, channels
    )
    last = lax.broadcasted_iota(jnp.int32, (half_rows, 8, channels), 1) == 0
    rim = right[...].astype(F32).reshape(half_rows, 1, channels)
    wide[0:half_rows, half_cols:, :] = jnp.where(last, rim, 0.0)
    low = below[...].astype(F32)
    wide[half_rows, :, :] = low
    pairs[:, :, 0:channels] = wide[:, 0:half_cols, :].astype(BF16)
    pairs[:, :, channels:] = wide[:, 1 : half_cols + 1, :].astype(BF16)
    zero = jnp.zeros((channels, channels), BF16)
    blocks = [(1, 1, None), (1, 2, 0), (2, 1, None), (2, 2, 0)]
    for at, (row_off, here, next_off) in enumerate(blocks):
        rows = slice(at * channels, (at + 1) * channels)
        near_mat[rows, 0:channels] = down_weight[row_off, here]
        near_mat[rows, channels:] = zero if next_off is None else down_weight[row_off, next_off]
    for at, (here, next_off) in enumerate([(1, None), (2, 0)]):
        rows = slice(at * channels, (at + 1) * channels)
        low_mat[rows, 0:channels] = down_weight[0, here]
        low_mat[rows, channels:] = zero if next_off is None else down_weight[0, next_off]
    step = 8
    dims = (((1,), (1,)), ((), ()))
    for start in range(0, half_rows, step):
        count = step * half_cols
        here = pairs[start : start + step].reshape(count, 2 * channels)
        under = pairs[start + 1 : start + 1 + step].reshape(count, 2 * channels)
        near = lax.dot_general(here, near_mat[...], dims, preferred_element_type=F32)
        far = lax.dot_general(under, low_mat[...], dims, preferred_element_type=F32)
        shape = (step, half_cols, channels)
        for row_par in range(2):
            for col_par in range(2):
                lanes = slice((2 * row_par + col_par) * channels, (2 * row_par + col_par + 1) * channels)
                value = near[:, lanes]
                if row_par:
                    value = value + far[:, col_par * channels : (col_par + 1) * channels]
                woven[:, row_par, pl.ds(col_par, half_cols, stride=2), :] = value.reshape(shape)
        span = slice(2 * start, 2 * (start + step))
        total = cot[span].astype(F32) + woven[...].reshape(2 * step, tile_cols, channels)
        out[span] = total.astype(BF16)


def passed_along(value, axis, steps):
    count = lax.axis_size(axis)
    first, last = (max(0, -steps), min(count, count - steps))
    return lax.ppermute(value, axis, [(source, source + steps) for source in range(first, last)])


def traded(value, position):
    count, cores = lax.axis_size("wide"), lax.axis_size("narrow")
    pairs = []
    for at in range(count):
        for core in range(cores):
            mate = at ^ (1 << position[0 if core == 0 else 1])
            pairs.append((at * cores + core, mate * cores + core))
    return lax.ppermute(value, ("wide", "narrow"), pairs)


def shards(features, cotangent, down_weight, down_bias, up_weight):
    tile_rows, tile_cols, channels = features.shape
    half_rows, half_cols = tile_rows // 2, tile_cols // 2
    pixels = half_rows * half_cols
    taps = 9 * channels
    rows, cols = call(
        edge_body,
        (sds((2, tile_cols, channels), BF16), sds((2, tile_rows, channels), BF16)),
        scratch=[
            pltpu.VMEM((2, tile_rows, 16, channels), BF16),
            pltpu.VMEM((tile_rows * 16, channels), F32),
            pltpu.SemaphoreType.DMA((4,)),
        ],
        in_specs=[ANY, ANY],
        nbytes=1 << 19,
        name="edges",
    )(features, cotangent)
    from_above = passed_along(rows, "wide", 1)
    phases = call(
        phase_body,
        sds((3, tile_rows, half_cols, channels), BF16),
        scratch=[pltpu.VMEM((tile_rows, tile_cols + 8, channels), F32)],
        n_in=1,
        flops=1 << 28,
        nbytes=3 << 20,
        name="phases",
    )
    feat_phases = phases(features)
    cot_phases = phases(cotangent)
    cols = jnp.concatenate(
        [from_above[:, -1:], cols, jnp.zeros((2, 7, channels), BF16)], axis=1
    )
    from_left = passed_along(cols, "narrow", 1)
    grads, first_row, first_col, mine, other, bias_sum = call(
        main_body,
        (
            sds((pixels, channels), BF16),
            sds((half_cols, channels), BF16),
            sds((half_rows, channels), BF16),
            sds((taps, channels), F32),
            sds((taps + SIDE, channels), BF16),
            sds((8, channels), F32),
        ),
        scratch=[
            pltpu.VMEM((half_rows, half_cols, taps), BF16),
            pltpu.VMEM((half_rows, half_cols, taps), BF16),
            pltpu.VMEM((channels, taps), BF16),
            pltpu.VMEM((pixels, channels), BF16),
            pltpu.VMEM((pixels, channels), F32),
            pltpu.VMEM((tile_cols + 8, channels), F32),
            pltpu.VMEM((tile_rows + 8, channels), F32),
        ],
        n_in=7,
        flops=8 * pixels * taps * channels,
        nbytes=6 << 20,
        name="main",
    )(feat_phases, cot_phases, from_above, from_left, down_weight, down_bias, up_weight)

    got = lax.ppermute(other, "narrow", [(0, 1), (1, 0)])

    from_right = passed_along(first_col, "narrow", -1)
    low_row = jnp.concatenate(
        [first_row, from_right[:1], jnp.zeros((7, channels), BF16)], axis=0
    )
    from_below = passed_along(low_row, "wide", -1)
    feature_grad = call(
        feature_body,
        sds((tile_rows, tile_cols, channels), BF16),
        scratch=[
            pltpu.VMEM((half_rows + 1, half_cols + 8, channels), F32),
            pltpu.VMEM((half_rows + 1, half_cols, 2 * channels), BF16),
            pltpu.VMEM((4 * channels, 2 * channels), BF16),
            pltpu.VMEM((2 * channels, 2 * channels), BF16),
            pltpu.VMEM((8, 2, tile_cols, channels), F32),
        ],
        n_in=5,
        flops=2 * pixels * 6 * 2 * channels * channels,
        nbytes=3 << 20,
        name="feature",
    )(grads, from_right, from_below, cotangent, down_weight)

    count = lax.axis_size("wide")
    bits = count.bit_length() - 1
    order = [(bit, bit) for bit in range(bits)]
    if bits > 1:
        order[0], order[1] = (0, 1), (1, 0)
    halvings = min(bits - 1, 3)
    held = mine
    for step in range(halvings):
        half = held.shape[0] // 2
        held, send, bias_sum = call(
            functools.partial(halve_body, order[step]),
            (sds((half, channels), F32), sds((half + SIDE, channels), BF16), sds((8, channels), F32)),
            n_in=3,
            nbytes=held.size * 4,
            name="halve",
        )(held, got, bias_sum)
        got = traded(send, order[step])
    for step in range(halvings, bits):
        size = held.shape[0] if step == halvings else held.shape[0] - SIDE
        send, bias_sum = call(
            whole_body,
            (sds((size + SIDE, channels), BF16), sds((8, channels), F32)),
            n_in=3,
            nbytes=held.size * 4,
            name="whole",
        )(held, got, bias_sum)
        got = traded(send, order[step])
        held = send
    size = got.shape[0] - SIDE
    block, bias_sum = call(
        last_body,
        (sds((size, channels), BF16), sds((8, channels), F32)),
        n_in=3,
        nbytes=size * channels * 4,
        name="last",
    )(held, got, bias_sum)
    for step in reversed(range(halvings)):
        got = traded(block, order[step])
        block = call(
            functools.partial(place_body, order[step]),
            sds((2 * block.shape[0], channels), BF16),
            n_in=2,
            nbytes=block.size * 4,
            name="place",
        )(block, got)
    got = lax.ppermute(block, "narrow", [(0, 1), (1, 0)])
    down, up, bias_grad = call(
        final_body,
        (
            sds((9, channels, channels), F32),
            sds((9, channels, channels), F32),
            sds((1, channels), F32),
        ),
        n_in=3,
        nbytes=12 * taps * channels,
        name="final",
    )(block, got, bias_sum)
    shape = (3, 3, channels, channels)
    return (feature_grad, down.reshape(shape), up.reshape(shape), bias_grad.reshape(channels))


def solution(mesh):
    return jax.shard_map(
        shards,
        mesh=mesh,
        in_specs=(
            P(("groups", "wide"), "narrow", None),
            P(("groups", "wide"), "narrow", None),
            P(),
            P(),
            P(),
        ),
        out_specs=(
            P(("groups", "wide"), "narrow", None),
            P("groups", None, None, None),
            P("groups", None, None, None),
            P("groups"),
        ),
        check_vma=False,
    )
```

```python
import functools

import jax
import jax.numpy as jnp
from jax import lax
from jax.experimental import pallas as pl
from jax.experimental.pallas import tpu as pltpu
from jax.sharding import PartitionSpec as P

F32 = jnp.float32
BF16 = jnp.bfloat16
VM = pl.BlockSpec(memory_space=pltpu.VMEM)
ANY = pl.BlockSpec(memory_space=pl.ANY)
SIDE = 16


def call(body, out_shape, scratch=(), in_specs=None, n_in=0, flops=0, nbytes=0, name=None, near=(), far=(), room=4):
    kernel = pl.pallas_call(
        body,
        out_shape=out_shape,
        in_specs=in_specs if in_specs is not None else [VM] * n_in,
        out_specs=jax.tree.map(lambda _: VM, out_shape),
        scratch_shapes=list(scratch),
        name=name,
        compiler_params=pltpu.CompilerParams(vmem_limit_bytes=room << 20),
        cost_estimate=pl.CostEstimate(flops=flops, transcendentals=0, bytes_accessed=nbytes),
    )

    def run(*args):
        placed = [
            pltpu.with_memory_space_constraint(arg, pltpu.VMEM if at in near else pltpu.HBM)
            if at in near or at in far
            else arg
            for at, arg in enumerate(args)
        ]
        return kernel(*placed)

    return run


def vm(shape, dtype):
    return pltpu.VMEM(shape, dtype)


def sds(shape, dtype):
    return jax.ShapeDtypeStruct(shape, dtype)


def edge_body(feat, cot, rows, cols, strip, wide_strip, sems):
    tile_rows, tile_cols, _ = feat.shape
    copies = []
    for which, ref in enumerate((feat, cot)):
        copies.append(
            pltpu.make_async_copy(ref.at[tile_rows - 1], rows.at[which], sems.at[2 * which])
        )
        copies.append(
            pltpu.make_async_copy(
                ref.at[:, pl.ds(tile_cols - 16, 16), :], strip.at[which], sems.at[2 * which + 1]
            )
        )
    for copy in copies:
        copy.start()
    for copy in copies:
        copy.wait()
    for which in range(2):
        wide_strip[...] = strip[which].astype(F32).reshape(wide_strip.shape)
        cols[which] = wide_strip[pl.ds(15, tile_rows, stride=16), :].astype(BF16)


def phase_body(tile, out, wide):
    rows, cols, channels = tile.shape
    wide[:, 0:8, :] = jnp.zeros((rows, 8, channels), F32)
    wide[:, 8:, :] = tile[...].astype(F32)
    for col_off in range(3):
        out[col_off] = wide[:, pl.ds(7 + col_off, cols // 2, stride=2), :].astype(BF16)


def fill_patches(phases, top, left, patch, line, column):
    _, rows, half_cols, channels = phases.shape
    half_rows = rows // 2
    line[0:8, :] = jnp.broadcast_to(left[0:1, :].astype(F32), (8, channels))
    line[8:, :] = top[...].astype(F32)
    column[...] = left[...].astype(F32)
    first = lax.broadcasted_iota(jnp.int32, (half_rows, half_cols, channels), 1) == 0
    paired = phases.reshape(3, half_rows, 2, half_cols, channels)
    for col_off in range(3):
        lanes = [pl.ds((3 * row_off + col_off) * channels, channels) for row_off in range(3)]
        even = paired[col_off, :, 0].astype(F32) if col_off == 0 else paired[col_off, :, 0]
        odd = paired[col_off, :, 1].astype(F32) if col_off == 0 else paired[col_off, :, 1]
        if col_off == 0:
            rim = [
                column[pl.ds(off, half_rows, stride=2), :].reshape(half_rows, 1, channels)
                for off in (1, 2)
            ]
            even = jnp.where(first, rim[0], even).astype(BF16)
            odd = jnp.where(first, rim[1], odd).astype(BF16)
        patch[:, :, lanes[1]] = even
        patch[:, :, lanes[2]] = odd
        patch[1:, :, lanes[0]] = odd[:-1]
        patch[0, :, lanes[0]] = line[pl.ds(7 + col_off, half_cols, stride=2), :].astype(BF16)


def main_body(
    feat_phases, cot_phases, top, left, down_weight, down_bias, up_weight,
    grads, first_row, first_col, mine, other, bias_part,
    feat_patch, cot_patch, up_mat, act, wide_grads, line, column,
):
    _, rows, half_cols, channels = feat_phases.shape
    half_rows = rows // 2
    pixels = half_rows * half_cols
    taps = 9 * channels
    fill_patches(feat_phases, top.at[0], left.at[0], feat_patch, line, column)
    fill_patches(cot_phases, top.at[1], left.at[1], cot_patch, line, column)
    for tap in range(9):
        up_mat[:, pl.ds(tap * channels, channels)] = up_weight[tap // 3, tap % 3]
    down_mat = down_weight[...].reshape(taps, channels)
    bias_row = down_bias[...].reshape(1, channels)
    step = 8
    for start in range(0, half_rows, step):
        span = pl.ds(start * half_cols, step * half_cols)
        feat_rows = feat_patch[start : start + step].reshape(step * half_cols, taps)
        cot_rows = cot_patch[start : start + step].reshape(step * half_cols, taps)
        pre = jnp.dot(feat_rows, down_mat, preferred_element_type=F32) + bias_row
        act_grad = lax.dot_general(
            cot_rows, up_mat[...], (((1,), (1,)), ((), ())), preferred_element_type=F32
        )
        sigm = 1.0 / (1.0 + jnp.exp(-pre))
        act[span, :] = (pre * sigm).astype(BF16)
        pre_grad = (act_grad * sigm * (1.0 + pre * (1.0 - sigm))).astype(BF16)
        grads[span, :] = pre_grad
        wide_grads[span, :] = pre_grad.astype(F32)
    first_row[...] = grads[0:half_cols, :]
    first_col[...] = wide_grads[pl.ds(0, half_rows, stride=half_cols), :].astype(BF16)
    raw_bias = jnp.sum(wide_grads[...], axis=0, keepdims=True)
    coarse = raw_bias.astype(BF16)
    fine = (raw_bias - coarse.astype(F32)).astype(BF16)
    bias_part[...] = jnp.broadcast_to(coarse.astype(F32) + fine.astype(F32), bias_part.shape)
    put_side(other, taps, coarse, fine)
    raw_up = lax.dot_general(
        act[...], cot_patch[...].reshape(pixels, taps), (((0,), (0,)), ((), ())),
        preferred_element_type=F32,
    )
    raw_down = lax.dot_general(
        feat_patch[...].reshape(pixels, taps), grads[...], (((0,), (0,)), ((), ())),
        preferred_element_type=F32,
    )
    core = lax.axis_index("narrow")

    @pl.when(core == 0)
    def _():
        mine[...] = raw_down
        for tap in range(9):
            span = pl.ds(tap * channels, channels)
            other[span, :] = raw_up[:, tap * channels : (tap + 1) * channels].astype(BF16)

    @pl.when(core != 0)
    def _():
        other[0:taps, :] = raw_down.astype(BF16)
        for tap in range(9):
            span = pl.ds(tap * channels, channels)
            mine[span, :] = raw_up[:, tap * channels : (tap + 1) * channels]


def put_side(out, at, coarse, fine):
    channels = out.shape[1]
    row = lax.broadcasted_iota(jnp.int32, (SIDE, channels), 0)
    block = jnp.where(row == 0, coarse.astype(F32), jnp.where(row == 1, fine.astype(F32), 0.0))
    out[at : at + SIDE, :] = block.astype(BF16)


def take_side(ref, at):
    block = ref[at : at + SIDE, :].astype(F32)
    return block[0:1] + block[1:2]


def bit_of(position):
    low, high = position
    at = lax.axis_index("wide")
    shift = jnp.where(lax.axis_index("narrow") == 0, low, high)
    return lax.rem(lax.shift_right_logical(at, shift.astype(at.dtype)), 2)


def joined_bias(bias_in, got, size, out, sent, at):
    total = bias_in[0:1, :] + take_side(got, size)
    coarse = total.astype(BF16)
    fine = (total - coarse.astype(F32)).astype(BF16)
    out[...] = jnp.broadcast_to(coarse.astype(F32) + fine.astype(F32), out.shape)
    if sent is not None:
        put_side(sent, at, coarse, fine)


def halve_body(position, held, got, bias_in, keep, send, bias_out):
    size = held.shape[0]
    half = size // 2
    bit = bit_of(position)
    near = pl.ds(pl.multiple_of(bit * half, 16), half)
    away = pl.ds(pl.multiple_of((1 - bit) * half, 16), half)
    send[0:half, :] = (held[away, :] + got[away, :].astype(F32)).astype(BF16)
    keep[...] = held[near, :] + got[near, :].astype(F32)
    joined_bias(bias_in, got, size, bias_out, send, half)


def whole_body(held, got, bias_in, send, bias_out):
    size = got.shape[0] - SIDE
    send[0:size, :] = (held[0:size, :].astype(F32) + got[0:size, :].astype(F32)).astype(BF16)
    joined_bias(bias_in, got, size, bias_out, send, size)


def last_body(held, got, bias_in, total, bias_out):
    size = got.shape[0] - SIDE
    total[...] = (held[0:size, :].astype(F32) + got[0:size, :].astype(F32)).astype(BF16)
    joined_bias(bias_in, got, size, bias_out, None, 0)


def place_body(position, held, got, out):
    size = held.shape[0]
    bit = bit_of(position)
    out[pl.ds(pl.multiple_of(bit * size, 16), size), :] = held[...]
    out[pl.ds(pl.multiple_of((1 - bit) * size, 16), size), :] = got[...]


def final_body(held, got, bias_in, down, up, bias_out):
    channels = held.shape[1]
    core = lax.axis_index("narrow")
    squares = jnp.zeros((channels, channels), F32)
    for ref in (held, got):
        part = jnp.zeros((channels, channels), F32)
        for tap in range(9):
            block = ref[tap * channels : (tap + 1) * channels, :].astype(F32)
            part = part + block * block
        squares = squares + part
    bias = bias_in[0:1, :]
    total = jnp.sum(jnp.sum(squares, axis=0, keepdims=True) + bias * bias, axis=1, keepdims=True)
    clip_level = 0.5 * float(18 * channels * channels + channels) ** 0.5
    factor = jnp.minimum(1.0, clip_level / jnp.sqrt(total))
    factor = jnp.broadcast_to(factor, (1, channels))
    bias_out[...] = bias * factor

    def write(down_ref, up_ref):
        for tap in range(9):
            rows = slice(tap * channels, (tap + 1) * channels)
            down[tap] = down_ref[rows, :].astype(F32) * factor
            up[tap] = up_ref[rows, :].astype(F32) * factor

    @pl.when(core == 0)
    def _():
        write(held, got)

    @pl.when(core != 0)
    def _():
        write(got, held)


def feature_body(grads, right, below, cot, down_weight, out, wide, pairs, near_mat, low_mat, woven):
    tile_rows, tile_cols, channels = cot.shape
    half_rows, half_cols = tile_rows // 2, tile_cols // 2
    wide[0:half_rows, 0:half_cols, :] = grads[...].astype(F32).reshape(
        half_rows, half_cols, channels
    )
    last = lax.broadcasted_iota(jnp.int32, (half_rows, 8, channels), 1) == 0
    rim = right[...].astype(F32).reshape(half_rows, 1, channels)
    wide[0:half_rows, half_cols:, :] = jnp.where(last, rim, 0.0)
    low = below[...].astype(F32)
    wide[half_rows, :, :] = low
    pairs[:, :, 0:channels] = wide[:, 0:half_cols, :].astype(BF16)
    pairs[:, :, channels:] = wide[:, 1 : half_cols + 1, :].astype(BF16)
    zero = jnp.zeros((channels, channels), BF16)
    blocks = [(1, 1, None), (1, 2, 0), (2, 1, None), (2, 2, 0)]
    for at, (row_off, here, next_off) in enumerate(blocks):
        rows = slice(at * channels, (at + 1) * channels)
        near_mat[rows, 0:channels] = down_weight[row_off, here]
        near_mat[rows, channels:] = zero if next_off is None else down_weight[row_off, next_off]
    for at, (here, next_off) in enumerate([(1, None), (2, 0)]):
        rows = slice(at * channels, (at + 1) * channels)
        low_mat[rows, 0:channels] = down_weight[0, here]
        low_mat[rows, channels:] = zero if next_off is None else down_weight[0, next_off]
    step = 8
    dims = (((1,), (1,)), ((), ()))
    for start in range(0, half_rows, step):
        count = step * half_cols
        here = pairs[start : start + step].reshape(count, 2 * channels)
        under = pairs[start + 1 : start + 1 + step].reshape(count, 2 * channels)
        near = lax.dot_general(here, near_mat[...], dims, preferred_element_type=F32)
        far = lax.dot_general(under, low_mat[...], dims, preferred_element_type=F32)
        shape = (step, half_cols, channels)
        for row_par in range(2):
            for col_par in range(2):
                lanes = slice((2 * row_par + col_par) * channels, (2 * row_par + col_par + 1) * channels)
                value = near[:, lanes]
                if row_par:
                    value = value + far[:, col_par * channels : (col_par + 1) * channels]
                woven[:, row_par, pl.ds(col_par, half_cols, stride=2), :] = value.reshape(shape)
        span = slice(2 * start, 2 * (start + step))
        total = cot[span].astype(F32) + woven[...].reshape(2 * step, tile_cols, channels)
        out[span] = total.astype(BF16)


def passed_along(value, axis, steps):
    count = lax.axis_size(axis)
    first, last = (max(0, -steps), min(count, count - steps))
    return lax.ppermute(value, axis, [(source, source + steps) for source in range(first, last)])


def traded(value, position):
    count, cores = lax.axis_size("wide"), lax.axis_size("narrow")
    pairs = []
    for at in range(count):
        for core in range(cores):
            mate = at ^ (1 << position[0 if core == 0 else 1])
            pairs.append((at * cores + core, mate * cores + core))
    return lax.ppermute(value, ("wide", "narrow"), pairs)


def shards(features, cotangent, down_weight, down_bias, up_weight):
    tile_rows, tile_cols, channels = features.shape
    half_rows, half_cols = tile_rows // 2, tile_cols // 2
    pixels = half_rows * half_cols
    taps = 9 * channels
    rows, cols = call(
        edge_body,
        (vm((2, tile_cols, channels), BF16), vm((2, tile_rows, channels), BF16)),
        scratch=[
            pltpu.VMEM((2, tile_rows, 16, channels), BF16),
            pltpu.VMEM((tile_rows * 16, channels), F32),
            pltpu.SemaphoreType.DMA((4,)),
        ],
        in_specs=[ANY, ANY],
        nbytes=1 << 19,
        name="edges",
        far=(0, 1),
        room=8,
    )(features, cotangent)
    from_above = passed_along(rows, "wide", 1)
    phases = call(
        phase_body,
        vm((3, tile_rows, half_cols, channels), BF16),
        scratch=[pltpu.VMEM((tile_rows, tile_cols + 8, channels), F32)],
        n_in=1,
        flops=1 << 28,
        nbytes=3 << 20,
        name="phases",
        room=16,
    )
    feat_phases = phases(features)
    from_above, feat_phases = lax.optimization_barrier((from_above, feat_phases))
    cot_phases = phases(cotangent)
    cols = jnp.concatenate(
        [from_above[:, -1:], cols, jnp.zeros((2, 7, channels), BF16)], axis=1
    )
    from_left = passed_along(cols, "narrow", 1)
    grads, first_row, first_col, mine, other, bias_sum = call(
        main_body,
        (
            vm((pixels, channels), BF16),
            vm((half_cols, channels), BF16),
            vm((half_rows, channels), BF16),
            vm((taps, channels), F32),
            vm((taps + SIDE, channels), BF16),
            vm((8, channels), F32),
        ),
        scratch=[
            pltpu.VMEM((half_rows, half_cols, taps), BF16),
            pltpu.VMEM((half_rows, half_cols, taps), BF16),
            pltpu.VMEM((channels, taps), BF16),
            pltpu.VMEM((pixels, channels), BF16),
            pltpu.VMEM((pixels, channels), F32),
            pltpu.VMEM((tile_cols + 8, channels), F32),
            pltpu.VMEM((tile_rows + 8, channels), F32),
        ],
        n_in=7,
        flops=8 * pixels * taps * channels,
        nbytes=6 << 20,
        name="main",
        room=32,
        near=(0, 1, 2, 3),
    )(feat_phases, cot_phases, from_above, from_left, down_weight, down_bias, up_weight)

    got = lax.ppermute(other, "narrow", [(0, 1), (1, 0)])

    from_right = passed_along(first_col, "narrow", -1)
    got, from_right = lax.optimization_barrier((got, from_right))
    low_row = jnp.concatenate(
        [first_row, from_right[:1], jnp.zeros((7, channels), BF16)], axis=0
    )
    from_below = passed_along(low_row, "wide", -1)
    count = lax.axis_size("wide")
    bits = count.bit_length() - 1
    order = [(bit, bit) for bit in range(bits)]
    if bits > 1:
        order[0], order[1] = (0, 1), (1, 0)
    halvings = min(bits - 1, 3)
    held = mine
    for step in range(halvings):
        half = held.shape[0] // 2
        held, send, bias_sum = call(
            functools.partial(halve_body, order[step]),
            (vm((half, channels), F32), vm((half + SIDE, channels), BF16), vm((8, channels), F32)),
            n_in=3,
            nbytes=held.size * 4,
            name="halve",
            near=(0, 1, 2),
        )(held, got, bias_sum)
        got = traded(send, order[step])
        if step == 0:
            got, from_below = lax.optimization_barrier((got, from_below))
    feature_grad = call(
        feature_body,
        sds((tile_rows, tile_cols, channels), BF16),
        scratch=[
            pltpu.VMEM((half_rows + 1, half_cols + 8, channels), F32),
            pltpu.VMEM((half_rows + 1, half_cols, 2 * channels), BF16),
            pltpu.VMEM((4 * channels, 2 * channels), BF16),
            pltpu.VMEM((2 * channels, 2 * channels), BF16),
            pltpu.VMEM((8, 2, tile_cols, channels), F32),
        ],
        n_in=5,
        flops=2 * pixels * 6 * 2 * channels * channels,
        nbytes=3 << 20,
        name="feature",
        room=16,
        near=(0, 1, 2),
    )(grads, from_right, from_below, cotangent, down_weight)
    for step in range(halvings, bits):
        size = held.shape[0] if step == halvings else held.shape[0] - SIDE
        send, bias_sum = call(
            whole_body,
            (vm((size + SIDE, channels), BF16), vm((8, channels), F32)),
            n_in=3,
            nbytes=held.size * 4,
            name="whole",
            near=(0, 1, 2),
        )(held, got, bias_sum)
        got = traded(send, order[step])
        if step == bits - 1:
            got, feature_grad = lax.optimization_barrier((got, feature_grad))
        held = send
    size = got.shape[0] - SIDE
    block, bias_sum = call(
        last_body,
        (vm((size, channels), BF16), vm((8, channels), F32)),
        n_in=3,
        nbytes=size * channels * 4,
        name="last",
            near=(0, 1, 2),
    )(held, got, bias_sum)
    for step in reversed(range(halvings)):
        got = traded(block, order[step])
        block = call(
            functools.partial(place_body, order[step]),
            vm((2 * block.shape[0], channels), BF16),
            n_in=2,
            nbytes=block.size * 4,
            name="place",
            near=(0, 1),
        )(block, got)
    got = lax.ppermute(block, "narrow", [(0, 1), (1, 0)])
    down, up, bias_grad = call(
        final_body,
        (
            sds((9, channels, channels), F32),
            sds((9, channels, channels), F32),
            sds((1, channels), F32),
        ),
        n_in=3,
        nbytes=12 * taps * channels,
        name="final",
            room=8,
            near=(0, 1, 2),
    )(block, got, bias_sum)
    shape = (3, 3, channels, channels)
    return (feature_grad, down.reshape(shape), up.reshape(shape), bias_grad.reshape(channels))


def solution(mesh):
    return jax.shard_map(
        shards,
        mesh=mesh,
        in_specs=(
            P(("groups", "wide"), "narrow", None),
            P(("groups", "wide"), "narrow", None),
            P(),
            P(),
            P(),
        ),
        out_specs=(
            P(("groups", "wide"), "narrow", None),
            P("groups", None, None, None),
            P("groups", None, None, None),
            P("groups"),
        ),
        check_vma=False,
    )
```

```python
import functools

import jax
import jax.numpy as jnp
from jax import lax
from jax.experimental import pallas as pl
from jax.experimental.pallas import tpu as pltpu
from jax.sharding import PartitionSpec as P

F32 = jnp.float32
BF16 = jnp.bfloat16
VM = pl.BlockSpec(memory_space=pltpu.VMEM)
ANY = pl.BlockSpec(memory_space=pl.ANY)
SIDE = 16


def call(body, out_shape, scratch=(), in_specs=None, n_in=0, flops=0, nbytes=0, name=None, near=(), far=(), room=4):
    kernel = pl.pallas_call(
        body,
        out_shape=out_shape,
        in_specs=in_specs if in_specs is not None else [VM] * n_in,
        out_specs=jax.tree.map(lambda _: VM, out_shape),
        scratch_shapes=list(scratch),
        name=name,
        compiler_params=pltpu.CompilerParams(vmem_limit_bytes=room << 20),
        cost_estimate=pl.CostEstimate(flops=flops, transcendentals=0, bytes_accessed=nbytes),
    )

    def run(*args):
        placed = [
            pltpu.with_memory_space_constraint(arg, pltpu.VMEM if at in near else pltpu.HBM)
            if at in near or at in far
            else arg
            for at, arg in enumerate(args)
        ]
        return kernel(*placed)

    return run


def vm(shape, dtype):
    return pltpu.VMEM(shape, dtype)


def sds(shape, dtype):
    return jax.ShapeDtypeStruct(shape, dtype)


def edge_body(feat, cot, rows, cols, corner, strip, wide_strip, sems):
    tile_rows, tile_cols, _ = feat.shape
    copies = []
    for which, ref in enumerate((feat, cot)):
        copies.append(
            pltpu.make_async_copy(ref.at[tile_rows - 1], rows.at[which], sems.at[2 * which])
        )
        copies.append(
            pltpu.make_async_copy(
                ref.at[:, pl.ds(tile_cols - 16, 16), :], strip.at[which], sems.at[2 * which + 1]
            )
        )
    for copy in copies:
        copy.start()
    for copy in copies:
        copy.wait()
    for which in range(2):
        wide_strip[...] = strip[which].astype(F32).reshape(wide_strip.shape)
        cols[which] = wide_strip[pl.ds(15, tile_rows, stride=16), :].astype(BF16)
        corner[which] = wide_strip[tile_rows * 16 - 8 :, :].astype(BF16)


def phase_body(tile, out, wide):
    rows, cols, channels = tile.shape
    wide[:, 0:8, :] = jnp.zeros((rows, 8, channels), F32)
    wide[:, 8:, :] = tile[...].astype(F32)
    for col_off in range(3):
        out[col_off] = wide[:, pl.ds(7 + col_off, cols // 2, stride=2), :].astype(BF16)


def if_any(there, value):
    return jnp.where(there, value, jnp.zeros_like(value))


def fill_patches(phases, top, left, corner, patch, line, column):
    _, rows, half_cols, channels = phases.shape
    half_rows = rows // 2
    above = lax.axis_index("wide") > 0
    aside = lax.axis_index("narrow") > 0
    line[0:8, :] = if_any(above & aside, corner[...].astype(F32))
    line[8:, :] = if_any(above, top[...].astype(F32))
    column[...] = if_any(aside, left[...].astype(F32))
    first = lax.broadcasted_iota(jnp.int32, (half_rows, half_cols, channels), 1) == 0
    paired = phases.reshape(3, half_rows, 2, half_cols, channels)
    for col_off in range(3):
        lanes = [pl.ds((3 * row_off + col_off) * channels, channels) for row_off in range(3)]
        even = paired[col_off, :, 0].astype(F32) if col_off == 0 else paired[col_off, :, 0]
        odd = paired[col_off, :, 1].astype(F32) if col_off == 0 else paired[col_off, :, 1]
        if col_off == 0:
            rim = [
                column[pl.ds(off, half_rows, stride=2), :].reshape(half_rows, 1, channels)
                for off in (0, 1)
            ]
            even = jnp.where(first, rim[0], even).astype(BF16)
            odd = jnp.where(first, rim[1], odd).astype(BF16)
        patch[:, :, lanes[1]] = even
        patch[:, :, lanes[2]] = odd
        patch[1:, :, lanes[0]] = odd[:-1]
        patch[0, :, lanes[0]] = line[pl.ds(7 + col_off, half_cols, stride=2), :].astype(BF16)


def main_body(
    feat_phases, cot_phases, top, left, corner, down_weight, down_bias, up_weight,
    grads, first_row, first_col, mine, other, bias_part,
    feat_patch, cot_patch, up_mat, act, wide_grads, line, column,
):
    _, rows, half_cols, channels = feat_phases.shape
    half_rows = rows // 2
    pixels = half_rows * half_cols
    taps = 9 * channels
    fill_patches(feat_phases, top.at[0], left.at[0], corner.at[0], feat_patch, line, column)
    fill_patches(cot_phases, top.at[1], left.at[1], corner.at[1], cot_patch, line, column)
    for tap in range(9):
        up_mat[:, pl.ds(tap * channels, channels)] = up_weight[tap // 3, tap % 3]
    down_mat = down_weight[...].reshape(taps, channels)
    bias_row = down_bias[...].reshape(1, channels)
    step = 8
    for start in range(0, half_rows, step):
        span = pl.ds(start * half_cols, step * half_cols)
        feat_rows = feat_patch[start : start + step].reshape(step * half_cols, taps)
        cot_rows = cot_patch[start : start + step].reshape(step * half_cols, taps)
        pre = jnp.dot(feat_rows, down_mat, preferred_element_type=F32) + bias_row
        act_grad = lax.dot_general(
            cot_rows, up_mat[...], (((1,), (1,)), ((), ())), preferred_element_type=F32
        )
        sigm = 1.0 / (1.0 + jnp.exp(-pre))
        act[span, :] = (pre * sigm).astype(BF16)
        pre_grad = (act_grad * sigm * (1.0 + pre * (1.0 - sigm))).astype(BF16)
        grads[span, :] = pre_grad
        wide_grads[span, :] = pre_grad.astype(F32)
    first_row[...] = grads[0:half_cols, :]
    first_col[...] = wide_grads[pl.ds(0, half_rows, stride=half_cols), :].astype(BF16)
    raw_bias = jnp.sum(wide_grads[...], axis=0, keepdims=True)
    coarse = raw_bias.astype(BF16)
    fine = (raw_bias - coarse.astype(F32)).astype(BF16)
    bias_part[...] = jnp.broadcast_to(coarse.astype(F32) + fine.astype(F32), bias_part.shape)
    put_side(other, taps, coarse, fine)
    raw_up = lax.dot_general(
        act[...], cot_patch[...].reshape(pixels, taps), (((0,), (0,)), ((), ())),
        preferred_element_type=F32,
    )
    raw_down = lax.dot_general(
        feat_patch[...].reshape(pixels, taps), grads[...], (((0,), (0,)), ((), ())),
        preferred_element_type=F32,
    )
    core = lax.axis_index("narrow")

    @pl.when(core == 0)
    def _():
        mine[...] = raw_down
        for tap in range(9):
            span = pl.ds(tap * channels, channels)
            other[span, :] = raw_up[:, tap * channels : (tap + 1) * channels].astype(BF16)

    @pl.when(core != 0)
    def _():
        other[0:taps, :] = raw_down.astype(BF16)
        for tap in range(9):
            span = pl.ds(tap * channels, channels)
            mine[span, :] = raw_up[:, tap * channels : (tap + 1) * channels]


def put_side(out, at, coarse, fine):
    channels = out.shape[1]
    row = lax.broadcasted_iota(jnp.int32, (SIDE, channels), 0)
    block = jnp.where(row == 0, coarse.astype(F32), jnp.where(row == 1, fine.astype(F32), 0.0))
    out[at : at + SIDE, :] = block.astype(BF16)


def take_side(ref, at):
    block = ref[at : at + SIDE, :].astype(F32)
    return block[0:1] + block[1:2]


def bit_of(position):
    return lax.rem(lax.shift_right_logical(lax.axis_index("wide"), jnp.int32(position)), 2)


def joined_bias(bias_in, got, size, out, sent, at):
    total = bias_in[0:1, :] + take_side(got, size)
    coarse = total.astype(BF16)
    fine = (total - coarse.astype(F32)).astype(BF16)
    out[...] = jnp.broadcast_to(coarse.astype(F32) + fine.astype(F32), out.shape)
    if sent is not None:
        put_side(sent, at, coarse, fine)


def split(position, held, got, base, size, keep, send):
    half = size // 2
    bit = bit_of(position)
    near = pl.ds(pl.multiple_of(base + bit * half, 16), half)
    away = pl.ds(pl.multiple_of(base + (1 - bit) * half, 16), half)
    send[0:half, :] = (held[away, :] + got[away, :].astype(F32)).astype(BF16)
    keep[...] = held[near, :] + got[near, :].astype(F32)


def first_body(positions, held, got, bias_in, keep_a, send_a, keep_b, send_b, bias_out):
    size = held.shape[0] // 2
    split(positions[0], held, got, 0, size, keep_a, send_a)
    split(positions[1], held, got, size, size, keep_b, send_b)
    joined_bias(bias_in, got, 2 * size, bias_out, send_a, size // 2)


def halve_body(position, held, got, *rest):
    size = held.shape[0]
    if len(rest) == 4:
        bias_in, keep, send, bias_out = rest
        joined_bias(bias_in, got, size, bias_out, send, size // 2)
    else:
        keep, send = rest
    split(position, held, got, 0, size, keep, send)


def whole_body(size, held, got, *rest):
    send = rest[-2] if len(rest) == 3 else rest[-1]
    send[0:size, :] = (held[0:size, :].astype(F32) + got[0:size, :].astype(F32)).astype(BF16)
    if len(rest) == 3:
        bias_in, _, bias_out = rest
        joined_bias(bias_in, got, size, bias_out, send if send.shape[0] > size else None, size)


def place_body(position, held, got, out):
    place(position, held, got, out, 0)


def place(position, held, got, out, base):
    size = held.shape[0]
    bit = bit_of(position)
    out[pl.ds(pl.multiple_of(base + bit * size, 16), size), :] = held[...]
    out[pl.ds(pl.multiple_of(base + (1 - bit) * size, 16), size), :] = got[...]


def both_body(positions, held_a, got_a, held_b, got_b, out):
    place(positions[0], held_a, got_a, out, 0)
    place(positions[1], held_b, got_b, out, 2 * held_a.shape[0])


def final_body(held, got, bias_in, down, up, bias_out):
    channels = held.shape[1]
    core = lax.axis_index("narrow")
    squares = jnp.zeros((channels, channels), F32)
    for ref in (held, got):
        part = jnp.zeros((channels, channels), F32)
        for tap in range(9):
            block = ref[tap * channels : (tap + 1) * channels, :].astype(F32)
            part = part + block * block
        squares = squares + part
    bias = bias_in[0:1, :]
    total = jnp.sum(jnp.sum(squares, axis=0, keepdims=True) + bias * bias, axis=1, keepdims=True)
    clip_level = 0.5 * float(18 * channels * channels + channels) ** 0.5
    factor = jnp.minimum(1.0, clip_level / jnp.sqrt(total))
    factor = jnp.broadcast_to(factor, (1, channels))
    bias_out[...] = bias * factor

    def write(down_ref, up_ref):
        for tap in range(9):
            rows = slice(tap * channels, (tap + 1) * channels)
            down[tap] = down_ref[rows, :].astype(F32) * factor
            up[tap] = up_ref[rows, :].astype(F32) * factor

    @pl.when(core == 0)
    def _():
        write(held, got)

    @pl.when(core != 0)
    def _():
        write(got, held)


def feature_body(grads, right, below, cot, down_weight, out, wide, pairs, near_mat, low_mat, woven):
    tile_rows, tile_cols, channels = cot.shape
    half_rows, half_cols = tile_rows // 2, tile_cols // 2
    wide[0:half_rows, 0:half_cols, :] = grads[...].astype(F32).reshape(
        half_rows, half_cols, channels
    )
    last = lax.broadcasted_iota(jnp.int32, (half_rows, 8, channels), 1) == 0
    aside = lax.axis_index("narrow") < lax.axis_size("narrow") - 1
    under = lax.axis_index("wide") < lax.axis_size("wide") - 1
    rim = if_any(aside, right[...].astype(F32)).reshape(half_rows, 1, channels)
    wide[0:half_rows, half_cols:, :] = jnp.where(last, rim, 0.0)
    wide[half_rows, 0:half_cols, :] = if_any(under, below[0:half_cols, :].astype(F32))
    wide[half_rows, half_cols:, :] = if_any(under & aside, below[half_cols:, :].astype(F32))
    pairs[:, :, 0:channels] = wide[:, 0:half_cols, :].astype(BF16)
    pairs[:, :, channels:] = wide[:, 1 : half_cols + 1, :].astype(BF16)
    zero = jnp.zeros((channels, channels), BF16)
    blocks = [(1, 1, None), (1, 2, 0), (2, 1, None), (2, 2, 0)]
    for at, (row_off, here, next_off) in enumerate(blocks):
        rows = slice(at * channels, (at + 1) * channels)
        near_mat[rows, 0:channels] = down_weight[row_off, here]
        near_mat[rows, channels:] = zero if next_off is None else down_weight[row_off, next_off]
    for at, (here, next_off) in enumerate([(1, None), (2, 0)]):
        rows = slice(at * channels, (at + 1) * channels)
        low_mat[rows, 0:channels] = down_weight[0, here]
        low_mat[rows, channels:] = zero if next_off is None else down_weight[0, next_off]
    step = 8
    dims = (((1,), (1,)), ((), ()))
    for start in range(0, half_rows, step):
        count = step * half_cols
        here = pairs[start : start + step].reshape(count, 2 * channels)
        lower = pairs[start + 1 : start + 1 + step].reshape(count, 2 * channels)
        near = lax.dot_general(here, near_mat[...], dims, preferred_element_type=F32)
        far = lax.dot_general(lower, low_mat[...], dims, preferred_element_type=F32)
        shape = (step, half_cols, channels)
        for row_par in range(2):
            for col_par in range(2):
                lanes = slice((2 * row_par + col_par) * channels, (2 * row_par + col_par + 1) * channels)
                value = near[:, lanes]
                if row_par:
                    value = value + far[:, col_par * channels : (col_par + 1) * channels]
                woven[:, row_par, pl.ds(col_par, half_cols, stride=2), :] = value.reshape(shape)
        span = slice(2 * start, 2 * (start + step))
        total = cot[span].astype(F32) + woven[...].reshape(2 * step, tile_cols, channels)
        out[span] = total.astype(BF16)


def turned(value, axis, steps):
    count = lax.axis_size(axis)
    return lax.ppermute(value, axis, [(at, (at + steps) % count) for at in range(count)])


def turned_both(value):
    count, cores = lax.axis_size("wide"), lax.axis_size("narrow")
    pairs = [
        (at * cores + core, (at + 1) % count * cores + (core + 1) % cores)
        for at in range(count)
        for core in range(cores)
    ]
    return lax.ppermute(value, ("wide", "narrow"), pairs)


def traded(value, position):
    count = lax.axis_size("wide")
    return lax.ppermute(value, "wide", [(at, at ^ (1 << position)) for at in range(count)])


def shards(features, cotangent, down_weight, down_bias, up_weight):
    tile_rows, tile_cols, channels = features.shape
    half_rows, half_cols = tile_rows // 2, tile_cols // 2
    pixels = half_rows * half_cols
    taps = 9 * channels
    rows, cols, corner = call(
        edge_body,
        (
            vm((2, tile_cols, channels), BF16),
            vm((2, tile_rows, channels), BF16),
            vm((2, 8, channels), BF16),
        ),
        scratch=[
            pltpu.VMEM((2, tile_rows, 16, channels), BF16),
            pltpu.VMEM((tile_rows * 16, channels), F32),
            pltpu.SemaphoreType.DMA((4,)),
        ],
        in_specs=[ANY, ANY],
        nbytes=1 << 19,
        name="edges",
        far=(0, 1),
        room=8,
    )(features, cotangent)
    from_above = turned(rows, "wide", 1)
    from_corner = turned_both(corner)
    from_left = turned(cols, "narrow", 1)
    phases = call(
        phase_body,
        vm((3, tile_rows, half_cols, channels), BF16),
        scratch=[pltpu.VMEM((tile_rows, tile_cols + 8, channels), F32)],
        n_in=1,
        flops=1 << 28,
        nbytes=3 << 20,
        name="phases",
        room=16,
    )
    feat_phases = phases(features)
    cot_phases = phases(cotangent)
    from_above, from_corner, from_left, feat_phases, cot_phases = lax.optimization_barrier(
        (from_above, from_corner, from_left, feat_phases, cot_phases)
    )
    grads, first_row, first_col, mine, other, bias_sum = call(
        main_body,
        (
            vm((pixels, channels), BF16),
            vm((half_cols, channels), BF16),
            vm((half_rows, channels), BF16),
            vm((taps, channels), F32),
            vm((taps + SIDE, channels), BF16),
            vm((8, channels), F32),
        ),
        scratch=[
            pltpu.VMEM((half_rows, half_cols, taps), BF16),
            pltpu.VMEM((half_rows, half_cols, taps), BF16),
            pltpu.VMEM((channels, taps), BF16),
            pltpu.VMEM((pixels, channels), BF16),
            pltpu.VMEM((pixels, channels), F32),
            pltpu.VMEM((tile_cols + 8, channels), F32),
            pltpu.VMEM((tile_rows, channels), F32),
        ],
        n_in=8,
        flops=8 * pixels * taps * channels,
        nbytes=6 << 20,
        name="main",
        near=(0, 1, 2, 3, 4),
        room=32,
    )(
        feat_phases, cot_phases, from_above, from_left, from_corner,
        down_weight, down_bias, up_weight,
    )

    got = turned(other, "narrow", 1)
    from_right = turned(first_col, "narrow", -1)
    got, from_right = lax.optimization_barrier((got, from_right))
    from_below = turned(jnp.concatenate([first_row, from_right[:8]], axis=0), "wide", -1)

    bits = lax.axis_size("wide").bit_length() - 1
    order_a = list(range(bits))
    order_b = order_a[1::-1] + order_a[2:]
    halvings = 1 if bits <= 3 else 2
    half = taps // 4
    held_a, send_a, held_b, send_b, bias_sum = call(
        functools.partial(first_body, (order_a[0], order_b[0])),
        (
            vm((half, channels), F32),
            vm((half + SIDE, channels), BF16),
            vm((half, channels), F32),
            vm((half, channels), BF16),
            vm((8, channels), F32),
        ),
        n_in=3,
        nbytes=taps * channels * 6,
        name="first",
        near=(0, 1, 2),
    )(mine, got, bias_sum)
    got_a = traded(send_a, order_a[0])
    got_b = traded(send_b, order_b[0])
    for step in range(1, halvings):
        half //= 2
        held_a, send_a, bias_sum = call(
            functools.partial(halve_body, order_a[step]),
            (vm((half, channels), F32), vm((half + SIDE, channels), BF16), vm((8, channels), F32)),
            n_in=3,
            name="halve",
            near=(0, 1, 2),
        )(held_a, got_a, bias_sum)
        held_b, send_b = call(
            functools.partial(halve_body, order_b[step]),
            (vm((half, channels), F32), vm((half, channels), BF16)),
            n_in=2,
            name="halve",
            near=(0, 1),
        )(held_b, got_b)
        got_a = traded(send_a, order_a[step])
        got_b = traded(send_b, order_b[step])
    feature_grad = call(
        feature_body,
        sds((tile_rows, tile_cols, channels), BF16),
        scratch=[
            pltpu.VMEM((half_rows + 1, half_cols + 8, channels), F32),
            pltpu.VMEM((half_rows + 1, half_cols, 2 * channels), BF16),
            pltpu.VMEM((4 * channels, 2 * channels), BF16),
            pltpu.VMEM((2 * channels, 2 * channels), BF16),
            pltpu.VMEM((8, 2, tile_cols, channels), F32),
        ],
        n_in=5,
        flops=2 * pixels * 6 * 2 * channels * channels,
        nbytes=3 << 20,
        name="feature",
        near=(0, 1, 2),
        room=16,
    )(grads, from_right, from_below, cotangent, down_weight)
    for step in range(halvings, bits + 1):
        side = SIDE if step < bits else 0
        held_a, bias_sum = call(
            functools.partial(whole_body, half),
            (vm((half + side, channels), BF16), vm((8, channels), F32)),
            n_in=3,
            nbytes=half * channels * 8,
            name="whole",
            near=(0, 1, 2),
        )(held_a, got_a, bias_sum)
        held_b = call(
            functools.partial(whole_body, half),
            vm((half, channels), BF16),
            n_in=2,
            nbytes=half * channels * 8,
            name="whole",
            near=(0, 1),
        )(held_b, got_b)
        if step < bits:
            got_a = traded(held_a, order_a[step])
            got_b = traded(held_b, order_b[step])
            if step == halvings:
                got_a, from_below = lax.optimization_barrier((got_a, from_below))
            if step == bits - 1:
                got_a, feature_grad = lax.optimization_barrier((got_a, feature_grad))
    for step in reversed(range(halvings)):
        got_a = traded(held_a, order_a[step])
        got_b = traded(held_b, order_b[step])
        if step:
            half *= 2
            held_a = call(
                functools.partial(place_body, order_a[step]),
                vm((half, channels), BF16),
                n_in=2,
                name="place",
                near=(0, 1),
            )(held_a, got_a)
            held_b = call(
                functools.partial(place_body, order_b[step]),
                vm((half, channels), BF16),
                n_in=2,
                name="place",
                near=(0, 1),
            )(held_b, got_b)
    block = call(
        functools.partial(both_body, (order_a[0], order_b[0])),
        vm((taps, channels), BF16),
        n_in=4,
        nbytes=taps * channels * 4,
        name="both",
        near=(0, 1, 2, 3),
    )(held_a, got_a, held_b, got_b)
    got = turned(block, "narrow", 1)
    down, up, bias_grad = call(
        final_body,
        (
            sds((9, channels, channels), F32),
            sds((9, channels, channels), F32),
            sds((1, channels), F32),
        ),
        n_in=3,
        nbytes=12 * taps * channels,
        name="final",
        near=(0, 1, 2),
        room=8,
    )(block, got, bias_sum)
    shape = (3, 3, channels, channels)
    return (feature_grad, down.reshape(shape), up.reshape(shape), bias_grad.reshape(channels))


def solution(mesh):
    return jax.shard_map(
        shards,
        mesh=mesh,
        in_specs=(
            P(("groups", "wide"), "narrow", None),
            P(("groups", "wide"), "narrow", None),
            P(),
            P(),
            P(),
        ),
        out_specs=(
            P(("groups", "wide"), "narrow", None),
            P("groups", None, None, None),
            P("groups", None, None, None),
            P("groups"),
        ),
        check_vma=False,
    )
```

```python
import functools

import jax
import jax.numpy as jnp
from jax import lax
from jax.experimental import pallas as pl
from jax.experimental.pallas import tpu as pltpu
from jax.sharding import PartitionSpec as P

F32 = jnp.float32
BF16 = jnp.bfloat16
VM = pl.BlockSpec(memory_space=pltpu.VMEM)
ANY = pl.BlockSpec(memory_space=pl.ANY)
SIDE = 16


def call(body, out_shape, scratch=(), in_specs=None, n_in=0, flops=0, nbytes=0, name=None, near=(), far=(), room=4):
    kernel = pl.pallas_call(
        body,
        out_shape=out_shape,
        in_specs=in_specs if in_specs is not None else [VM] * n_in,
        out_specs=jax.tree.map(lambda _: VM, out_shape),
        scratch_shapes=list(scratch),
        name=name,
        compiler_params=pltpu.CompilerParams(vmem_limit_bytes=room << 20),
        cost_estimate=pl.CostEstimate(flops=flops, transcendentals=0, bytes_accessed=nbytes),
    )

    def run(*args):
        placed = [
            pltpu.with_memory_space_constraint(arg, pltpu.VMEM if at in near else pltpu.HBM)
            if at in near or at in far
            else arg
            for at, arg in enumerate(args)
        ]
        return kernel(*placed)

    return run


def vm(shape, dtype):
    return pltpu.VMEM(shape, dtype)


def sds(shape, dtype):
    return jax.ShapeDtypeStruct(shape, dtype)


def edge_body(feat, cot, rows, cols, corner, strip, wide_strip, sems):
    tile_rows, tile_cols, _ = feat.shape
    copies = []
    for which, ref in enumerate((feat, cot)):
        copies.append(
            pltpu.make_async_copy(ref.at[tile_rows - 1], rows.at[which], sems.at[2 * which])
        )
        copies.append(
            pltpu.make_async_copy(
                ref.at[:, pl.ds(tile_cols - 16, 16), :], strip.at[which], sems.at[2 * which + 1]
            )
        )
    for copy in copies:
        copy.start()
    for copy in copies:
        copy.wait()
    for which in range(2):
        wide_strip[...] = strip[which].astype(F32).reshape(wide_strip.shape)
        cols[which] = wide_strip[pl.ds(15, tile_rows, stride=16), :].astype(BF16)
        corner[which] = wide_strip[tile_rows * 16 - 8 :, :].astype(BF16)


def if_any(there, value):
    return jnp.where(there, value, jnp.zeros_like(value))


def own_patches(tile, wide, strip, patch, firsts):
    rows, cols, channels = tile.shape
    half_rows, half_cols = rows // 2, cols // 2
    wide[:, :, 0:8, :] = jnp.zeros((half_rows, 2, 8, channels), F32)
    wide[:, :, 8:, :] = tile[...].astype(F32).reshape(half_rows, 2, cols, channels)
    for col_off in range(3):
        lanes = [pl.ds((3 * row_off + col_off) * channels, channels) for row_off in range(3)]
        taken = pl.ds(7 + col_off, half_cols, stride=2)
        patch[:, :, lanes[1]] = wide[:, 0, taken, :].astype(BF16)
        odd = wide[:, 1, taken, :].astype(BF16)
        patch[:, :, lanes[2]] = odd
        patch[1:, :, lanes[0]] = odd[:-1]
        patch[0, :, lanes[0]] = jnp.zeros((half_cols, channels), BF16)
    strip[...] = tile[:, 0:16, :].astype(F32).reshape(strip.shape)
    for col in range(2):
        firsts[col] = strip[pl.ds(col, rows, stride=16), :].astype(BF16)


def pointwise(pre, act_grad):
    sigm = 1.0 / (1.0 + jnp.exp(-pre))
    return pre * sigm, act_grad * sigm * (1.0 + pre * (1.0 - sigm))


def interior_body(
    feat, cot, down_weight, down_bias, up_weight,
    grads, raw_up, raw_down, raw_bias, feat_row, cot_row, feat_firsts, cot_firsts, up_mat,
    feat_patch, cot_patch, act, wide, strip,
):
    rows, cols, channels = feat.shape
    half_rows, half_cols = rows // 2, cols // 2
    pixels = half_rows * half_cols
    taps = 9 * channels
    own_patches(feat, wide, strip, feat_patch, feat_firsts)
    own_patches(cot, wide, strip, cot_patch, cot_firsts)
    feat_row[...] = feat_patch[0]
    cot_row[...] = cot_patch[0]
    for tap in range(9):
        up_mat[:, pl.ds(tap * channels, channels)] = up_weight[tap // 3, tap % 3]
    down_mat = down_weight[...].reshape(taps, channels)
    bias_row = down_bias[...].reshape(1, channels)
    step = 8
    count = step * half_cols
    total = jnp.zeros((1, channels), F32)
    at = lax.broadcasted_iota(jnp.int32, (count, channels), 0)
    for start in range(0, half_rows, step):
        span = pl.ds(start * half_cols, count)
        feat_rows = feat_patch[start : start + step].reshape(count, taps)
        cot_rows = cot_patch[start : start + step].reshape(count, taps)
        pre = jnp.dot(feat_rows, down_mat, preferred_element_type=F32) + bias_row
        act_grad = lax.dot_general(
            cot_rows, up_mat[...], (((1,), (1,)), ((), ())), preferred_element_type=F32
        )
        inside = lax.rem(at, half_cols) > 0
        if start == 0:
            inside = inside & (at >= half_cols)
        value, grad = pointwise(pre, act_grad)
        act[span, :] = if_any(inside, value).astype(BF16)
        grad = if_any(inside, grad).astype(BF16)
        grads[span, :] = grad
        total = total + jnp.sum(grad.astype(F32), axis=0, keepdims=True)
    raw_bias[...] = jnp.broadcast_to(total, raw_bias.shape)
    raw_up[...] = lax.dot_general(
        act[...], cot_patch[...].reshape(pixels, taps), (((0,), (0,)), ((), ())),
        preferred_element_type=F32,
    )
    raw_down[...] = lax.dot_general(
        feat_patch[...].reshape(pixels, taps), grads[...], (((0,), (0,)), ((), ())),
        preferred_element_type=F32,
    )


def rim_patches(row_part, firsts, top, left, corner, out, line, column):
    half_cols, taps = row_part.shape
    channels = taps // 9
    half_rows = left.shape[0] // 2
    above = lax.axis_index("wide") > 0
    aside = lax.axis_index("narrow") > 0
    line[0:8, :] = if_any(above & aside, corner[...].astype(F32))
    line[8:, :] = if_any(above, top[...].astype(F32))
    column[0, 0:8, :] = line[0:8, :]
    column[0, 8:, :] = if_any(aside, left[...].astype(F32))
    for col in range(2):
        column[1 + col, 0:8, :] = jnp.zeros((8, channels), F32)
        column[1 + col, 8:, :] = firsts[col].astype(F32)
    out[0:half_cols, 3 * channels :] = row_part[:, 3 * channels :]
    first = lax.broadcasted_iota(jnp.int32, (half_cols, channels), 0) == 0
    for off in range(3):
        out[0:half_cols, off * channels : (off + 1) * channels] = line[
            pl.ds(7 + off, half_cols, stride=2), :
        ].astype(BF16)
        for col_off in range(3):
            lanes = slice((3 * off + col_off) * channels, (3 * off + col_off + 1) * channels)
            out[half_cols:, lanes] = column[
                col_off, pl.ds(7 + off, half_rows, stride=2), :
            ].astype(BF16)
    for off in (1, 2):
        lanes = slice(3 * off * channels, (3 * off + 1) * channels)
        rest = row_part[:, lanes].astype(F32)
        halo = jnp.broadcast_to(column[0, 7 + off : 8 + off, :], rest.shape)
        out[0:half_cols, lanes] = jnp.where(first, halo, rest).astype(BF16)


def rim_body(
    feat_row, cot_row, feat_firsts, cot_firsts, top, left, corner, raw_up, raw_down, raw_bias,
    up_mat, down_weight, down_bias,
    rim_grads, mine, other, bias_part,
    feat_rim, cot_rim, line, column,
):
    half_cols, taps = feat_row.shape
    channels = taps // 9
    rim_patches(feat_row, feat_firsts, top.at[0], left.at[0], corner.at[0], feat_rim, line, column)
    rim_patches(cot_row, cot_firsts, top.at[1], left.at[1], corner.at[1], cot_rim, line, column)
    pre = jnp.dot(
        feat_rim[...], down_weight[...].reshape(taps, channels), preferred_element_type=F32
    ) + down_bias[...].reshape(1, channels)
    act_grad = lax.dot_general(
        cot_rim[...], up_mat[...], (((1,), (1,)), ((), ())), preferred_element_type=F32
    )
    value, grad = pointwise(pre, act_grad)
    once = lax.broadcasted_iota(jnp.int32, value.shape, 0) != half_cols
    act = if_any(once, value).astype(BF16)
    masked = if_any(once, grad).astype(BF16)
    full = grad.astype(BF16).astype(F32)
    rim_grads[...] = jnp.where(once, full, jnp.broadcast_to(full[0:1], full.shape)).astype(BF16)
    total = raw_bias[0:1, :] + jnp.sum(masked.astype(F32), axis=0, keepdims=True)
    coarse = total.astype(BF16)
    fine = (total - coarse.astype(F32)).astype(BF16)
    bias_part[...] = jnp.broadcast_to(coarse.astype(F32) + fine.astype(F32), bias_part.shape)
    put_side(other, taps, coarse, fine)
    more_up = lax.dot_general(
        act, cot_rim[...], (((0,), (0,)), ((), ())), preferred_element_type=F32
    )
    more_down = lax.dot_general(
        feat_rim[...], masked, (((0,), (0,)), ((), ())), preferred_element_type=F32
    )
    core = lax.axis_index("narrow")

    @pl.when(core == 0)
    def _():
        mine[...] = raw_down[...] + more_down
        for tap in range(9):
            span = slice(tap * channels, (tap + 1) * channels)
            other[span, :] = (raw_up[:, span] + more_up[:, span]).astype(BF16)

    @pl.when(core != 0)
    def _():
        other[0:taps, :] = (raw_down[...] + more_down).astype(BF16)
        for tap in range(9):
            span = slice(tap * channels, (tap + 1) * channels)
            mine[span, :] = raw_up[:, span] + more_up[:, span]


def put_side(out, at, coarse, fine):
    channels = out.shape[1]
    row = lax.broadcasted_iota(jnp.int32, (SIDE, channels), 0)
    block = jnp.where(row == 0, coarse.astype(F32), jnp.where(row == 1, fine.astype(F32), 0.0))
    out[at : at + SIDE, :] = block.astype(BF16)


def take_side(ref, at):
    block = ref[at : at + SIDE, :].astype(F32)
    return block[0:1] + block[1:2]


def bit_of(position):
    return lax.rem(lax.shift_right_logical(lax.axis_index("wide"), jnp.int32(position)), 2)


def joined_bias(bias_in, got, size, out, sent, at):
    total = bias_in[0:1, :] + take_side(got, size)
    coarse = total.astype(BF16)
    fine = (total - coarse.astype(F32)).astype(BF16)
    out[...] = jnp.broadcast_to(coarse.astype(F32) + fine.astype(F32), out.shape)
    if sent is not None:
        put_side(sent, at, coarse, fine)


def split(position, held, got, base, size, keep, send):
    half = size // 2
    bit = bit_of(position)
    near = pl.ds(pl.multiple_of(base + bit * half, 16), half)
    away = pl.ds(pl.multiple_of(base + (1 - bit) * half, 16), half)
    send[0:half, :] = (held[away, :] + got[away, :].astype(F32)).astype(BF16)
    keep[...] = held[near, :] + got[near, :].astype(F32)


def first_body(positions, held, got, bias_in, keep_a, send_a, keep_b, send_b, bias_out):
    size = held.shape[0] // 2
    split(positions[0], held, got, 0, size, keep_a, send_a)
    split(positions[1], held, got, size, size, keep_b, send_b)
    joined_bias(bias_in, got, 2 * size, bias_out, send_a, size // 2)


def halve_body(position, held, got, *rest):
    size = held.shape[0]
    if len(rest) == 4:
        bias_in, keep, send, bias_out = rest
        joined_bias(bias_in, got, size, bias_out, send, size // 2)
    else:
        keep, send = rest
    split(position, held, got, 0, size, keep, send)


def whole_body(size, held, got, *rest):
    send = rest[-2] if len(rest) == 3 else rest[-1]
    send[0:size, :] = (held[0:size, :].astype(F32) + got[0:size, :].astype(F32)).astype(BF16)
    if len(rest) == 3:
        bias_in, _, bias_out = rest
        joined_bias(bias_in, got, size, bias_out, send if send.shape[0] > size else None, size)


def place_body(position, held, got, out):
    place(position, held, got, out, 0)


def place(position, held, got, out, base):
    size = held.shape[0]
    bit = bit_of(position)
    out[pl.ds(pl.multiple_of(base + bit * size, 16), size), :] = held[...]
    out[pl.ds(pl.multiple_of(base + (1 - bit) * size, 16), size), :] = got[...]


def both_body(positions, held_a, got_a, held_b, got_b, out):
    place(positions[0], held_a, got_a, out, 0)
    place(positions[1], held_b, got_b, out, 2 * held_a.shape[0])


def final_body(held, got, bias_in, down, up, bias_out):
    channels = held.shape[1]
    core = lax.axis_index("narrow")
    squares = jnp.zeros((channels, channels), F32)
    for ref in (held, got):
        part = jnp.zeros((channels, channels), F32)
        for tap in range(9):
            block = ref[tap * channels : (tap + 1) * channels, :].astype(F32)
            part = part + block * block
        squares = squares + part
    bias = bias_in[0:1, :]
    total = jnp.sum(jnp.sum(squares, axis=0, keepdims=True) + bias * bias, axis=1, keepdims=True)
    clip_level = 0.5 * float(18 * channels * channels + channels) ** 0.5
    factor = jnp.minimum(1.0, clip_level / jnp.sqrt(total))
    factor = jnp.broadcast_to(factor, (1, channels))
    bias_out[...] = bias * factor

    def write(down_ref, up_ref):
        for tap in range(9):
            rows = slice(tap * channels, (tap + 1) * channels)
            down[tap] = down_ref[rows, :].astype(F32) * factor
            up[tap] = up_ref[rows, :].astype(F32) * factor

    @pl.when(core == 0)
    def _():
        write(held, got)

    @pl.when(core != 0)
    def _():
        write(got, held)


def feature_body(grads, rim_grads, right, below, cot, down_weight, out, wide, pairs, near_mat, low_mat, woven):
    tile_rows, tile_cols, channels = cot.shape
    half_rows, half_cols = tile_rows // 2, tile_cols // 2
    wide[0:half_rows, 0:half_cols, :] = grads[...].astype(F32).reshape(
        half_rows, half_cols, channels
    )
    last = lax.broadcasted_iota(jnp.int32, (half_rows, 8, channels), 1) == 0
    own = rim_grads[half_cols:, :].astype(F32).reshape(half_rows, 1, channels)
    wide[0:half_rows, 0:8, :] = jnp.where(last, own, wide[0:half_rows, 0:8, :])
    wide[0, 0:half_cols, :] = rim_grads[0:half_cols, :].astype(F32)
    aside = lax.axis_index("narrow") < lax.axis_size("narrow") - 1
    under = lax.axis_index("wide") < lax.axis_size("wide") - 1
    rim = if_any(aside, right[...].astype(F32)).reshape(half_rows, 1, channels)
    wide[0:half_rows, half_cols:, :] = jnp.where(last, rim, 0.0)
    wide[half_rows, 0:half_cols, :] = if_any(under, below[0:half_cols, :].astype(F32))
    wide[half_rows, half_cols:, :] = if_any(under & aside, below[half_cols:, :].astype(F32))
    pairs[:, :, 0:channels] = wide[:, 0:half_cols, :].astype(BF16)
    pairs[:, :, channels:] = wide[:, 1 : half_cols + 1, :].astype(BF16)
    zero = jnp.zeros((channels, channels), BF16)
    blocks = [(1, 1, None), (1, 2, 0), (2, 1, None), (2, 2, 0)]
    for at, (row_off, here, next_off) in enumerate(blocks):
        rows = slice(at * channels, (at + 1) * channels)
        near_mat[rows, 0:channels] = down_weight[row_off, here]
        near_mat[rows, channels:] = zero if next_off is None else down_weight[row_off, next_off]
    for at, (here, next_off) in enumerate([(1, None), (2, 0)]):
        rows = slice(at * channels, (at + 1) * channels)
        low_mat[rows, 0:channels] = down_weight[0, here]
        low_mat[rows, channels:] = zero if next_off is None else down_weight[0, next_off]
    step = 8
    dims = (((1,), (1,)), ((), ()))
    for start in range(0, half_rows, step):
        count = step * half_cols
        here = pairs[start : start + step].reshape(count, 2 * channels)
        lower = pairs[start + 1 : start + 1 + step].reshape(count, 2 * channels)
        near = lax.dot_general(here, near_mat[...], dims, preferred_element_type=F32)
        far = lax.dot_general(lower, low_mat[...], dims, preferred_element_type=F32)
        shape = (step, half_cols, channels)
        for row_par in range(2):
            for col_par in range(2):
                lanes = slice((2 * row_par + col_par) * channels, (2 * row_par + col_par + 1) * channels)
                value = near[:, lanes]
                if row_par:
                    value = value + far[:, col_par * channels : (col_par + 1) * channels]
                woven[:, row_par, pl.ds(col_par, half_cols, stride=2), :] = value.reshape(shape)
        span = slice(2 * start, 2 * (start + step))
        total = cot[span].astype(F32) + woven[...].reshape(2 * step, tile_cols, channels)
        out[span] = total.astype(BF16)


def turned(value, axis, steps):
    count = lax.axis_size(axis)
    return lax.ppermute(value, axis, [(at, (at + steps) % count) for at in range(count)])


def turned_both(value):
    count, cores = lax.axis_size("wide"), lax.axis_size("narrow")
    pairs = [
        (at * cores + core, (at + 1) % count * cores + (core + 1) % cores)
        for at in range(count)
        for core in range(cores)
    ]
    return lax.ppermute(value, ("wide", "narrow"), pairs)


def traded(value, position):
    count = lax.axis_size("wide")
    return lax.ppermute(value, "wide", [(at, at ^ (1 << position)) for at in range(count)])


def shards(features, cotangent, down_weight, down_bias, up_weight):
    tile_rows, tile_cols, channels = features.shape
    half_rows, half_cols = tile_rows // 2, tile_cols // 2
    pixels = half_rows * half_cols
    taps = 9 * channels
    rows, cols, corner = call(
        edge_body,
        (
            vm((2, tile_cols, channels), BF16),
            vm((2, tile_rows, channels), BF16),
            vm((2, 8, channels), BF16),
        ),
        scratch=[
            pltpu.VMEM((2, tile_rows, 16, channels), BF16),
            pltpu.VMEM((tile_rows * 16, channels), F32),
            pltpu.SemaphoreType.DMA((4,)),
        ],
        in_specs=[ANY, ANY],
        nbytes=1 << 19,
        name="edges",
        far=(0, 1),
        room=8,
    )(features, cotangent)
    from_above = turned(rows, "wide", 1)
    from_corner = turned_both(corner)
    from_left = turned(cols, "narrow", 1)
    out_of_interior = (
        vm((pixels, channels), BF16),
        vm((channels, taps), F32),
        vm((taps, channels), F32),
        vm((8, channels), F32),
        vm((half_cols, taps), BF16),
        vm((half_cols, taps), BF16),
        vm((2, tile_rows, channels), BF16),
        vm((2, tile_rows, channels), BF16),
        vm((channels, taps), BF16),
    )
    (
        grads, raw_up, raw_down, raw_bias, feat_row, cot_row, feat_firsts, cot_firsts, up_mat
    ) = call(
        interior_body,
        out_of_interior,
        scratch=[
            pltpu.VMEM((half_rows, half_cols, taps), BF16),
            pltpu.VMEM((half_rows, half_cols, taps), BF16),
            pltpu.VMEM((pixels, channels), BF16),
            pltpu.VMEM((half_rows, 2, tile_cols + 8, channels), F32),
            pltpu.VMEM((tile_rows * 16, channels), F32),
        ],
        n_in=5,
        flops=8 * pixels * taps * channels,
        nbytes=6 << 20,
        name="interior",
        near=(0, 1),
        room=16,
    )(features, cotangent, down_weight, down_bias, up_weight)
    from_above, from_corner, from_left, raw_up = lax.optimization_barrier(
        (from_above, from_corner, from_left, raw_up)
    )
    rim_grads, mine, other, bias_sum = call(
        rim_body,
        (
            vm((half_cols + half_rows, channels), BF16),
            vm((taps, channels), F32),
            vm((taps + SIDE, channels), BF16),
            vm((8, channels), F32),
        ),
        scratch=[
            pltpu.VMEM((half_cols + half_rows, taps), BF16),
            pltpu.VMEM((half_cols + half_rows, taps), BF16),
            pltpu.VMEM((tile_cols + 8, channels), F32),
            pltpu.VMEM((3, tile_rows + 8, channels), F32),
        ],
        n_in=13,
        flops=1 << 26,
        nbytes=3 << 20,
        name="rim",
        near=tuple(range(11)),
        room=16,
    )(
        feat_row, cot_row, feat_firsts, cot_firsts, from_above, from_left, from_corner,
        raw_up, raw_down, raw_bias, up_mat, down_weight, down_bias,
    )

    got = turned(other, "narrow", 1)
    from_right = turned(rim_grads[half_cols:], "narrow", -1)
    got, from_right = lax.optimization_barrier((got, from_right))
    from_below = turned(jnp.concatenate([rim_grads[:half_cols], from_right[:8]], axis=0), "wide", -1)

    bits = lax.axis_size("wide").bit_length() - 1
    order_a = list(range(bits))
    order_b = order_a[1::-1] + order_a[2:]
    halvings = 1 if bits <= 3 else 2
    half = taps // 4
    held_a, send_a, held_b, send_b, bias_sum = call(
        functools.partial(first_body, (order_a[0], order_b[0])),
        (
            vm((half, channels), F32),
            vm((half + SIDE, channels), BF16),
            vm((half, channels), F32),
            vm((half, channels), BF16),
            vm((8, channels), F32),
        ),
        n_in=3,
        nbytes=taps * channels * 6,
        name="first",
        near=(0, 1, 2),
    )(mine, got, bias_sum)
    got_a = traded(send_a, order_a[0])
    got_b = traded(send_b, order_b[0])
    for step in range(1, halvings):
        half //= 2
        held_a, send_a, bias_sum = call(
            functools.partial(halve_body, order_a[step]),
            (vm((half, channels), F32), vm((half + SIDE, channels), BF16), vm((8, channels), F32)),
            n_in=3,
            name="halve",
            near=(0, 1, 2),
        )(held_a, got_a, bias_sum)
        held_b, send_b = call(
            functools.partial(halve_body, order_b[step]),
            (vm((half, channels), F32), vm((half, channels), BF16)),
            n_in=2,
            name="halve",
            near=(0, 1),
        )(held_b, got_b)
        got_a = traded(send_a, order_a[step])
        got_b = traded(send_b, order_b[step])
    feature_grad = call(
        feature_body,
        sds((tile_rows, tile_cols, channels), BF16),
        scratch=[
            pltpu.VMEM((half_rows + 1, half_cols + 8, channels), F32),
            pltpu.VMEM((half_rows + 1, half_cols, 2 * channels), BF16),
            pltpu.VMEM((4 * channels, 2 * channels), BF16),
            pltpu.VMEM((2 * channels, 2 * channels), BF16),
            pltpu.VMEM((8, 2, tile_cols, channels), F32),
        ],
        n_in=6,
        flops=2 * pixels * 6 * 2 * channels * channels,
        nbytes=3 << 20,
        name="feature",
        near=(0, 1, 2, 3),
        room=16,
    )(grads, rim_grads, from_right, from_below, cotangent, down_weight)
    for step in range(halvings, bits + 1):
        side = SIDE if step < bits else 0
        held_a, bias_sum = call(
            functools.partial(whole_body, half),
            (vm((half + side, channels), BF16), vm((8, channels), F32)),
            n_in=3,
            nbytes=half * channels * 8,
            name="whole",
            near=(0, 1, 2),
        )(held_a, got_a, bias_sum)
        held_b = call(
            functools.partial(whole_body, half),
            vm((half, channels), BF16),
            n_in=2,
            nbytes=half * channels * 8,
            name="whole",
            near=(0, 1),
        )(held_b, got_b)
        if step < bits:
            got_a = traded(held_a, order_a[step])
            got_b = traded(held_b, order_b[step])
            if step == bits - 1:
                got_a, from_below = lax.optimization_barrier((got_a, from_below))
    for step in reversed(range(halvings)):
        got_a = traded(held_a, order_a[step])
        got_b = traded(held_b, order_b[step])
        if step == 0:
            got_a, feature_grad = lax.optimization_barrier((got_a, feature_grad))
        if step:
            half *= 2
            held_a = call(
                functools.partial(place_body, order_a[step]),
                vm((half, channels), BF16),
                n_in=2,
                name="place",
                near=(0, 1),
            )(held_a, got_a)
            held_b = call(
                functools.partial(place_body, order_b[step]),
                vm((half, channels), BF16),
                n_in=2,
                name="place",
                near=(0, 1),
            )(held_b, got_b)
    block = call(
        functools.partial(both_body, (order_a[0], order_b[0])),
        vm((taps, channels), BF16),
        n_in=4,
        nbytes=taps * channels * 4,
        name="both",
        near=(0, 1, 2, 3),
    )(held_a, got_a, held_b, got_b)
    got = turned(block, "narrow", 1)
    down, up, bias_grad = call(
        final_body,
        (
            sds((9, channels, channels), F32),
            sds((9, channels, channels), F32),
            sds((1, channels), F32),
        ),
        n_in=3,
        nbytes=12 * taps * channels,
        name="final",
        near=(0, 1, 2),
        room=8,
    )(block, got, bias_sum)
    shape = (3, 3, channels, channels)
    return (feature_grad, down.reshape(shape), up.reshape(shape), bias_grad.reshape(channels))


def solution(mesh):
    return jax.shard_map(
        shards,
        mesh=mesh,
        in_specs=(
            P(("groups", "wide"), "narrow", None),
            P(("groups", "wide"), "narrow", None),
            P(),
            P(),
            P(),
        ),
        out_specs=(
            P(("groups", "wide"), "narrow", None),
            P("groups", None, None, None),
            P("groups", None, None, None),
            P("groups"),
        ),
        check_vma=False,
    )
```

```python
import functools

import jax
import jax.numpy as jnp
from jax import lax
from jax.experimental import pallas as pl
from jax.experimental.pallas import tpu as pltpu
from jax.sharding import PartitionSpec as P

F32 = jnp.float32
BF16 = jnp.bfloat16
VM = pl.BlockSpec(memory_space=pltpu.VMEM)
ANY = pl.BlockSpec(memory_space=pl.ANY)
SIDE = 16


def call(body, out_shape, scratch=(), in_specs=None, n_in=0, flops=0, nbytes=0, name=None, near=(), far=(), room=4, out_specs=None):
    kernel = pl.pallas_call(
        body,
        out_shape=out_shape,
        in_specs=in_specs if in_specs is not None else [VM] * n_in,
        out_specs=out_specs or jax.tree.map(lambda _: VM, out_shape),
        scratch_shapes=list(scratch),
        name=name,
        compiler_params=pltpu.CompilerParams(vmem_limit_bytes=room << 20),
        cost_estimate=pl.CostEstimate(flops=flops, transcendentals=0, bytes_accessed=nbytes),
    )

    def run(*args):
        placed = [
            pltpu.with_memory_space_constraint(arg, pltpu.VMEM if at in near else pltpu.HBM)
            if at in near or at in far
            else arg
            for at, arg in enumerate(args)
        ]
        return kernel(*placed)

    return run


def vm(shape, dtype):
    return pltpu.VMEM(shape, dtype)


def sds(shape, dtype):
    return jax.ShapeDtypeStruct(shape, dtype)


def edge_body(
    feat, cot, down, up, bias, feat_near, cot_near, down_near, up_near, bias_near,
    rows, cols, corner, strip, wide_strip, sems,
):
    tile_rows, tile_cols, _ = feat.shape
    copies = []
    for which, ref in enumerate((feat, cot)):
        copies.append(
            pltpu.make_async_copy(ref.at[tile_rows - 1], rows.at[which], sems.at[2 * which])
        )
        copies.append(
            pltpu.make_async_copy(
                ref.at[:, pl.ds(tile_cols - 16, 16), :], strip.at[which], sems.at[2 * which + 1]
            )
        )
    bulk = [
        pltpu.make_async_copy(feat, feat_near, sems.at[4]),
        pltpu.make_async_copy(cot, cot_near, sems.at[5]),
        pltpu.make_async_copy(down, down_near, sems.at[6]),
        pltpu.make_async_copy(up, up_near, sems.at[7]),
        pltpu.make_async_copy(bias, bias_near, sems.at[8]),
    ]
    for copy in copies + bulk:
        copy.start()
    for copy in copies:
        copy.wait()
    for which in range(2):
        wide_strip[...] = strip[which].astype(F32).reshape(wide_strip.shape)
        cols[which] = wide_strip[pl.ds(15, tile_rows, stride=16), :].astype(BF16)
        corner[which] = wide_strip[tile_rows * 16 - 8 :, :].astype(BF16)
    for copy in bulk:
        copy.wait()


def if_any(there, value):
    return jnp.where(there, value, jnp.zeros_like(value))


def own_patches(tile, wide, strip, patch, firsts):
    rows, cols, channels = tile.shape
    half_rows, half_cols = rows // 2, cols // 2
    wide[:, :, 0:8, :] = jnp.zeros((half_rows, 2, 8, channels), F32)
    wide[:, :, 8:, :] = tile[...].astype(F32).reshape(half_rows, 2, cols, channels)
    for col_off in range(3):
        lanes = [pl.ds((3 * row_off + col_off) * channels, channels) for row_off in range(3)]
        taken = pl.ds(7 + col_off, half_cols, stride=2)
        patch[:, :, lanes[1]] = wide[:, 0, taken, :].astype(BF16)
        odd = wide[:, 1, taken, :].astype(BF16)
        patch[:, :, lanes[2]] = odd
        patch[1:, :, lanes[0]] = odd[:-1]
        patch[0, :, lanes[0]] = jnp.zeros((half_cols, channels), BF16)
    strip[...] = tile[:, 0:16, :].astype(F32).reshape(strip.shape)
    for col in range(2):
        firsts[col] = strip[pl.ds(col, rows, stride=16), :].astype(BF16)


def pointwise(pre, act_grad):
    sigm = 1.0 / (1.0 + jnp.exp(-pre))
    return pre * sigm, act_grad * sigm * (1.0 + pre * (1.0 - sigm))


def taps_of(core_is, patch, values):
    if core_is:
        return lax.dot_general(
            patch, values, (((0,), (0,)), ((), ())), preferred_element_type=F32
        )
    channels = values.shape[1]
    rows = lax.dot_general(values, patch, (((0,), (0,)), ((), ())), preferred_element_type=F32)
    return jnp.concatenate(
        [rows[:, tap * channels : (tap + 1) * channels] for tap in range(9)], axis=0
    )


def interior_body(
    feat, cot, down_weight, down_bias, up_weight,
    feat_patch, cot_patch, act, grads, raw_other, raw_bias, feat_firsts, cot_firsts, up_mat,
    wide, strip,
):
    rows, cols, channels = feat.shape
    half_rows, half_cols = rows // 2, cols // 2
    pixels = half_rows * half_cols
    taps = 9 * channels
    own_patches(feat, wide, strip, feat_patch, feat_firsts)
    own_patches(cot, wide, strip, cot_patch, cot_firsts)
    for tap in range(9):
        up_mat[:, pl.ds(tap * channels, channels)] = up_weight[tap // 3, tap % 3]
    down_mat = down_weight[...].reshape(taps, channels)
    bias_row = down_bias[...].reshape(1, channels)
    step = 8
    count = step * half_cols
    total = jnp.zeros((1, channels), F32)
    at = lax.broadcasted_iota(jnp.int32, (count, channels), 0)
    for start in range(0, half_rows, step):
        span = pl.ds(start * half_cols, count)
        feat_rows = feat_patch[start : start + step].reshape(count, taps)
        cot_rows = cot_patch[start : start + step].reshape(count, taps)
        pre = jnp.dot(feat_rows, down_mat, preferred_element_type=F32) + bias_row
        act_grad = lax.dot_general(
            cot_rows, up_mat[...], (((1,), (1,)), ((), ())), preferred_element_type=F32
        )
        inside = lax.rem(at, half_cols) > 0
        if start == 0:
            inside = inside & (at >= half_cols)
        value, grad = pointwise(pre, act_grad)
        act[span, :] = if_any(inside, value).astype(BF16)
        grad = if_any(inside, grad).astype(BF16)
        grads[span, :] = grad
        total = total + jnp.sum(grad.astype(F32), axis=0, keepdims=True)
    raw_bias[...] = jnp.broadcast_to(total, raw_bias.shape)
    core = lax.axis_index("narrow")

    @pl.when(core == 0)
    def _():
        raw_other[...] = taps_of(False, cot_patch[...].reshape(pixels, taps), act[...])

    @pl.when(core != 0)
    def _():
        raw_other[...] = taps_of(True, feat_patch[...].reshape(pixels, taps), grads[...])


def rim_patches(patch, firsts, top, left, corner, out, line, column):
    half_rows, half_cols, taps = patch.shape
    channels = taps // 9
    above = lax.axis_index("wide") > 0
    aside = lax.axis_index("narrow") > 0
    line[0:8, :] = if_any(above & aside, corner[...].astype(F32))
    line[8:, :] = if_any(above, top[...].astype(F32))
    column[0, 0:8, :] = line[0:8, :]
    column[0, 8:, :] = if_any(aside, left[...].astype(F32))
    for col in range(2):
        column[1 + col, 0:8, :] = jnp.zeros((8, channels), F32)
        column[1 + col, 8:, :] = firsts[col].astype(F32)
    out[0:half_cols, 3 * channels :] = patch[0, :, 3 * channels :]
    first = lax.broadcasted_iota(jnp.int32, (half_cols, channels), 0) == 0
    for off in range(3):
        out[0:half_cols, off * channels : (off + 1) * channels] = line[
            pl.ds(7 + off, half_cols, stride=2), :
        ].astype(BF16)
        for col_off in range(3):
            lanes = slice((3 * off + col_off) * channels, (3 * off + col_off + 1) * channels)
            out[half_cols:, lanes] = column[
                col_off, pl.ds(7 + off, half_rows, stride=2), :
            ].astype(BF16)
    for off in (1, 2):
        lanes = slice(3 * off * channels, (3 * off + 1) * channels)
        rest = patch[0, :, lanes].astype(F32)
        halo = jnp.broadcast_to(column[0, 7 + off : 8 + off, :], rest.shape)
        out[0:half_cols, lanes] = jnp.where(first, halo, rest).astype(BF16)


def rim_body(
    feat_patch, cot_patch, feat_firsts, cot_firsts, top, left, corner, raw_other, raw_bias,
    up_mat, down_weight, down_bias,
    rim_grads, feat_rim, cot_rim, rim_act, rim_masked, other_a, other_b, bias_part,
    line, column,
):
    _, half_cols, taps = feat_patch.shape
    channels = taps // 9
    half = taps // 2
    rim_patches(
        feat_patch, feat_firsts, top.at[0], left.at[0], corner.at[0], feat_rim, line, column
    )
    rim_patches(cot_patch, cot_firsts, top.at[1], left.at[1], corner.at[1], cot_rim, line, column)
    pre = jnp.dot(
        feat_rim[...], down_weight[...].reshape(taps, channels), preferred_element_type=F32
    ) + down_bias[...].reshape(1, channels)
    act_grad = lax.dot_general(
        cot_rim[...], up_mat[...], (((1,), (1,)), ((), ())), preferred_element_type=F32
    )
    value, grad = pointwise(pre, act_grad)
    once = lax.broadcasted_iota(jnp.int32, value.shape, 0) != half_cols
    act = if_any(once, value).astype(BF16)
    masked = if_any(once, grad).astype(BF16)
    rim_act[...] = act
    rim_masked[...] = masked
    full = grad.astype(BF16).astype(F32)
    rim_grads[...] = jnp.where(once, full, jnp.broadcast_to(full[0:1], full.shape)).astype(BF16)
    total = raw_bias[0:1, :] + jnp.sum(masked.astype(F32), axis=0, keepdims=True)
    coarse = total.astype(BF16)
    fine = (total - coarse.astype(F32)).astype(BF16)
    bias_part[...] = jnp.broadcast_to(coarse.astype(F32) + fine.astype(F32), bias_part.shape)
    put_side(other_a, half, coarse, fine)
    core = lax.axis_index("narrow")

    def give(more):
        other_a[0:half, :] = (raw_other[0:half, :] + more[0:half]).astype(BF16)
        other_b[...] = (raw_other[half:, :] + more[half:]).astype(BF16)

    @pl.when(core == 0)
    def _():
        give(taps_of(False, cot_rim[...], act))

    @pl.when(core != 0)
    def _():
        give(taps_of(True, feat_rim[...], masked))


def mine_body(
    feat_patch, cot_patch, act, grads, feat_rim, cot_rim, rim_act, rim_masked, mine_a, mine_b
):
    half_rows, half_cols, taps = feat_patch.shape
    pixels = half_rows * half_cols
    half = taps // 2
    core = lax.axis_index("narrow")

    def keep(which, patch, values, rim_patch, rim_values):
        total = taps_of(which, patch[...].reshape(pixels, taps), values[...])
        total = total + taps_of(which, rim_patch[...], rim_values[...])
        mine_a[...] = total[0:half]
        mine_b[...] = total[half:]

    @pl.when(core == 0)
    def _():
        keep(True, feat_patch, grads, feat_rim, rim_masked)

    @pl.when(core != 0)
    def _():
        keep(False, cot_patch, act, cot_rim, rim_act)


def put_side(out, at, coarse, fine):
    channels = out.shape[1]
    row = lax.broadcasted_iota(jnp.int32, (SIDE, channels), 0)
    block = jnp.where(row == 0, coarse.astype(F32), jnp.where(row == 1, fine.astype(F32), 0.0))
    out[at : at + SIDE, :] = block.astype(BF16)


def take_side(ref, at):
    block = ref[at : at + SIDE, :].astype(F32)
    return block[0:1] + block[1:2]


def bit_of(position):
    return lax.rem(lax.shift_right_logical(lax.axis_index("wide"), jnp.int32(position)), 2)


def joined_bias(bias_in, got, size, out, sent, at):
    total = bias_in[0:1, :] + take_side(got, size)
    coarse = total.astype(BF16)
    fine = (total - coarse.astype(F32)).astype(BF16)
    out[...] = jnp.broadcast_to(coarse.astype(F32) + fine.astype(F32), out.shape)
    if sent is not None:
        put_side(sent, at, coarse, fine)


def split(position, held, got, base, size, keep, send):
    half = size // 2
    bit = bit_of(position)
    near = pl.ds(pl.multiple_of(base + bit * half, 16), half)
    away = pl.ds(pl.multiple_of(base + (1 - bit) * half, 16), half)
    send[0:half, :] = (held[away, :] + got[away, :].astype(F32)).astype(BF16)
    keep[...] = held[near, :] + got[near, :].astype(F32)


def halve_body(position, held, got, *rest):
    size = held.shape[0]
    if len(rest) == 4:
        bias_in, keep, send, bias_out = rest
        joined_bias(bias_in, got, size, bias_out, send, size // 2)
    else:
        keep, send = rest
    split(position, held, got, 0, size, keep, send)


def whole_body(size, held, got, *rest):
    send = rest[-2] if len(rest) == 3 else rest[-1]
    send[0:size, :] = (held[0:size, :].astype(F32) + got[0:size, :].astype(F32)).astype(BF16)
    if len(rest) == 3:
        bias_in, _, bias_out = rest
        joined_bias(bias_in, got, size, bias_out, send if send.shape[0] > size else None, size)


def place_body(position, held, got, out):
    place(position, held, got, out, 0)


def place(position, held, got, out, base):
    size = held.shape[0]
    bit = bit_of(position)
    out[pl.ds(pl.multiple_of(base + bit * size, 16), size), :] = held[...]
    out[pl.ds(pl.multiple_of(base + (1 - bit) * size, 16), size), :] = got[...]


def final_body(
    positions, held_a, got_a, held_b, got_b, far_held_a, far_got_a, far_held_b, far_got_b, bias_in,
    down, up, bias_out, mine, far, sems,
):
    channels = held_a.shape[1]
    core = lax.axis_index("narrow")
    bit_a, bit_b = bit_of(positions[0]), bit_of(positions[1])
    def square(ref):
        block = ref[...].astype(F32).reshape(-1, 8, channels)
        return jnp.sum(block * block, axis=0)

    def pair(one, two, three, four):
        return (square(one) + square(two)) + (square(three) + square(four))

    squares = pair(held_a, got_a, held_b, got_b) + pair(
        far_held_a, far_got_a, far_held_b, far_got_b
    )
    bias = bias_in[0:1, :]
    total = jnp.sum(jnp.sum(squares, axis=0, keepdims=True) + bias * bias, axis=1, keepdims=True)
    clip_level = 0.5 * float(18 * channels * channels + channels) ** 0.5
    factor = jnp.minimum(1.0, clip_level / jnp.sqrt(total))
    factor = jnp.broadcast_to(factor, (1, channels))
    bias_out[...] = bias * factor
    spots = (bit_a, 1 - bit_a, 2 + bit_b, 3 - bit_b)
    for at, (near_ref, far_ref) in enumerate(
        ((held_a, far_held_a), (got_a, far_got_a), (held_b, far_held_b), (got_b, far_got_b))
    ):
        mine[at] = near_ref[...].astype(F32) * factor
        far[at] = far_ref[...].astype(F32) * factor

        @pl.when(core == 0)
        def _():
            pltpu.make_async_copy(mine.at[at], down.at[spots[at]], sems.at[at]).start()
            pltpu.make_async_copy(far.at[at], up.at[spots[at]], sems.at[4 + at]).start()

        @pl.when(core != 0)
        def _():
            pltpu.make_async_copy(mine.at[at], up.at[spots[at]], sems.at[at]).start()
            pltpu.make_async_copy(far.at[at], down.at[spots[at]], sems.at[4 + at]).start()

    for at in range(4):
        pltpu.make_async_copy(mine.at[at], down.at[spots[at]], sems.at[at]).wait()
        pltpu.make_async_copy(far.at[at], up.at[spots[at]], sems.at[4 + at]).wait()


def feature_body(grads, rim_grads, right, below, cot, down_weight, out, wide, pairs, near_mat, low_mat, woven):
    tile_rows, tile_cols, channels = cot.shape
    half_rows, half_cols = tile_rows // 2, tile_cols // 2
    wide[0:half_rows, 0:half_cols, :] = grads[...].astype(F32).reshape(
        half_rows, half_cols, channels
    )
    last = lax.broadcasted_iota(jnp.int32, (half_rows, 8, channels), 1) == 0
    own = rim_grads[half_cols:, :].astype(F32).reshape(half_rows, 1, channels)
    wide[0:half_rows, 0:8, :] = jnp.where(last, own, wide[0:half_rows, 0:8, :])
    wide[0, 0:half_cols, :] = rim_grads[0:half_cols, :].astype(F32)
    aside = lax.axis_index("narrow") < lax.axis_size("narrow") - 1
    under = lax.axis_index("wide") < lax.axis_size("wide") - 1
    rim = if_any(aside, right[...].astype(F32)).reshape(half_rows, 1, channels)
    wide[0:half_rows, half_cols:, :] = jnp.where(last, rim, 0.0)
    wide[half_rows, 0:half_cols, :] = if_any(under, below[0:half_cols, :].astype(F32))
    wide[half_rows, half_cols:, :] = if_any(under & aside, below[half_cols:, :].astype(F32))
    pairs[:, :, 0:channels] = wide[:, 0:half_cols, :].astype(BF16)
    pairs[:, :, channels:] = wide[:, 1 : half_cols + 1, :].astype(BF16)
    zero = jnp.zeros((channels, channels), BF16)
    blocks = [(1, 1, None), (1, 2, 0), (2, 1, None), (2, 2, 0)]
    for at, (row_off, here, next_off) in enumerate(blocks):
        rows = slice(at * channels, (at + 1) * channels)
        near_mat[rows, 0:channels] = down_weight[row_off, here]
        near_mat[rows, channels:] = zero if next_off is None else down_weight[row_off, next_off]
    for at, (here, next_off) in enumerate([(1, None), (2, 0)]):
        rows = slice(at * channels, (at + 1) * channels)
        low_mat[rows, 0:channels] = down_weight[0, here]
        low_mat[rows, channels:] = zero if next_off is None else down_weight[0, next_off]
    step = 8
    dims = (((1,), (1,)), ((), ()))
    for start in range(0, half_rows, step):
        count = step * half_cols
        here = pairs[start : start + step].reshape(count, 2 * channels)
        lower = pairs[start + 1 : start + 1 + step].reshape(count, 2 * channels)
        near = lax.dot_general(here, near_mat[...], dims, preferred_element_type=F32)
        far = lax.dot_general(lower, low_mat[...], dims, preferred_element_type=F32)
        shape = (step, half_cols, channels)
        for row_par in range(2):
            for col_par in range(2):
                lanes = slice((2 * row_par + col_par) * channels, (2 * row_par + col_par + 1) * channels)
                value = near[:, lanes]
                if row_par:
                    value = value + far[:, col_par * channels : (col_par + 1) * channels]
                woven[:, row_par, pl.ds(col_par, half_cols, stride=2), :] = value.reshape(shape)
        span = slice(2 * start, 2 * (start + step))
        total = cot[span].astype(F32) + woven[...].reshape(2 * step, tile_cols, channels)
        out[span] = total.astype(BF16)


def turned(value, axis, steps):
    count = lax.axis_size(axis)
    return lax.ppermute(value, axis, [(at, (at + steps) % count) for at in range(count)])


def turned_both(value):
    count, cores = lax.axis_size("wide"), lax.axis_size("narrow")
    pairs = [
        (at * cores + core, (at + 1) % count * cores + (core + 1) % cores)
        for at in range(count)
        for core in range(cores)
    ]
    return lax.ppermute(value, ("wide", "narrow"), pairs)


def traded(value, position):
    count = lax.axis_size("wide")
    return lax.ppermute(value, "wide", [(at, at ^ (1 << position)) for at in range(count)])


def shards(features, cotangent, down_weight, down_bias, up_weight):
    tile_rows, tile_cols, channels = features.shape
    half_rows, half_cols = tile_rows // 2, tile_cols // 2
    pixels = half_rows * half_cols
    taps = 9 * channels
    feat_near, cot_near, down_near, up_near, bias_near, rows, cols, corner = call(
        edge_body,
        (
            vm(features.shape, BF16),
            vm(features.shape, BF16),
            vm(down_weight.shape, BF16),
            vm(up_weight.shape, BF16),
            vm((1, channels), F32),
            vm((2, tile_cols, channels), BF16),
            vm((2, tile_rows, channels), BF16),
            vm((2, 8, channels), BF16),
        ),
        scratch=[
            pltpu.VMEM((2, tile_rows, 16, channels), BF16),
            pltpu.VMEM((tile_rows * 16, channels), F32),
            pltpu.SemaphoreType.DMA((9,)),
        ],
        in_specs=[ANY] * 5,
        nbytes=1 << 19,
        name="edges",
        far=(0, 1, 2, 3, 4),
        room=8,
    )(features, cotangent, down_weight, up_weight, down_bias.reshape(1, channels))
    from_above = turned(rows, "wide", 1)
    from_corner = turned_both(corner)
    from_left = turned(cols, "narrow", 1)
    patches = vm((half_rows, half_cols, taps), BF16)
    firsts = vm((2, tile_rows, channels), BF16)
    (
        feat_patch, cot_patch, act, grads, raw_other, raw_bias, feat_firsts, cot_firsts, up_mat
    ) = call(
        interior_body,
        (
            patches,
            patches,
            vm((pixels, channels), BF16),
            vm((pixels, channels), BF16),
            vm((taps, channels), F32),
            vm((8, channels), F32),
            firsts,
            firsts,
            vm((channels, taps), BF16),
        ),
        scratch=[
            pltpu.VMEM((half_rows, 2, tile_cols + 8, channels), F32),
            pltpu.VMEM((tile_rows * 16, channels), F32),
        ],
        n_in=5,
        flops=6 * pixels * taps * channels,
        nbytes=6 << 20,
        name="interior",
        near=(0, 1, 2, 3, 4),
        room=12,
    )(feat_near, cot_near, down_near, bias_near, up_near)
    from_above, from_corner, from_left, raw_other = lax.optimization_barrier(
        (from_above, from_corner, from_left, raw_other)
    )
    pieces = half_cols + half_rows
    rim_grads, feat_rim, cot_rim, rim_act, rim_masked, other_a, other_b, bias_sum = call(
        rim_body,
        (
            vm((pieces, channels), BF16),
            vm((pieces, taps), BF16),
            vm((pieces, taps), BF16),
            vm((pieces, channels), BF16),
            vm((pieces, channels), BF16),
            vm((taps // 2 + SIDE, channels), BF16),
            vm((taps // 2, channels), BF16),
            vm((8, channels), F32),
        ),
        scratch=[
            pltpu.VMEM((tile_cols + 8, channels), F32),
            pltpu.VMEM((3, tile_rows + 8, channels), F32),
        ],
        n_in=12,
        flops=1 << 26,
        nbytes=3 << 20,
        name="rim",
        near=tuple(range(12)),
        room=8,
    )(
        feat_patch, cot_patch, feat_firsts, cot_firsts, from_above, from_left, from_corner,
        raw_other, raw_bias, up_mat, down_near, bias_near,
    )
    got_a = turned(other_a, "narrow", 1)
    got_b = turned(other_b, "narrow", 1)
    mine_a, mine_b = call(
        mine_body,
        (vm((taps // 2, channels), F32), vm((taps // 2, channels), F32)),
        n_in=8,
        flops=2 * pixels * taps * channels,
        nbytes=3 << 20,
        name="mine",
        near=tuple(range(8)),
        room=12,
    )(feat_patch, cot_patch, act, grads, feat_rim, cot_rim, rim_act, rim_masked)
    from_right = turned(rim_grads[half_cols:], "narrow", -1)
    got_a, mine_a, mine_b = lax.optimization_barrier((got_a, mine_a, mine_b))
    got_b, from_right = lax.optimization_barrier((got_b, from_right))
    from_below = turned(
        jnp.concatenate([rim_grads[:half_cols], from_right[:8]], axis=0), "wide", -1
    )

    bits = lax.axis_size("wide").bit_length() - 1
    order_a = list(range(bits))
    order_b = order_a[1::-1] + order_a[2:]
    halvings = 1 if bits <= 3 else 2
    half = taps // 2
    held_a, held_b = mine_a, mine_b
    for step in range(halvings):
        half //= 2
        held_a, send_a, bias_sum = call(
            functools.partial(halve_body, order_a[step]),
            (vm((half, channels), F32), vm((half + SIDE, channels), BF16), vm((8, channels), F32)),
            n_in=3,
            nbytes=half * channels * 12,
            name="halve",
            near=(0, 1, 2),
        )(held_a, got_a, bias_sum)
        held_b, send_b = call(
            functools.partial(halve_body, order_b[step]),
            (vm((half, channels), F32), vm((half, channels), BF16)),
            n_in=2,
            nbytes=half * channels * 12,
            name="halve",
            near=(0, 1),
        )(held_b, got_b)
        got_a = traded(send_a, order_a[step])
        got_b = traded(send_b, order_b[step])
    feature_grad = call(
        feature_body,
        sds((tile_rows, tile_cols, channels), BF16),
        scratch=[
            pltpu.VMEM((half_rows + 1, half_cols + 8, channels), F32),
            pltpu.VMEM((half_rows + 1, half_cols, 2 * channels), BF16),
            pltpu.VMEM((4 * channels, 2 * channels), BF16),
            pltpu.VMEM((2 * channels, 2 * channels), BF16),
            pltpu.VMEM((8, 2, tile_cols, channels), F32),
        ],
        n_in=6,
        flops=2 * pixels * 6 * 2 * channels * channels,
        nbytes=3 << 20,
        name="feature",
        near=(0, 1, 2, 3, 4, 5),
        room=16,
    )(grads, rim_grads, from_right, from_below, cot_near, down_near)
    for step in range(halvings, bits + 1):
        side = SIDE if step < bits else 0
        held_a, bias_sum = call(
            functools.partial(whole_body, half),
            (vm((half + side, channels), BF16), vm((8, channels), F32)),
            n_in=3,
            nbytes=half * channels * 8,
            name="whole",
            near=(0, 1, 2),
        )(held_a, got_a, bias_sum)
        held_b = call(
            functools.partial(whole_body, half),
            vm((half, channels), BF16),
            n_in=2,
            nbytes=half * channels * 8,
            name="whole",
            near=(0, 1),
        )(held_b, got_b)
        if step < bits:
            got_a = traded(held_a, order_a[step])
            got_b = traded(held_b, order_b[step])
            if step == halvings:
                got_b, from_below = lax.optimization_barrier((got_b, from_below))
            if step == bits - 1:
                got_b, feature_grad = lax.optimization_barrier((got_b, feature_grad))
    for step in reversed(range(halvings)):
        got_a = traded(held_a, order_a[step])
        got_b = traded(held_b, order_b[step])
        if step:
            half *= 2
            held_a = call(
                functools.partial(place_body, order_a[step]),
                vm((half, channels), BF16),
                n_in=2,
                name="place",
                near=(0, 1),
            )(held_a, got_a)
            held_b = call(
                functools.partial(place_body, order_b[step]),
                vm((half, channels), BF16),
                n_in=2,
                name="place",
                near=(0, 1),
            )(held_b, got_b)
    blocks = (held_a, got_a, held_b, got_b)
    far_blocks = [turned(block, "narrow", 1) for block in blocks]
    size = taps // 4
    down, up, bias_grad = call(
        functools.partial(final_body, (order_a[0], order_b[0])),
        (
            sds((4, size, channels), F32),
            sds((4, size, channels), F32),
            sds((1, channels), F32),
        ),
        scratch=[
            pltpu.VMEM((4, size, channels), F32),
            pltpu.VMEM((4, size, channels), F32),
            pltpu.SemaphoreType.DMA((8,)),
        ],
        n_in=9,
        nbytes=12 * taps * channels,
        name="final",
        near=tuple(range(9)),
        room=8,
        out_specs=(ANY, ANY, VM),
    )(*blocks, *far_blocks, bias_sum)
    shape = (3, 3, channels, channels)
    return (feature_grad, down.reshape(shape), up.reshape(shape), bias_grad.reshape(channels))


def solution(mesh):
    return jax.shard_map(
        shards,
        mesh=mesh,
        in_specs=(
            P(("groups", "wide"), "narrow", None),
            P(("groups", "wide"), "narrow", None),
            P(),
            P(),
            P(),
        ),
        out_specs=(
            P(("groups", "wide"), "narrow", None),
            P("groups", None, None, None),
            P("groups", None, None, None),
            P("groups"),
        ),
        check_vma=False,
    )
```

```python
import functools

import jax
import jax.numpy as jnp
from jax import lax
from jax.experimental import pallas as pl
from jax.experimental.pallas import tpu as pltpu
from jax.sharding import PartitionSpec as P

F32 = jnp.float32
BF16 = jnp.bfloat16
VM = pl.BlockSpec(memory_space=pltpu.VMEM)
ANY = pl.BlockSpec(memory_space=pl.ANY)
SIDE = 16


def call(body, out_shape, scratch=(), in_specs=None, n_in=0, flops=0, nbytes=0, name=None, near=(), far=(), room=4, out_specs=None):
    kernel = pl.pallas_call(
        body,
        out_shape=out_shape,
        in_specs=in_specs if in_specs is not None else [VM] * n_in,
        out_specs=out_specs or jax.tree.map(lambda _: VM, out_shape),
        scratch_shapes=list(scratch),
        name=name,
        compiler_params=pltpu.CompilerParams(vmem_limit_bytes=room << 20),
        cost_estimate=pl.CostEstimate(flops=flops, transcendentals=0, bytes_accessed=nbytes),
    )

    def run(*args):
        placed = [
            pltpu.with_memory_space_constraint(arg, pltpu.VMEM if at in near else pltpu.HBM)
            if at in near or at in far
            else arg
            for at, arg in enumerate(args)
        ]
        return kernel(*placed)

    return run


def vm(shape, dtype):
    return pltpu.VMEM(shape, dtype)


def sds(shape, dtype):
    return jax.ShapeDtypeStruct(shape, dtype)


def edge_body(feat, cot, feat_near, rows, cols, corner, strip, wide_strip, sems):
    tile_rows, tile_cols, _ = feat.shape
    copies = []
    for which, ref in enumerate((feat, cot)):
        copies.append(
            pltpu.make_async_copy(ref.at[tile_rows - 1], rows.at[which], sems.at[2 * which])
        )
        copies.append(
            pltpu.make_async_copy(
                ref.at[:, pl.ds(tile_cols - 16, 16), :], strip.at[which], sems.at[2 * which + 1]
            )
        )
    bulk = [pltpu.make_async_copy(feat, feat_near, sems.at[4])]
    for copy in copies + bulk:
        copy.start()
    for copy in copies:
        copy.wait()
    for which in range(2):
        wide_strip[...] = strip[which].astype(F32).reshape(wide_strip.shape)
        cols[which] = wide_strip[pl.ds(15, tile_rows, stride=16), :].astype(BF16)
        corner[which] = wide_strip[tile_rows * 16 - 8 :, :].astype(BF16)
    for copy in bulk:
        copy.wait()


def if_any(there, value):
    return jnp.where(there, value, jnp.zeros_like(value))


def own_patches(tile, wide, strip, patch, firsts):
    rows, cols, channels = tile.shape
    half_rows, half_cols = rows // 2, cols // 2
    wide[:, :, 0:8, :] = jnp.zeros((half_rows, 2, 8, channels), F32)
    wide[:, :, 8:, :] = tile[...].astype(F32).reshape(half_rows, 2, cols, channels)
    for col_off in range(3):
        lanes = [pl.ds((3 * row_off + col_off) * channels, channels) for row_off in range(3)]
        taken = pl.ds(7 + col_off, half_cols, stride=2)
        patch[:, :, lanes[1]] = wide[:, 0, taken, :].astype(BF16)
        odd = wide[:, 1, taken, :].astype(BF16)
        patch[:, :, lanes[2]] = odd
        patch[1:, :, lanes[0]] = odd[:-1]
        patch[0, :, lanes[0]] = jnp.zeros((half_cols, channels), BF16)
    strip[...] = tile[:, 0:16, :].astype(F32).reshape(strip.shape)
    for col in range(2):
        firsts[col] = strip[pl.ds(col, rows, stride=16), :].astype(BF16)


def pointwise(pre, act_grad):
    sigm = 1.0 / (1.0 + jnp.exp(-pre))
    return pre * sigm, act_grad * sigm * (1.0 + pre * (1.0 - sigm))


def taps_of(core_is, patch, values):
    if core_is:
        return lax.dot_general(
            patch, values, (((0,), (0,)), ((), ())), preferred_element_type=F32
        )
    channels = values.shape[1]
    rows = lax.dot_general(values, patch, (((0,), (0,)), ((), ())), preferred_element_type=F32)
    return jnp.concatenate(
        [rows[:, tap * channels : (tap + 1) * channels] for tap in range(9)], axis=0
    )


def interior_body(
    feat, far_cot, far_down, far_bias, far_up,
    feat_patch, cot_patch, act, grads, raw_other, raw_bias, feat_firsts, cot_firsts, up_mat,
    wide, strip, cot, down_weight, down_bias, sems,
):
    rows, cols, channels = feat.shape
    half_rows, half_cols = rows // 2, cols // 2
    pixels = half_rows * half_cols
    taps = 9 * channels
    copies = [
        pltpu.make_async_copy(far_cot, cot, sems.at[9]),
        pltpu.make_async_copy(far_down, down_weight, sems.at[10]),
        pltpu.make_async_copy(far_bias, down_bias, sems.at[11]),
    ] + [
        pltpu.make_async_copy(
            far_up.at[tap // 3, tap % 3], up_mat.at[:, pl.ds(tap * channels, channels)],
            sems.at[tap],
        )
        for tap in range(9)
    ]
    for copy in copies:
        copy.start()
    own_patches(feat, wide, strip, feat_patch, feat_firsts)
    copies[0].wait()
    own_patches(cot, wide, strip, cot_patch, cot_firsts)
    for copy in copies[1:]:
        copy.wait()
    down_mat = down_weight[...].reshape(taps, channels)
    bias_row = down_bias[...].reshape(1, channels)
    step = 8
    count = step * half_cols
    total = jnp.zeros((1, channels), F32)
    at = lax.broadcasted_iota(jnp.int32, (count, channels), 0)
    for start in range(0, half_rows, step):
        span = pl.ds(start * half_cols, count)
        feat_rows = feat_patch[start : start + step].reshape(count, taps)
        cot_rows = cot_patch[start : start + step].reshape(count, taps)
        pre = jnp.dot(feat_rows, down_mat, preferred_element_type=F32) + bias_row
        act_grad = lax.dot_general(
            cot_rows, up_mat[...], (((1,), (1,)), ((), ())), preferred_element_type=F32
        )
        inside = lax.rem(at, half_cols) > 0
        if start == 0:
            inside = inside & (at >= half_cols)
        value, grad = pointwise(pre, act_grad)
        act[span, :] = if_any(inside, value).astype(BF16)
        grad = if_any(inside, grad).astype(BF16)
        grads[span, :] = grad
        total = total + jnp.sum(grad.astype(F32), axis=0, keepdims=True)
    raw_bias[...] = jnp.broadcast_to(total, raw_bias.shape)
    core = lax.axis_index("narrow")

    @pl.when(core == 0)
    def _():
        raw_other[...] = taps_of(False, cot_patch[...].reshape(pixels, taps), act[...])

    @pl.when(core != 0)
    def _():
        raw_other[...] = taps_of(True, feat_patch[...].reshape(pixels, taps), grads[...])


def rim_patches(patch, firsts, top, left, corner, out, line, column):
    half_rows, half_cols, taps = patch.shape
    channels = taps // 9
    above = lax.axis_index("wide") > 0
    aside = lax.axis_index("narrow") > 0
    line[0:8, :] = if_any(above & aside, corner[...].astype(F32))
    line[8:, :] = if_any(above, top[...].astype(F32))
    column[0, 0:8, :] = line[0:8, :]
    column[0, 8:, :] = if_any(aside, left[...].astype(F32))
    for col in range(2):
        column[1 + col, 0:8, :] = jnp.zeros((8, channels), F32)
        column[1 + col, 8:, :] = firsts[col].astype(F32)
    out[0:half_cols, 3 * channels :] = patch[0, :, 3 * channels :]
    first = lax.broadcasted_iota(jnp.int32, (half_cols, channels), 0) == 0
    for off in range(3):
        out[0:half_cols, off * channels : (off + 1) * channels] = line[
            pl.ds(7 + off, half_cols, stride=2), :
        ].astype(BF16)
        for col_off in range(3):
            lanes = slice((3 * off + col_off) * channels, (3 * off + col_off + 1) * channels)
            out[half_cols:, lanes] = column[
                col_off, pl.ds(7 + off, half_rows, stride=2), :
            ].astype(BF16)
    for off in (1, 2):
        lanes = slice(3 * off * channels, (3 * off + 1) * channels)
        rest = patch[0, :, lanes].astype(F32)
        halo = jnp.broadcast_to(column[0, 7 + off : 8 + off, :], rest.shape)
        out[0:half_cols, lanes] = jnp.where(first, halo, rest).astype(BF16)


def rim_body(
    feat_patch, cot_patch, feat_firsts, cot_firsts, top, left, corner, raw_other, raw_bias,
    up_mat, down_weight, down_bias,
    rim_grads, feat_rim, cot_rim, rim_act, rim_masked, other_a, other_b, bias_part,
    line, column,
):
    _, half_cols, taps = feat_patch.shape
    channels = taps // 9
    half = taps // 2
    rim_patches(
        feat_patch, feat_firsts, top.at[0], left.at[0], corner.at[0], feat_rim, line, column
    )
    rim_patches(cot_patch, cot_firsts, top.at[1], left.at[1], corner.at[1], cot_rim, line, column)
    pre = jnp.dot(
        feat_rim[...], down_weight[...].reshape(taps, channels), preferred_element_type=F32
    ) + down_bias[...].reshape(1, channels)
    act_grad = lax.dot_general(
        cot_rim[...], up_mat[...], (((1,), (1,)), ((), ())), preferred_element_type=F32
    )
    value, grad = pointwise(pre, act_grad)
    once = lax.broadcasted_iota(jnp.int32, value.shape, 0) != half_cols
    act = if_any(once, value).astype(BF16)
    masked = if_any(once, grad).astype(BF16)
    rim_act[...] = act
    rim_masked[...] = masked
    full = grad.astype(BF16).astype(F32)
    rim_grads[...] = jnp.where(once, full, jnp.broadcast_to(full[0:1], full.shape)).astype(BF16)
    total = raw_bias[0:1, :] + jnp.sum(masked.astype(F32), axis=0, keepdims=True)
    coarse = total.astype(BF16)
    fine = (total - coarse.astype(F32)).astype(BF16)
    bias_part[...] = jnp.broadcast_to(coarse.astype(F32) + fine.astype(F32), bias_part.shape)
    put_side(other_a, half, coarse, fine)
    core = lax.axis_index("narrow")

    def give(more):
        other_a[0:half, :] = (raw_other[0:half, :] + more[0:half]).astype(BF16)
        other_b[...] = (raw_other[half:, :] + more[half:]).astype(BF16)

    @pl.when(core == 0)
    def _():
        give(taps_of(False, cot_rim[...], act))

    @pl.when(core != 0)
    def _():
        give(taps_of(True, feat_rim[...], masked))


def mine_body(
    feat_patch, cot_patch, act, grads, feat_rim, cot_rim, rim_act, rim_masked, mine_a, mine_b
):
    half_rows, half_cols, taps = feat_patch.shape
    pixels = half_rows * half_cols
    half = taps // 2
    core = lax.axis_index("narrow")

    def keep(which, patch, values, rim_patch, rim_values):
        total = taps_of(which, patch[...].reshape(pixels, taps), values[...])
        total = total + taps_of(which, rim_patch[...], rim_values[...])
        mine_a[...] = total[0:half]
        mine_b[...] = total[half:]

    @pl.when(core == 0)
    def _():
        keep(True, feat_patch, grads, feat_rim, rim_masked)

    @pl.when(core != 0)
    def _():
        keep(False, cot_patch, act, cot_rim, rim_act)


def put_side(out, at, coarse, fine):
    channels = out.shape[1]
    row = lax.broadcasted_iota(jnp.int32, (SIDE, channels), 0)
    block = jnp.where(row == 0, coarse.astype(F32), jnp.where(row == 1, fine.astype(F32), 0.0))
    out[at : at + SIDE, :] = block.astype(BF16)


def take_side(ref, at):
    block = ref[at : at + SIDE, :].astype(F32)
    return block[0:1] + block[1:2]


def bit_of(position):
    return lax.rem(lax.shift_right_logical(lax.axis_index("wide"), jnp.int32(position)), 2)


def joined_bias(bias_in, got, size, out, sent, at):
    total = bias_in[0:1, :] + take_side(got, size)
    coarse = total.astype(BF16)
    fine = (total - coarse.astype(F32)).astype(BF16)
    out[...] = jnp.broadcast_to(coarse.astype(F32) + fine.astype(F32), out.shape)
    if sent is not None:
        put_side(sent, at, coarse, fine)


def split(position, held, got, base, size, keep, send):
    half = size // 2
    bit = bit_of(position)
    near = pl.ds(pl.multiple_of(base + bit * half, 16), half)
    away = pl.ds(pl.multiple_of(base + (1 - bit) * half, 16), half)
    send[0:half, :] = (held[away, :] + got[away, :].astype(F32)).astype(BF16)
    keep[...] = held[near, :] + got[near, :].astype(F32)


def halve_body(position, held, got, *rest):
    size = held.shape[0]
    if len(rest) == 4:
        bias_in, keep, send, bias_out = rest
        joined_bias(bias_in, got, size, bias_out, send, size // 2)
    else:
        keep, send = rest
    split(position, held, got, 0, size, keep, send)


def whole_body(size, held, got, *rest):
    send = rest[-2] if len(rest) == 3 else rest[-1]
    send[0:size, :] = (held[0:size, :].astype(F32) + got[0:size, :].astype(F32)).astype(BF16)
    if len(rest) == 3:
        bias_in, _, bias_out = rest
        joined_bias(bias_in, got, size, bias_out, send if send.shape[0] > size else None, size)


def place_body(position, held, got, out):
    place(position, held, got, out, 0)


def place(position, held, got, out, base):
    size = held.shape[0]
    bit = bit_of(position)
    out[pl.ds(pl.multiple_of(base + bit * size, 16), size), :] = held[...]
    out[pl.ds(pl.multiple_of(base + (1 - bit) * size, 16), size), :] = got[...]


def final_body(
    positions, held_a, got_a, held_b, got_b, far_held_a, far_got_a, far_held_b, far_got_b, bias_in,
    down, up, bias_out,
):
    channels = held_a.shape[1]
    core = lax.axis_index("narrow")
    bit_a, bit_b = bit_of(positions[0]), bit_of(positions[1])
    def square(ref):
        block = ref[...].astype(F32).reshape(-1, 8, channels)
        return jnp.sum(block * block, axis=0)

    def pair(one, two, three, four):
        return (square(one) + square(two)) + (square(three) + square(four))

    squares = pair(held_a, got_a, held_b, got_b) + pair(
        far_held_a, far_got_a, far_held_b, far_got_b
    )
    bias = bias_in[0:1, :]
    total = jnp.sum(jnp.sum(squares, axis=0, keepdims=True) + bias * bias, axis=1, keepdims=True)
    clip_level = 0.5 * float(18 * channels * channels + channels) ** 0.5
    factor = jnp.minimum(1.0, clip_level / jnp.sqrt(total))
    factor = jnp.broadcast_to(factor, (1, channels))
    bias_out[...] = bias * factor
    spots = (bit_a, 1 - bit_a, 2 + bit_b, 3 - bit_b)
    for at, (near_ref, far_ref) in enumerate(
        ((held_a, far_held_a), (got_a, far_got_a), (held_b, far_held_b), (got_b, far_got_b))
    ):
        near_block = near_ref[...].astype(F32) * factor
        far_block = far_ref[...].astype(F32) * factor

        @pl.when(core == 0)
        def _():
            down[spots[at]] = near_block
            up[spots[at]] = far_block

        @pl.when(core != 0)
        def _():
            up[spots[at]] = near_block
            down[spots[at]] = far_block


def feature_body(grads, rim_grads, right, below, cot, down_weight, out, wide, pairs, near_mat, low_mat, woven):
    tile_rows, tile_cols, channels = cot.shape
    half_rows, half_cols = tile_rows // 2, tile_cols // 2
    wide[0:half_rows, 0:half_cols, :] = grads[...].astype(F32).reshape(
        half_rows, half_cols, channels
    )
    last = lax.broadcasted_iota(jnp.int32, (half_rows, 8, channels), 1) == 0
    own = rim_grads[half_cols:, :].astype(F32).reshape(half_rows, 1, channels)
    wide[0:half_rows, 0:8, :] = jnp.where(last, own, wide[0:half_rows, 0:8, :])
    wide[0, 0:half_cols, :] = rim_grads[0:half_cols, :].astype(F32)
    aside = lax.axis_index("narrow") < lax.axis_size("narrow") - 1
    under = lax.axis_index("wide") < lax.axis_size("wide") - 1
    rim = if_any(aside, right[...].astype(F32)).reshape(half_rows, 1, channels)
    wide[0:half_rows, half_cols:, :] = jnp.where(last, rim, 0.0)
    wide[half_rows, 0:half_cols, :] = if_any(under, below[0:half_cols, :].astype(F32))
    wide[half_rows, half_cols:, :] = if_any(under & aside, below[half_cols:, :].astype(F32))
    pairs[:, :, 0:channels] = wide[:, 0:half_cols, :].astype(BF16)
    pairs[:, :, channels:] = wide[:, 1 : half_cols + 1, :].astype(BF16)
    zero = jnp.zeros((channels, channels), BF16)
    blocks = [(1, 1, None), (1, 2, 0), (2, 1, None), (2, 2, 0)]
    for at, (row_off, here, next_off) in enumerate(blocks):
        rows = slice(at * channels, (at + 1) * channels)
        near_mat[rows, 0:channels] = down_weight[row_off, here]
        near_mat[rows, channels:] = zero if next_off is None else down_weight[row_off, next_off]
    for at, (here, next_off) in enumerate([(1, None), (2, 0)]):
        rows = slice(at * channels, (at + 1) * channels)
        low_mat[rows, 0:channels] = down_weight[0, here]
        low_mat[rows, channels:] = zero if next_off is None else down_weight[0, next_off]
    step = 8
    dims = (((1,), (1,)), ((), ()))
    for start in range(0, half_rows, step):
        count = step * half_cols
        here = pairs[start : start + step].reshape(count, 2 * channels)
        lower = pairs[start + 1 : start + 1 + step].reshape(count, 2 * channels)
        near = lax.dot_general(here, near_mat[...], dims, preferred_element_type=F32)
        far = lax.dot_general(lower, low_mat[...], dims, preferred_element_type=F32)
        shape = (step, half_cols, channels)
        for row_par in range(2):
            for col_par in range(2):
                lanes = slice((2 * row_par + col_par) * channels, (2 * row_par + col_par + 1) * channels)
                value = near[:, lanes]
                if row_par:
                    value = value + far[:, col_par * channels : (col_par + 1) * channels]
                woven[:, row_par, pl.ds(col_par, half_cols, stride=2), :] = value.reshape(shape)
        span = slice(2 * start, 2 * (start + step))
        total = cot[span].astype(F32) + woven[...].reshape(2 * step, tile_cols, channels)
        out[span] = total.astype(BF16)


def turned(value, axis, steps):
    count = lax.axis_size(axis)
    return lax.ppermute(value, axis, [(at, (at + steps) % count) for at in range(count)])


def turned_both(value):
    count, cores = lax.axis_size("wide"), lax.axis_size("narrow")
    pairs = [
        (at * cores + core, (at + 1) % count * cores + (core + 1) % cores)
        for at in range(count)
        for core in range(cores)
    ]
    return lax.ppermute(value, ("wide", "narrow"), pairs)


def traded(value, position):
    count = lax.axis_size("wide")
    return lax.ppermute(value, "wide", [(at, at ^ (1 << position)) for at in range(count)])


def shards(features, cotangent, down_weight, down_bias, up_weight):
    tile_rows, tile_cols, channels = features.shape
    half_rows, half_cols = tile_rows // 2, tile_cols // 2
    pixels = half_rows * half_cols
    taps = 9 * channels
    feat_near, rows, cols, corner = call(
        edge_body,
        (
            vm(features.shape, BF16),
            vm((2, tile_cols, channels), BF16),
            vm((2, tile_rows, channels), BF16),
            vm((2, 8, channels), BF16),
        ),
        scratch=[
            pltpu.VMEM((2, tile_rows, 16, channels), BF16),
            pltpu.VMEM((tile_rows * 16, channels), F32),
            pltpu.SemaphoreType.DMA((5,)),
        ],
        in_specs=[ANY] * 2,
        nbytes=1 << 19,
        name="edges",
        far=(0, 1),
        room=8,
    )(features, cotangent)
    from_above = turned(rows, "wide", 1)
    from_corner = turned_both(corner)
    from_left = turned(cols, "narrow", 1)
    patches = vm((half_rows, half_cols, taps), BF16)
    firsts = vm((2, tile_rows, channels), BF16)
    (
        feat_patch, cot_patch, act, grads, raw_other, raw_bias, feat_firsts, cot_firsts, up_mat
    ) = call(
        interior_body,
        (
            patches,
            patches,
            vm((pixels, channels), BF16),
            vm((pixels, channels), BF16),
            vm((taps, channels), F32),
            vm((8, channels), F32),
            firsts,
            firsts,
            vm((channels, taps), BF16),
        ),
        scratch=[
            pltpu.VMEM((half_rows, 2, tile_cols + 8, channels), F32),
            pltpu.VMEM((tile_rows * 16, channels), F32),
            pltpu.VMEM(features.shape, BF16),
            pltpu.VMEM(down_weight.shape, BF16),
            pltpu.VMEM((1, channels), F32),
            pltpu.SemaphoreType.DMA((12,)),
        ],
        in_specs=[VM, ANY, ANY, ANY, ANY],
        flops=6 * pixels * taps * channels,
        nbytes=6 << 20,
        name="interior",
        near=(0,),
        far=(1, 2, 3, 4),
        room=12,
    )(feat_near, cotangent, down_weight, down_bias.reshape(1, channels), up_weight)
    from_above, from_corner, from_left, raw_other = lax.optimization_barrier(
        (from_above, from_corner, from_left, raw_other)
    )
    pieces = half_cols + half_rows
    rim_grads, feat_rim, cot_rim, rim_act, rim_masked, other_a, other_b, bias_sum = call(
        rim_body,
        (
            vm((pieces, channels), BF16),
            vm((pieces, taps), BF16),
            vm((pieces, taps), BF16),
            vm((pieces, channels), BF16),
            vm((pieces, channels), BF16),
            vm((taps // 2 + SIDE, channels), BF16),
            vm((taps // 2, channels), BF16),
            vm((8, channels), F32),
        ),
        scratch=[
            pltpu.VMEM((tile_cols + 8, channels), F32),
            pltpu.VMEM((3, tile_rows + 8, channels), F32),
        ],
        n_in=12,
        flops=1 << 26,
        nbytes=3 << 20,
        name="rim",
        near=tuple(range(10)),
        room=8,
    )(
        feat_patch, cot_patch, feat_firsts, cot_firsts, from_above, from_left, from_corner,
        raw_other, raw_bias, up_mat, down_weight, down_bias,
    )
    got_a = turned(other_a, "narrow", 1)
    got_b = turned(other_b, "narrow", 1)
    mine_a, mine_b = call(
        mine_body,
        (vm((taps // 2, channels), F32), vm((taps // 2, channels), F32)),
        n_in=8,
        flops=2 * pixels * taps * channels,
        nbytes=3 << 20,
        name="mine",
        near=tuple(range(8)),
        room=12,
    )(feat_patch, cot_patch, act, grads, feat_rim, cot_rim, rim_act, rim_masked)
    from_right = turned(rim_grads[half_cols:], "narrow", -1)
    got_a, mine_a, mine_b = lax.optimization_barrier((got_a, mine_a, mine_b))
    got_b, from_right = lax.optimization_barrier((got_b, from_right))
    from_below = turned(
        jnp.concatenate([rim_grads[:half_cols], from_right[:8]], axis=0), "wide", -1
    )

    bits = lax.axis_size("wide").bit_length() - 1
    order_a = list(range(bits))
    order_b = order_a[1::-1] + order_a[2:]
    halvings = 1 if bits <= 3 else 2
    half = taps // 2
    held_a, held_b = mine_a, mine_b
    for step in range(halvings):
        half //= 2
        held_a, send_a, bias_sum = call(
            functools.partial(halve_body, order_a[step]),
            (vm((half, channels), F32), vm((half + SIDE, channels), BF16), vm((8, channels), F32)),
            n_in=3,
            nbytes=half * channels * 12,
            name="halve",
            near=(0, 1, 2),
        )(held_a, got_a, bias_sum)
        held_b, send_b = call(
            functools.partial(halve_body, order_b[step]),
            (vm((half, channels), F32), vm((half, channels), BF16)),
            n_in=2,
            nbytes=half * channels * 12,
            name="halve",
            near=(0, 1),
        )(held_b, got_b)
        got_a = traded(send_a, order_a[step])
        got_b = traded(send_b, order_b[step])
    feature_grad = call(
        feature_body,
        sds((tile_rows, tile_cols, channels), BF16),
        scratch=[
            pltpu.VMEM((half_rows + 1, half_cols + 8, channels), F32),
            pltpu.VMEM((half_rows + 1, half_cols, 2 * channels), BF16),
            pltpu.VMEM((4 * channels, 2 * channels), BF16),
            pltpu.VMEM((2 * channels, 2 * channels), BF16),
            pltpu.VMEM((8, 2, tile_cols, channels), F32),
        ],
        n_in=6,
        flops=2 * pixels * 6 * 2 * channels * channels,
        nbytes=3 << 20,
        name="feature",
        near=(0, 1, 2, 3),
        room=16,
    )(grads, rim_grads, from_right, from_below, cotangent, down_weight)
    for step in range(halvings, bits + 1):
        side = SIDE if step < bits else 0
        held_a, bias_sum = call(
            functools.partial(whole_body, half),
            (vm((half + side, channels), BF16), vm((8, channels), F32)),
            n_in=3,
            nbytes=half * channels * 8,
            name="whole",
            near=(0, 1, 2),
        )(held_a, got_a, bias_sum)
        held_b = call(
            functools.partial(whole_body, half),
            vm((half, channels), BF16),
            n_in=2,
            nbytes=half * channels * 8,
            name="whole",
            near=(0, 1),
        )(held_b, got_b)
        if step < bits:
            got_a = traded(held_a, order_a[step])
            got_b = traded(held_b, order_b[step])
            if step == halvings:
                got_b, from_below = lax.optimization_barrier((got_b, from_below))
            if step == bits - 1:
                got_b, feature_grad = lax.optimization_barrier((got_b, feature_grad))
    for step in reversed(range(halvings)):
        got_a = traded(held_a, order_a[step])
        got_b = traded(held_b, order_b[step])
        if step:
            half *= 2
            held_a = call(
                functools.partial(place_body, order_a[step]),
                vm((half, channels), BF16),
                n_in=2,
                name="place",
                near=(0, 1),
            )(held_a, got_a)
            held_b = call(
                functools.partial(place_body, order_b[step]),
                vm((half, channels), BF16),
                n_in=2,
                name="place",
                near=(0, 1),
            )(held_b, got_b)
    blocks = (held_a, got_a, held_b, got_b)
    far_blocks = [turned(block, "narrow", 1) for block in blocks]
    size = taps // 4
    down, up, bias_grad = call(
        functools.partial(final_body, (order_a[0], order_b[0])),
        (
            sds((4, size, channels), F32),
            sds((4, size, channels), F32),
            sds((1, channels), F32),
        ),
        n_in=9,
        nbytes=12 * taps * channels,
        name="final",
        near=tuple(range(9)),
        room=8,
    )(*blocks, *far_blocks, bias_sum)
    shape = (3, 3, channels, channels)
    return (feature_grad, down.reshape(shape), up.reshape(shape), bias_grad.reshape(channels))


def solution(mesh):
    return jax.shard_map(
        shards,
        mesh=mesh,
        in_specs=(
            P(("groups", "wide"), "narrow", None),
            P(("groups", "wide"), "narrow", None),
            P(),
            P(),
            P(),
        ),
        out_specs=(
            P(("groups", "wide"), "narrow", None),
            P("groups", None, None, None),
            P("groups", None, None, None),
            P("groups"),
        ),
        check_vma=False,
    )
```

```python
import functools

import jax
import jax.numpy as jnp
from jax import lax
from jax.experimental import pallas as pl
from jax.experimental.pallas import tpu as pltpu
from jax.sharding import PartitionSpec as P


F32 = jnp.float32
BF16 = jnp.bfloat16
VM = pl.BlockSpec(memory_space=pltpu.VMEM)
ANY = pl.BlockSpec(memory_space=pl.ANY)
SIDE = 16


def call(body, out_shape, scratch=(), in_specs=None, n_in=0, flops=0, nbytes=0, near=(), far=(), room=4, out_specs=None):
    kernel = pl.pallas_call(
        body,
        out_shape=out_shape,
        in_specs=in_specs if in_specs is not None else [VM] * n_in,
        out_specs=out_specs or jax.tree.map(lambda _: VM, out_shape),
        scratch_shapes=list(scratch),
        compiler_params=pltpu.CompilerParams(vmem_limit_bytes=room << 20),
        cost_estimate=pl.CostEstimate(flops=flops, transcendentals=0, bytes_accessed=nbytes),
    )

    def run(*args):
        placed = [
            pltpu.with_memory_space_constraint(arg, pltpu.VMEM if at in near else pltpu.HBM)
            if at in near or at in far
            else arg
            for at, arg in enumerate(args)
        ]
        return kernel(*placed)

    return run


def vm(shape, dtype):
    return pltpu.VMEM(shape, dtype)


def sds(shape, dtype):
    return jax.ShapeDtypeStruct(shape, dtype)


def edge_body(
    feat, cot, down, up, bias, feat_near, cot_near, down_near, up_near, bias_near,
    rows, cols, corner, strip, wide_strip, sems,
):
    tile_rows, tile_cols, _ = feat.shape
    copies = []
    for which, ref in enumerate((feat, cot)):
        copies.append(
            pltpu.make_async_copy(ref.at[tile_rows - 1], rows.at[which], sems.at[2 * which])
        )
        copies.append(
            pltpu.make_async_copy(
                ref.at[:, pl.ds(tile_cols - 16, 16), :], strip.at[which], sems.at[2 * which + 1]
            )
        )
    bulk = [
        pltpu.make_async_copy(feat, feat_near, sems.at[4]),
        pltpu.make_async_copy(cot, cot_near, sems.at[5]),
        pltpu.make_async_copy(down, down_near, sems.at[6]),
        pltpu.make_async_copy(up, up_near, sems.at[7]),
        pltpu.make_async_copy(bias, bias_near, sems.at[8]),
    ]
    for copy in copies + bulk:
        copy.start()
    for copy in copies:
        copy.wait()
    for which in range(2):
        wide_strip[...] = strip[which].astype(F32).reshape(wide_strip.shape)
        cols[which] = wide_strip[pl.ds(15, tile_rows, stride=16), :].astype(BF16)
        corner[which] = wide_strip[tile_rows * 16 - 8 :, :].astype(BF16)
    for copy in bulk:
        copy.wait()


def if_any(there, value):
    return jnp.where(there, value, jnp.zeros_like(value))


def own_patches(tile, wide, strip, patch, firsts):
    rows, cols, channels = tile.shape
    half_rows, half_cols = rows // 2, cols // 2
    wide[:, :, 0:8, :] = jnp.zeros((half_rows, 2, 8, channels), F32)
    wide[:, :, 8:, :] = tile[...].astype(F32).reshape(half_rows, 2, cols, channels)
    for col_off in range(3):
        lanes = [pl.ds((3 * row_off + col_off) * channels, channels) for row_off in range(3)]
        taken = pl.ds(7 + col_off, half_cols, stride=2)
        patch[:, :, lanes[1]] = wide[:, 0, taken, :].astype(BF16)
        odd = wide[:, 1, taken, :].astype(BF16)
        patch[:, :, lanes[2]] = odd
        patch[1:, :, lanes[0]] = odd[:-1]
        patch[0, :, lanes[0]] = jnp.zeros((half_cols, channels), BF16)
    strip[...] = tile[:, 0:16, :].astype(F32).reshape(strip.shape)
    for col in range(2):
        firsts[col] = strip[pl.ds(col, rows, stride=16), :].astype(BF16)


def pointwise(pre, act_grad):
    sigm = 1.0 / (1.0 + jnp.exp(-pre))
    return pre * sigm, act_grad * sigm * (1.0 + pre * (1.0 - sigm))


def taps_of(core_is, patch, values):
    if core_is:
        return lax.dot_general(
            patch, values, (((0,), (0,)), ((), ())), preferred_element_type=F32
        )
    channels = values.shape[1]
    rows = lax.dot_general(values, patch, (((0,), (0,)), ((), ())), preferred_element_type=F32)
    return jnp.concatenate(
        [rows[:, tap * channels : (tap + 1) * channels] for tap in range(9)], axis=0
    )


def interior_body(
    feat, cot, down_weight, down_bias, up_weight,
    feat_patch, cot_patch, act, grads, raw_other, raw_bias, feat_firsts, cot_firsts, up_mat,
    wide, strip,
):
    rows, cols, channels = feat.shape
    half_rows, half_cols = rows // 2, cols // 2
    pixels = half_rows * half_cols
    taps = 9 * channels
    own_patches(feat, wide, strip, feat_patch, feat_firsts)
    own_patches(cot, wide, strip, cot_patch, cot_firsts)
    for tap in range(9):
        up_mat[:, pl.ds(tap * channels, channels)] = up_weight[tap // 3, tap % 3]
    down_mat = down_weight[...].reshape(taps, channels)
    bias_row = down_bias[...].reshape(1, channels)
    step = 8
    count = step * half_cols
    total = jnp.zeros((1, channels), F32)
    at = lax.broadcasted_iota(jnp.int32, (count, channels), 0)
    for start in range(0, half_rows, step):
        span = pl.ds(start * half_cols, count)
        feat_rows = feat_patch[start : start + step].reshape(count, taps)
        cot_rows = cot_patch[start : start + step].reshape(count, taps)
        pre = jnp.dot(feat_rows, down_mat, preferred_element_type=F32) + bias_row
        act_grad = lax.dot_general(
            cot_rows, up_mat[...], (((1,), (1,)), ((), ())), preferred_element_type=F32
        )
        inside = lax.rem(at, half_cols) > 0
        if start == 0:
            inside = inside & (at >= half_cols)
        value, grad = pointwise(pre, act_grad)
        act[span, :] = if_any(inside, value).astype(BF16)
        grad = if_any(inside, grad).astype(BF16)
        grads[span, :] = grad
        total = total + jnp.sum(grad.astype(F32), axis=0, keepdims=True)
    raw_bias[...] = jnp.broadcast_to(total, raw_bias.shape)
    core = lax.axis_index("narrow")

    @pl.when(core == 0)
    def _():
        raw_other[...] = taps_of(False, cot_patch[...].reshape(pixels, taps), act[...])

    @pl.when(core != 0)
    def _():
        raw_other[...] = taps_of(True, feat_patch[...].reshape(pixels, taps), grads[...])


def rim_patches(patch, firsts, top, left, corner, out, line, column):
    half_rows, half_cols, taps = patch.shape
    channels = taps // 9
    above = lax.axis_index("wide") > 0
    aside = lax.axis_index("narrow") > 0
    line[0:8, :] = if_any(above & aside, corner[...].astype(F32))
    line[8:, :] = if_any(above, top[...].astype(F32))
    column[0, 0:8, :] = line[0:8, :]
    column[0, 8:, :] = if_any(aside, left[...].astype(F32))
    for col in range(2):
        column[1 + col, 0:8, :] = jnp.zeros((8, channels), F32)
        column[1 + col, 8:, :] = firsts[col].astype(F32)
    out[0:half_cols, 3 * channels :] = patch[0, :, 3 * channels :]
    first = lax.broadcasted_iota(jnp.int32, (half_cols, channels), 0) == 0
    for off in range(3):
        out[0:half_cols, off * channels : (off + 1) * channels] = line[
            pl.ds(7 + off, half_cols, stride=2), :
        ].astype(BF16)
        for col_off in range(3):
            lanes = slice((3 * off + col_off) * channels, (3 * off + col_off + 1) * channels)
            out[half_cols:, lanes] = column[
                col_off, pl.ds(7 + off, half_rows, stride=2), :
            ].astype(BF16)
    for off in (1, 2):
        lanes = slice(3 * off * channels, (3 * off + 1) * channels)
        rest = patch[0, :, lanes].astype(F32)
        halo = jnp.broadcast_to(column[0, 7 + off : 8 + off, :], rest.shape)
        out[0:half_cols, lanes] = jnp.where(first, halo, rest).astype(BF16)


def rim_body(
    feat_patch, cot_patch, feat_firsts, cot_firsts, top, left, corner, raw_other, raw_bias,
    up_mat, down_weight, down_bias,
    rim_grads, feat_rim, cot_rim, rim_act, rim_masked, other_a, other_b, bias_part,
    line, column,
):
    _, half_cols, taps = feat_patch.shape
    channels = taps // 9
    half = taps // 2
    rim_patches(
        feat_patch, feat_firsts, top.at[0], left.at[0], corner.at[0], feat_rim, line, column
    )
    rim_patches(cot_patch, cot_firsts, top.at[1], left.at[1], corner.at[1], cot_rim, line, column)
    pre = jnp.dot(
        feat_rim[...], down_weight[...].reshape(taps, channels), preferred_element_type=F32
    ) + down_bias[...].reshape(1, channels)
    act_grad = lax.dot_general(
        cot_rim[...], up_mat[...], (((1,), (1,)), ((), ())), preferred_element_type=F32
    )
    value, grad = pointwise(pre, act_grad)
    once = lax.broadcasted_iota(jnp.int32, value.shape, 0) != half_cols
    act = if_any(once, value).astype(BF16)
    masked = if_any(once, grad).astype(BF16)
    rim_act[...] = act
    rim_masked[...] = masked
    full = grad.astype(BF16).astype(F32)
    rim_grads[...] = jnp.where(once, full, jnp.broadcast_to(full[0:1], full.shape)).astype(BF16)
    total = raw_bias[0:1, :] + jnp.sum(masked.astype(F32), axis=0, keepdims=True)
    coarse = total.astype(BF16)
    fine = (total - coarse.astype(F32)).astype(BF16)
    bias_part[...] = jnp.broadcast_to(coarse.astype(F32) + fine.astype(F32), bias_part.shape)
    put_side(other_a, half, coarse, fine)
    core = lax.axis_index("narrow")

    def give(more):
        other_a[0:half, :] = (raw_other[0:half, :] + more[0:half]).astype(BF16)
        other_b[...] = (raw_other[half:, :] + more[half:]).astype(BF16)

    @pl.when(core == 0)
    def _():
        give(taps_of(False, cot_rim[...], act))

    @pl.when(core != 0)
    def _():
        give(taps_of(True, feat_rim[...], masked))


def mine_body(
    feat_patch, cot_patch, act, grads, feat_rim, cot_rim, rim_act, rim_masked, mine_a, mine_b
):
    half_rows, half_cols, taps = feat_patch.shape
    pixels = half_rows * half_cols
    half = taps // 2
    core = lax.axis_index("narrow")

    def keep(which, patch, values, rim_patch, rim_values):
        total = taps_of(which, patch[...].reshape(pixels, taps), values[...])
        total = total + taps_of(which, rim_patch[...], rim_values[...])
        mine_a[...] = total[0:half]
        mine_b[...] = total[half:]

    @pl.when(core == 0)
    def _():
        keep(True, feat_patch, grads, feat_rim, rim_masked)

    @pl.when(core != 0)
    def _():
        keep(False, cot_patch, act, cot_rim, rim_act)


def put_side(out, at, coarse, fine):
    channels = out.shape[1]
    row = lax.broadcasted_iota(jnp.int32, (SIDE, channels), 0)
    block = jnp.where(row == 0, coarse.astype(F32), jnp.where(row == 1, fine.astype(F32), 0.0))
    out[at : at + SIDE, :] = block.astype(BF16)


def take_side(ref, at):
    block = ref[at : at + SIDE, :].astype(F32)
    return block[0:1] + block[1:2]


def bit_of(position):
    return lax.rem(lax.shift_right_logical(lax.axis_index("wide"), jnp.int32(position)), 2)


def joined_bias(bias_in, got, size, out, sent, at):
    total = bias_in[0:1, :] + take_side(got, size)
    coarse = total.astype(BF16)
    fine = (total - coarse.astype(F32)).astype(BF16)
    out[...] = jnp.broadcast_to(coarse.astype(F32) + fine.astype(F32), out.shape)
    if sent is not None:
        put_side(sent, at, coarse, fine)


def split(position, held, got, base, size, keep, send):
    half = size // 2
    bit = bit_of(position)
    near = pl.ds(pl.multiple_of(base + bit * half, 16), half)
    away = pl.ds(pl.multiple_of(base + (1 - bit) * half, 16), half)
    send[0:half, :] = (held[away, :] + got[away, :].astype(F32)).astype(BF16)
    keep[...] = held[near, :] + got[near, :].astype(F32)


def halve_body(position, held, got, *rest):
    size = held.shape[0]
    if len(rest) == 4:
        bias_in, keep, send, bias_out = rest
        joined_bias(bias_in, got, size, bias_out, send, size // 2)
    else:
        keep, send = rest
    split(position, held, got, 0, size, keep, send)


def whole_body(size, held, got, *rest):
    send = rest[-2] if len(rest) == 3 else rest[-1]
    send[0:size, :] = (held[0:size, :].astype(F32) + got[0:size, :].astype(F32)).astype(BF16)
    if len(rest) == 3:
        bias_in, _, bias_out = rest
        joined_bias(bias_in, got, size, bias_out, send if send.shape[0] > size else None, size)


def place_body(position, held, got, out):
    place(position, held, got, out, 0)


def place(position, held, got, out, base):
    size = held.shape[0]
    bit = bit_of(position)
    out[pl.ds(pl.multiple_of(base + bit * size, 16), size), :] = held[...]
    out[pl.ds(pl.multiple_of(base + (1 - bit) * size, 16), size), :] = got[...]


def final_body(
    positions, held_a, got_a, held_b, got_b, far_held_a, far_got_a, far_held_b, far_got_b, bias_in,
    down, up, bias_out,
):
    channels = held_a.shape[1]
    core = lax.axis_index("narrow")
    bit_a, bit_b = bit_of(positions[0]), bit_of(positions[1])

    def square(ref):
        block = ref[...].astype(F32).reshape(-1, 8, channels)
        return jnp.sum(block * block, axis=0)

    def pair(one, two, three, four):
        return (square(one) + square(two)) + (square(three) + square(four))

    squares = pair(held_a, got_a, held_b, got_b) + pair(
        far_held_a, far_got_a, far_held_b, far_got_b
    )
    bias = bias_in[0:1, :]
    total = jnp.sum(jnp.sum(squares, axis=0, keepdims=True) + bias * bias, axis=1, keepdims=True)
    clip_level = 0.5 * float(18 * channels * channels + channels) ** 0.5
    factor = jnp.minimum(1.0, clip_level / jnp.sqrt(total))
    factor = jnp.broadcast_to(factor, (1, channels))
    bias_out[...] = bias * factor
    spots = (bit_a, 1 - bit_a, 2 + bit_b, 3 - bit_b)
    for at, (near_ref, far_ref) in enumerate(
        ((held_a, far_held_a), (got_a, far_got_a), (held_b, far_held_b), (got_b, far_got_b))
    ):
        near_block = near_ref[...].astype(F32) * factor
        far_block = far_ref[...].astype(F32) * factor

        @pl.when(core == 0)
        def _():
            down[spots[at]] = near_block
            up[spots[at]] = far_block

        @pl.when(core != 0)
        def _():
            up[spots[at]] = near_block
            down[spots[at]] = far_block


def feature_body(grads, rim_grads, right, below, cot, down_weight, out, wide, pairs, near_mat, low_mat, woven):
    tile_rows, tile_cols, channels = cot.shape
    half_rows, half_cols = tile_rows // 2, tile_cols // 2
    wide[0:half_rows, 0:half_cols, :] = grads[...].astype(F32).reshape(
        half_rows, half_cols, channels
    )
    last = lax.broadcasted_iota(jnp.int32, (half_rows, 8, channels), 1) == 0
    own = rim_grads[half_cols:, :].astype(F32).reshape(half_rows, 1, channels)
    wide[0:half_rows, 0:8, :] = jnp.where(last, own, wide[0:half_rows, 0:8, :])
    wide[0, 0:half_cols, :] = rim_grads[0:half_cols, :].astype(F32)
    aside = lax.axis_index("narrow") < lax.axis_size("narrow") - 1
    under = lax.axis_index("wide") < lax.axis_size("wide") - 1
    rim = if_any(aside, right[...].astype(F32)).reshape(half_rows, 1, channels)
    wide[0:half_rows, half_cols:, :] = jnp.where(last, rim, 0.0)
    wide[half_rows, 0:half_cols, :] = if_any(under, below[0:half_cols, :].astype(F32))
    wide[half_rows, half_cols:, :] = if_any(under & aside, below[half_cols:, :].astype(F32))
    pairs[:, :, 0:channels] = wide[:, 0:half_cols, :].astype(BF16)
    pairs[:, :, channels:] = wide[:, 1 : half_cols + 1, :].astype(BF16)
    zero = jnp.zeros((channels, channels), BF16)
    blocks = [(1, 1, None), (1, 2, 0), (2, 1, None), (2, 2, 0)]
    for at, (row_off, here, next_off) in enumerate(blocks):
        rows = slice(at * channels, (at + 1) * channels)
        near_mat[rows, 0:channels] = down_weight[row_off, here]
        near_mat[rows, channels:] = zero if next_off is None else down_weight[row_off, next_off]
    for at, (here, next_off) in enumerate([(1, None), (2, 0)]):
        rows = slice(at * channels, (at + 1) * channels)
        low_mat[rows, 0:channels] = down_weight[0, here]
        low_mat[rows, channels:] = zero if next_off is None else down_weight[0, next_off]
    step = 8
    dims = (((1,), (1,)), ((), ()))
    for start in range(0, half_rows, step):
        count = step * half_cols
        here = pairs[start : start + step].reshape(count, 2 * channels)
        lower = pairs[start + 1 : start + 1 + step].reshape(count, 2 * channels)
        near = lax.dot_general(here, near_mat[...], dims, preferred_element_type=F32)
        far = lax.dot_general(lower, low_mat[...], dims, preferred_element_type=F32)
        shape = (step, half_cols, channels)
        for row_par in range(2):
            for col_par in range(2):
                lanes = slice((2 * row_par + col_par) * channels, (2 * row_par + col_par + 1) * channels)
                value = near[:, lanes]
                if row_par:
                    value = value + far[:, col_par * channels : (col_par + 1) * channels]
                woven[:, row_par, pl.ds(col_par, half_cols, stride=2), :] = value.reshape(shape)
        span = slice(2 * start, 2 * (start + step))
        total = cot[span].astype(F32) + woven[...].reshape(2 * step, tile_cols, channels)
        out[span] = total.astype(BF16)


def turned(value, axis, steps):
    count = lax.axis_size(axis)
    return lax.ppermute(value, axis, [(at, (at + steps) % count) for at in range(count)])


def turned_both(value):
    count, cores = lax.axis_size("wide"), lax.axis_size("narrow")
    pairs = [
        (at * cores + core, (at + 1) % count * cores + (core + 1) % cores)
        for at in range(count)
        for core in range(cores)
    ]
    return lax.ppermute(value, ("wide", "narrow"), pairs)


def traded(value, position):
    count = lax.axis_size("wide")
    return lax.ppermute(value, "wide", [(at, at ^ (1 << position)) for at in range(count)])


def program(features, cotangent, down_weight, down_bias, up_weight):
    tile_rows, tile_cols, channels = features.shape
    half_rows, half_cols = tile_rows // 2, tile_cols // 2
    pixels = half_rows * half_cols
    taps = 9 * channels
    feat_near, cot_near, down_near, up_near, bias_near, rows, cols, corner = call(
        edge_body,
        (
            vm(features.shape, BF16),
            vm(features.shape, BF16),
            vm(down_weight.shape, BF16),
            vm(up_weight.shape, BF16),
            vm((1, channels), F32),
            vm((2, tile_cols, channels), BF16),
            vm((2, tile_rows, channels), BF16),
            vm((2, 8, channels), BF16),
        ),
        scratch=[
            pltpu.VMEM((2, tile_rows, 16, channels), BF16),
            pltpu.VMEM((tile_rows * 16, channels), F32),
            pltpu.SemaphoreType.DMA((9,)),
        ],
        in_specs=[ANY] * 5,
        nbytes=1 << 19,
        far=(0, 1, 2, 3, 4),
        room=8,
    )(features, cotangent, down_weight, up_weight, down_bias.reshape(1, channels))
    from_above = turned(rows, "wide", 1)
    from_corner = turned_both(corner)
    from_left = turned(cols, "narrow", 1)
    patches = vm((half_rows, half_cols, taps), BF16)
    firsts = vm((2, tile_rows, channels), BF16)
    (
        feat_patch, cot_patch, act, grads, raw_other, raw_bias, feat_firsts, cot_firsts, up_mat
    ) = call(
        interior_body,
        (
            patches,
            patches,
            vm((pixels, channels), BF16),
            vm((pixels, channels), BF16),
            vm((taps, channels), F32),
            vm((8, channels), F32),
            firsts,
            firsts,
            vm((channels, taps), BF16),
        ),
        scratch=[
            pltpu.VMEM((half_rows, 2, tile_cols + 8, channels), F32),
            pltpu.VMEM((tile_rows * 16, channels), F32),
        ],
        n_in=5,
        flops=6 * pixels * taps * channels,
        nbytes=6 << 20,
        near=(0, 1, 2, 3, 4),
        room=12,
    )(feat_near, cot_near, down_near, bias_near, up_near)
    from_above, from_corner, from_left, raw_other = lax.optimization_barrier(
        (from_above, from_corner, from_left, raw_other)
    )
    pieces = half_cols + half_rows
    rim_grads, feat_rim, cot_rim, rim_act, rim_masked, other_a, other_b, bias_sum = call(
        rim_body,
        (
            vm((pieces, channels), BF16),
            vm((pieces, taps), BF16),
            vm((pieces, taps), BF16),
            vm((pieces, channels), BF16),
            vm((pieces, channels), BF16),
            vm((taps // 2 + SIDE, channels), BF16),
            vm((taps // 2, channels), BF16),
            vm((8, channels), F32),
        ),
        scratch=[
            pltpu.VMEM((tile_cols + 8, channels), F32),
            pltpu.VMEM((3, tile_rows + 8, channels), F32),
        ],
        n_in=12,
        flops=1 << 26,
        nbytes=3 << 20,
        near=tuple(range(12)),
        room=8,
    )(
        feat_patch, cot_patch, feat_firsts, cot_firsts, from_above, from_left, from_corner,
        raw_other, raw_bias, up_mat, down_near, bias_near,
    )
    got_a = turned(other_a, "narrow", 1)
    got_b = turned(other_b, "narrow", 1)
    mine_a, mine_b = call(
        mine_body,
        (vm((taps // 2, channels), F32), vm((taps // 2, channels), F32)),
        n_in=8,
        flops=2 * pixels * taps * channels,
        nbytes=3 << 20,
        near=tuple(range(8)),
        room=12,
    )(feat_patch, cot_patch, act, grads, feat_rim, cot_rim, rim_act, rim_masked)
    from_right = turned(rim_grads[half_cols:], "narrow", -1)
    got_a, mine_a, mine_b = lax.optimization_barrier((got_a, mine_a, mine_b))
    got_b, from_right = lax.optimization_barrier((got_b, from_right))
    from_below = turned(
        jnp.concatenate([rim_grads[:half_cols], from_right[:8]], axis=0), "wide", -1
    )

    bits = lax.axis_size("wide").bit_length() - 1
    order_a = list(range(bits))
    order_b = order_a[1::-1] + order_a[2:]
    halvings = 1 if bits <= 3 else 2
    half = taps // 2
    held_a, held_b = mine_a, mine_b
    for step in range(halvings):
        half //= 2
        held_a, send_a, bias_sum = call(
            functools.partial(halve_body, order_a[step]),
            (vm((half, channels), F32), vm((half + SIDE, channels), BF16), vm((8, channels), F32)),
            n_in=3,
            nbytes=half * channels * 12,
            near=(0, 1, 2),
        )(held_a, got_a, bias_sum)
        held_b, send_b = call(
            functools.partial(halve_body, order_b[step]),
            (vm((half, channels), F32), vm((half, channels), BF16)),
            n_in=2,
            nbytes=half * channels * 12,
            near=(0, 1),
        )(held_b, got_b)
        got_a = traded(send_a, order_a[step])
        got_b = traded(send_b, order_b[step])
    feature_grad = call(
        feature_body,
        sds((tile_rows, tile_cols, channels), BF16),
        scratch=[
            pltpu.VMEM((half_rows + 1, half_cols + 8, channels), F32),
            pltpu.VMEM((half_rows + 1, half_cols, 2 * channels), BF16),
            pltpu.VMEM((4 * channels, 2 * channels), BF16),
            pltpu.VMEM((2 * channels, 2 * channels), BF16),
            pltpu.VMEM((8, 2, tile_cols, channels), F32),
        ],
        n_in=6,
        flops=2 * pixels * 6 * 2 * channels * channels,
        nbytes=3 << 20,
        near=(0, 1, 2, 3, 4, 5),
        room=16,
    )(grads, rim_grads, from_right, from_below, cot_near, down_near)
    for step in range(halvings, bits + 1):
        side = SIDE if step < bits else 0
        held_a, bias_sum = call(
            functools.partial(whole_body, half),
            (vm((half + side, channels), BF16), vm((8, channels), F32)),
            n_in=3,
            nbytes=half * channels * 8,
            near=(0, 1, 2),
        )(held_a, got_a, bias_sum)
        held_b = call(
            functools.partial(whole_body, half),
            vm((half, channels), BF16),
            n_in=2,
            nbytes=half * channels * 8,
            near=(0, 1),
        )(held_b, got_b)
        if step < bits:
            got_a = traded(held_a, order_a[step])
            got_b = traded(held_b, order_b[step])
            if step == halvings:
                got_b, from_below = lax.optimization_barrier((got_b, from_below))
            if step == bits - 1:
                got_b, feature_grad = lax.optimization_barrier((got_b, feature_grad))
    for step in reversed(range(halvings)):
        got_a = traded(held_a, order_a[step])
        got_b = traded(held_b, order_b[step])
        if step:
            half *= 2
            held_a = call(
                functools.partial(place_body, order_a[step]),
                vm((half, channels), BF16),
                n_in=2,
                near=(0, 1),
            )(held_a, got_a)
            held_b = call(
                functools.partial(place_body, order_b[step]),
                vm((half, channels), BF16),
                n_in=2,
                near=(0, 1),
            )(held_b, got_b)
    blocks = (held_a, got_a, held_b, got_b)
    far_blocks = []
    for block in blocks:
        far_blocks.append(turned(block, "narrow", 1))
    size = taps // 4
    down, up, bias_grad = call(
        functools.partial(final_body, (order_a[0], order_b[0])),
        (
            sds((4, size, channels), F32),
            sds((4, size, channels), F32),
            sds((1, channels), F32),
        ),
        n_in=9,
        nbytes=12 * taps * channels,
        near=tuple(range(9)),
        room=8,
    )(*blocks, *far_blocks, bias_sum)
    shape = (3, 3, channels, channels)
    return (feature_grad, down.reshape(shape), up.reshape(shape), bias_grad.reshape(channels))


def solution(mesh):
    return jax.shard_map(
        program,
        mesh=mesh,
        in_specs=(
            P(("groups", "wide"), "narrow", None),
            P(("groups", "wide"), "narrow", None),
            P(),
            P(),
            P(),
        ),
        out_specs=(
            P(("groups", "wide"), "narrow", None),
            P("groups", None, None, None),
            P("groups", None, None, None),
            P("groups"),
        ),
        check_vma=False,
    )
```

```python
import functools

import jax
import jax.numpy as jnp
from jax import lax
from jax.experimental import pallas as pl
from jax.experimental.pallas import tpu as pltpu
from jax.sharding import PartitionSpec as P


F32 = jnp.float32
BF16 = jnp.bfloat16
VM = pl.BlockSpec(memory_space=pltpu.VMEM)
ANY = pl.BlockSpec(memory_space=pl.ANY)
SIDE = 16


def call(body, out_shape, scratch=(), in_specs=None, n_in=0, flops=0, nbytes=0, near=(), far=(), room=4, out_specs=None):
    kernel = pl.pallas_call(
        body,
        out_shape=out_shape,
        in_specs=in_specs if in_specs is not None else [VM] * n_in,
        out_specs=out_specs or jax.tree.map(lambda _: VM, out_shape),
        scratch_shapes=list(scratch),
        compiler_params=pltpu.CompilerParams(vmem_limit_bytes=room << 20),
        cost_estimate=pl.CostEstimate(flops=flops, transcendentals=0, bytes_accessed=nbytes),
    )

    def run(*args):
        placed = [
            pltpu.with_memory_space_constraint(arg, pltpu.VMEM if at in near else pltpu.HBM)
            if at in near or at in far
            else arg
            for at, arg in enumerate(args)
        ]
        return kernel(*placed)

    return run


def vm(shape, dtype):
    return pltpu.VMEM(shape, dtype)


def sds(shape, dtype):
    return jax.ShapeDtypeStruct(shape, dtype)


def edge_body(
    feat, cot, down, up, bias, feat_near, cot_near, down_near, up_near, bias_near,
    rows, cols, corner, strip, wide_strip, sems,
):
    tile_rows, tile_cols, _ = feat.shape
    copies = []
    for which, ref in enumerate((feat, cot)):
        copies.append(
            pltpu.make_async_copy(ref.at[tile_rows - 1], rows.at[which], sems.at[2 * which])
        )
        copies.append(
            pltpu.make_async_copy(
                ref.at[:, pl.ds(tile_cols - 16, 16), :], strip.at[which], sems.at[2 * which + 1]
            )
        )
    bulk = [
        pltpu.make_async_copy(feat, feat_near, sems.at[4]),
        pltpu.make_async_copy(cot, cot_near, sems.at[5]),
        pltpu.make_async_copy(down, down_near, sems.at[6]),
        pltpu.make_async_copy(up, up_near, sems.at[7]),
        pltpu.make_async_copy(bias, bias_near, sems.at[8]),
    ]
    for copy in copies + bulk:
        copy.start()
    for copy in copies:
        copy.wait()
    for which in range(2):
        wide_strip[...] = strip[which].astype(F32).reshape(wide_strip.shape)
        cols[which] = wide_strip[pl.ds(15, tile_rows, stride=16), :].astype(BF16)
        corner[which] = wide_strip[tile_rows * 16 - 8 :, :].astype(BF16)
    for copy in bulk:
        copy.wait()


def if_any(there, value):
    return jnp.where(there, value, jnp.zeros_like(value))


def own_patches(tile, wide, strip, patch, firsts):
    rows, cols, channels = tile.shape
    half_rows, half_cols = rows // 2, cols // 2
    wide[:, :, 0:8, :] = jnp.zeros((half_rows, 2, 8, channels), F32)
    wide[:, :, 8:, :] = tile[...].astype(F32).reshape(half_rows, 2, cols, channels)
    for col_off in range(3):
        lanes = [pl.ds((3 * row_off + col_off) * channels, channels) for row_off in range(3)]
        taken = pl.ds(7 + col_off, half_cols, stride=2)
        patch[:, :, lanes[1]] = wide[:, 0, taken, :].astype(BF16)
        odd = wide[:, 1, taken, :].astype(BF16)
        patch[:, :, lanes[2]] = odd
        patch[1:, :, lanes[0]] = odd[:-1]
        patch[0, :, lanes[0]] = jnp.zeros((half_cols, channels), BF16)
    strip[...] = tile[:, 0:16, :].astype(F32).reshape(strip.shape)
    for col in range(2):
        firsts[col] = strip[pl.ds(col, rows, stride=16), :].astype(BF16)


def pointwise(pre, act_grad):
    sigm = 1.0 / (1.0 + jnp.exp(-pre))
    return pre * sigm, act_grad * sigm * (1.0 + pre * (1.0 - sigm))


def taps_of(core_is, patch, values):
    if core_is:
        return lax.dot_general(
            patch, values, (((0,), (0,)), ((), ())), preferred_element_type=F32
        )
    channels = values.shape[1]
    rows = lax.dot_general(values, patch, (((0,), (0,)), ((), ())), preferred_element_type=F32)
    return jnp.concatenate(
        [rows[:, tap * channels : (tap + 1) * channels] for tap in range(9)], axis=0
    )


def interior_body(
    feat, cot, down_weight, down_bias, up_weight,
    feat_patch, cot_patch, act, grads, raw_other, raw_bias, feat_firsts, cot_firsts, up_mat,
    wide, strip,
):
    rows, cols, channels = feat.shape
    half_rows, half_cols = rows // 2, cols // 2
    pixels = half_rows * half_cols
    taps = 9 * channels
    own_patches(feat, wide, strip, feat_patch, feat_firsts)
    own_patches(cot, wide, strip, cot_patch, cot_firsts)
    for tap in range(9):
        up_mat[:, pl.ds(tap * channels, channels)] = up_weight[tap // 3, tap % 3]
    down_mat = down_weight[...].reshape(taps, channels)
    bias_row = down_bias[...].reshape(1, channels)
    step = 8
    count = step * half_cols
    total = jnp.zeros((1, channels), F32)
    at = lax.broadcasted_iota(jnp.int32, (count, channels), 0)
    for start in range(0, half_rows, step):
        span = pl.ds(start * half_cols, count)
        feat_rows = feat_patch[start : start + step].reshape(count, taps)
        cot_rows = cot_patch[start : start + step].reshape(count, taps)
        pre = jnp.dot(feat_rows, down_mat, preferred_element_type=F32) + bias_row
        act_grad = lax.dot_general(
            cot_rows, up_mat[...], (((1,), (1,)), ((), ())), preferred_element_type=F32
        )
        inside = lax.rem(at, half_cols) > 0
        if start == 0:
            inside = inside & (at >= half_cols)
        value, grad = pointwise(pre, act_grad)
        act[span, :] = if_any(inside, value).astype(BF16)
        grad = if_any(inside, grad).astype(BF16)
        grads[span, :] = grad
        total = total + jnp.sum(grad.astype(F32), axis=0, keepdims=True)
    raw_bias[...] = jnp.broadcast_to(total, raw_bias.shape)
    core = lax.axis_index("narrow")

    @pl.when(core == 0)
    def _():
        raw_other[...] = taps_of(False, cot_patch[...].reshape(pixels, taps), act[...])

    @pl.when(core != 0)
    def _():
        raw_other[...] = taps_of(True, feat_patch[...].reshape(pixels, taps), grads[...])


def rim_patches(patch, firsts, top, left, corner, out, line, column):
    half_rows, half_cols, taps = patch.shape
    channels = taps // 9
    above = lax.axis_index("wide") > 0
    aside = lax.axis_index("narrow") > 0
    line[0:8, :] = if_any(above & aside, corner[...].astype(F32))
    line[8:, :] = if_any(above, top[...].astype(F32))
    column[0, 0:8, :] = line[0:8, :]
    column[0, 8:, :] = if_any(aside, left[...].astype(F32))
    for col in range(2):
        column[1 + col, 0:8, :] = jnp.zeros((8, channels), F32)
        column[1 + col, 8:, :] = firsts[col].astype(F32)
    out[0:half_cols, 3 * channels :] = patch[0, :, 3 * channels :]
    first = lax.broadcasted_iota(jnp.int32, (half_cols, channels), 0) == 0
    for off in range(3):
        out[0:half_cols, off * channels : (off + 1) * channels] = line[
            pl.ds(7 + off, half_cols, stride=2), :
        ].astype(BF16)
        for col_off in range(3):
            lanes = slice((3 * off + col_off) * channels, (3 * off + col_off + 1) * channels)
            out[half_cols:, lanes] = column[
                col_off, pl.ds(7 + off, half_rows, stride=2), :
            ].astype(BF16)
    for off in (1, 2):
        lanes = slice(3 * off * channels, (3 * off + 1) * channels)
        rest = patch[0, :, lanes].astype(F32)
        halo = jnp.broadcast_to(column[0, 7 + off : 8 + off, :], rest.shape)
        out[0:half_cols, lanes] = jnp.where(first, halo, rest).astype(BF16)


def rim_body(
    feat_patch, cot_patch, feat_firsts, cot_firsts, top, left, corner, raw_other, raw_bias,
    up_mat, down_weight, down_bias,
    rim_grads, feat_rim, cot_rim, rim_act, rim_masked, other_a, other_b, bias_part,
    line, column,
):
    _, half_cols, taps = feat_patch.shape
    channels = taps // 9
    half = taps // 2
    rim_patches(
        feat_patch, feat_firsts, top.at[0], left.at[0], corner.at[0], feat_rim, line, column
    )
    rim_patches(cot_patch, cot_firsts, top.at[1], left.at[1], corner.at[1], cot_rim, line, column)
    pre = jnp.dot(
        feat_rim[...], down_weight[...].reshape(taps, channels), preferred_element_type=F32
    ) + down_bias[...].reshape(1, channels)
    act_grad = lax.dot_general(
        cot_rim[...], up_mat[...], (((1,), (1,)), ((), ())), preferred_element_type=F32
    )
    value, grad = pointwise(pre, act_grad)
    once = lax.broadcasted_iota(jnp.int32, value.shape, 0) != half_cols
    act = if_any(once, value).astype(BF16)
    masked = if_any(once, grad).astype(BF16)
    rim_act[...] = act
    rim_masked[...] = masked
    full = grad.astype(BF16).astype(F32)
    rim_grads[...] = jnp.where(once, full, jnp.broadcast_to(full[0:1], full.shape)).astype(BF16)
    total = raw_bias[0:1, :] + jnp.sum(masked.astype(F32), axis=0, keepdims=True)
    coarse = total.astype(BF16)
    fine = (total - coarse.astype(F32)).astype(BF16)
    bias_part[...] = jnp.broadcast_to(coarse.astype(F32) + fine.astype(F32), bias_part.shape)
    put_side(other_a, half, coarse, fine)
    core = lax.axis_index("narrow")

    def give(more):
        other_a[0:half, :] = (raw_other[0:half, :] + more[0:half]).astype(BF16)
        other_b[...] = (raw_other[half:, :] + more[half:]).astype(BF16)

    @pl.when(core == 0)
    def _():
        give(taps_of(False, cot_rim[...], act))

    @pl.when(core != 0)
    def _():
        give(taps_of(True, feat_rim[...], masked))


def mine_body(
    feat_patch, cot_patch, act, grads, feat_rim, cot_rim, rim_act, rim_masked, mine_a, mine_b
):
    half_rows, half_cols, taps = feat_patch.shape
    pixels = half_rows * half_cols
    half = taps // 2
    core = lax.axis_index("narrow")

    def keep(which, patch, values, rim_patch, rim_values):
        total = taps_of(which, patch[...].reshape(pixels, taps), values[...])
        total = total + taps_of(which, rim_patch[...], rim_values[...])
        mine_a[...] = total[0:half]
        mine_b[...] = total[half:]

    @pl.when(core == 0)
    def _():
        keep(True, feat_patch, grads, feat_rim, rim_masked)

    @pl.when(core != 0)
    def _():
        keep(False, cot_patch, act, cot_rim, rim_act)


def put_side(out, at, coarse, fine):
    channels = out.shape[1]
    row = lax.broadcasted_iota(jnp.int32, (SIDE, channels), 0)
    block = jnp.where(row == 0, coarse.astype(F32), jnp.where(row == 1, fine.astype(F32), 0.0))
    out[at : at + SIDE, :] = block.astype(BF16)


def take_side(ref, at):
    block = ref[at : at + SIDE, :].astype(F32)
    return block[0:1] + block[1:2]


def bit_of(position):
    return lax.rem(lax.shift_right_logical(lax.axis_index("wide"), jnp.int32(position)), 2)


def joined_bias(bias_in, got, size, out, sent, at):
    total = bias_in[0:1, :] + take_side(got, size)
    coarse = total.astype(BF16)
    fine = (total - coarse.astype(F32)).astype(BF16)
    out[...] = jnp.broadcast_to(coarse.astype(F32) + fine.astype(F32), out.shape)
    if sent is not None:
        put_side(sent, at, coarse, fine)


def split(position, held, got, base, size, keep, send):
    half = size // 2
    bit = bit_of(position)
    near = pl.ds(pl.multiple_of(base + bit * half, 16), half)
    away = pl.ds(pl.multiple_of(base + (1 - bit) * half, 16), half)
    send[0:half, :] = (held[away, :] + got[away, :].astype(F32)).astype(BF16)
    keep[...] = held[near, :] + got[near, :].astype(F32)


def halve_body(position, held, got, *rest):
    size = held.shape[0]
    if len(rest) == 4:
        bias_in, keep, send, bias_out = rest
        joined_bias(bias_in, got, size, bias_out, send, size // 2)
    else:
        keep, send = rest
    split(position, held, got, 0, size, keep, send)


def whole_body(size, held, got, *rest):
    send = rest[-2] if len(rest) == 3 else rest[-1]
    send[0:size, :] = (held[0:size, :].astype(F32) + got[0:size, :].astype(F32)).astype(BF16)
    if len(rest) == 3:
        bias_in, _, bias_out = rest
        joined_bias(bias_in, got, size, bias_out, send if send.shape[0] > size else None, size)


def place_body(position, held, got, out):
    place(position, held, got, out, 0)


def place(position, held, got, out, base):
    size = held.shape[0]
    bit = bit_of(position)
    out[pl.ds(pl.multiple_of(base + bit * size, 16), size), :] = held[...]
    out[pl.ds(pl.multiple_of(base + (1 - bit) * size, 16), size), :] = got[...]


def final_body(
    positions, held_a, got_a, held_b, got_b, far_held_a, far_got_a, far_held_b, far_got_b, bias_in,
    down, up, bias_out,
):
    channels = held_a.shape[1]
    core = lax.axis_index("narrow")
    bit_a, bit_b = bit_of(positions[0]), bit_of(positions[1])

    def square(ref):
        block = ref[...].astype(F32).reshape(-1, 8, channels)
        return jnp.sum(block * block, axis=0)

    def pair(one, two, three, four):
        return (square(one) + square(two)) + (square(three) + square(four))

    squares = pair(held_a, got_a, held_b, got_b) + pair(
        far_held_a, far_got_a, far_held_b, far_got_b
    )
    bias = bias_in[0:1, :]
    total = jnp.sum(jnp.sum(squares, axis=0, keepdims=True) + bias * bias, axis=1, keepdims=True)
    clip_level = 0.5 * float(18 * channels * channels + channels) ** 0.5
    factor = jnp.minimum(1.0, clip_level / jnp.sqrt(total))
    factor = jnp.broadcast_to(factor, (1, channels))
    bias_out[...] = bias * factor
    spots = (bit_a, 1 - bit_a, 2 + bit_b, 3 - bit_b)
    for at, (near_ref, far_ref) in enumerate(
        ((held_a, far_held_a), (got_a, far_got_a), (held_b, far_held_b), (got_b, far_got_b))
    ):
        near_block = near_ref[...].astype(F32) * factor
        far_block = far_ref[...].astype(F32) * factor

        @pl.when(core == 0)
        def _():
            down[spots[at]] = near_block
            up[spots[at]] = far_block

        @pl.when(core != 0)
        def _():
            up[spots[at]] = near_block
            down[spots[at]] = far_block


def feature_body(grads, rim_grads, right, below, cot, down_weight, out, wide, pairs, near_mat, low_mat, woven):
    tile_rows, tile_cols, channels = cot.shape
    half_rows, half_cols = tile_rows // 2, tile_cols // 2
    wide[0:half_rows, 0:half_cols, :] = grads[...].astype(F32).reshape(
        half_rows, half_cols, channels
    )
    last = lax.broadcasted_iota(jnp.int32, (half_rows, 8, channels), 1) == 0
    own = rim_grads[half_cols:, :].astype(F32).reshape(half_rows, 1, channels)
    wide[0:half_rows, 0:8, :] = jnp.where(last, own, wide[0:half_rows, 0:8, :])
    wide[0, 0:half_cols, :] = rim_grads[0:half_cols, :].astype(F32)
    aside = lax.axis_index("narrow") < lax.axis_size("narrow") - 1
    under = lax.axis_index("wide") < lax.axis_size("wide") - 1
    rim = if_any(aside, right[...].astype(F32)).reshape(half_rows, 1, channels)
    wide[0:half_rows, half_cols:, :] = jnp.where(last, rim, 0.0)
    wide[half_rows, 0:half_cols, :] = if_any(under, below[0:half_cols, :].astype(F32))
    wide[half_rows, half_cols:, :] = if_any(under & aside, below[half_cols:, :].astype(F32))
    pairs[:, :, 0:channels] = wide[:, 0:half_cols, :].astype(BF16)
    pairs[:, :, channels:] = wide[:, 1 : half_cols + 1, :].astype(BF16)
    zero = jnp.zeros((channels, channels), BF16)
    blocks = [(1, 1, None), (1, 2, 0), (2, 1, None), (2, 2, 0)]
    for at, (row_off, here, next_off) in enumerate(blocks):
        rows = slice(at * channels, (at + 1) * channels)
        near_mat[rows, 0:channels] = down_weight[row_off, here]
        near_mat[rows, channels:] = zero if next_off is None else down_weight[row_off, next_off]
    for at, (here, next_off) in enumerate([(1, None), (2, 0)]):
        rows = slice(at * channels, (at + 1) * channels)
        low_mat[rows, 0:channels] = down_weight[0, here]
        low_mat[rows, channels:] = zero if next_off is None else down_weight[0, next_off]
    step = 8
    dims = (((1,), (1,)), ((), ()))
    for start in range(0, half_rows, step):
        count = step * half_cols
        here = pairs[start : start + step].reshape(count, 2 * channels)
        lower = pairs[start + 1 : start + 1 + step].reshape(count, 2 * channels)
        near = lax.dot_general(here, near_mat[...], dims, preferred_element_type=F32)
        far = lax.dot_general(lower, low_mat[...], dims, preferred_element_type=F32)
        shape = (step, half_cols, channels)
        for row_par in range(2):
            for col_par in range(2):
                lanes = slice((2 * row_par + col_par) * channels, (2 * row_par + col_par + 1) * channels)
                value = near[:, lanes]
                if row_par:
                    value = value + far[:, col_par * channels : (col_par + 1) * channels]
                woven[:, row_par, pl.ds(col_par, half_cols, stride=2), :] = value.reshape(shape)
        span = slice(2 * start, 2 * (start + step))
        total = cot[span].astype(F32) + woven[...].reshape(2 * step, tile_cols, channels)
        out[span] = total.astype(BF16)


def turned(value, axis, steps):
    count = lax.axis_size(axis)
    return lax.ppermute(value, axis, [(at, (at + steps) % count) for at in range(count)])


def turned_both(value):
    count, cores = lax.axis_size("wide"), lax.axis_size("narrow")
    pairs = [
        (at * cores + core, (at + 1) % count * cores + (core + 1) % cores)
        for at in range(count)
        for core in range(cores)
    ]
    return lax.ppermute(value, ("wide", "narrow"), pairs)


def traded(value, position):
    count = lax.axis_size("wide")
    return lax.ppermute(value, "wide", [(at, at ^ (1 << position)) for at in range(count)])


def program(features, cotangent, down_weight, down_bias, up_weight):
    tile_rows, tile_cols, channels = features.shape
    half_rows, half_cols = tile_rows // 2, tile_cols // 2
    pixels = half_rows * half_cols
    taps = 9 * channels
    feat_near, cot_near, down_near, up_near, bias_near, rows, cols, corner = call(
        edge_body,
        (
            vm(features.shape, BF16),
            vm(features.shape, BF16),
            vm(down_weight.shape, BF16),
            vm(up_weight.shape, BF16),
            vm((1, channels), F32),
            vm((2, tile_cols, channels), BF16),
            vm((2, tile_rows, channels), BF16),
            vm((2, 8, channels), BF16),
        ),
        scratch=[
            pltpu.VMEM((2, tile_rows, 16, channels), BF16),
            pltpu.VMEM((tile_rows * 16, channels), F32),
            pltpu.SemaphoreType.DMA((9,)),
        ],
        in_specs=[ANY] * 5,
        nbytes=1 << 19,
        far=(0, 1, 2, 3, 4),
        room=8,
    )(features, cotangent, down_weight, up_weight, down_bias.reshape(1, channels))
    from_above = turned(rows, "wide", 1)
    from_corner = turned_both(corner)
    from_left = turned(cols, "narrow", 1)
    patches = vm((half_rows, half_cols, taps), BF16)
    firsts = vm((2, tile_rows, channels), BF16)
    (
        feat_patch, cot_patch, act, grads, raw_other, raw_bias, feat_firsts, cot_firsts, up_mat
    ) = call(
        interior_body,
        (
            patches,
            patches,
            vm((pixels, channels), BF16),
            vm((pixels, channels), BF16),
            vm((taps, channels), F32),
            vm((8, channels), F32),
            firsts,
            firsts,
            vm((channels, taps), BF16),
        ),
        scratch=[
            pltpu.VMEM((half_rows, 2, tile_cols + 8, channels), F32),
            pltpu.VMEM((tile_rows * 16, channels), F32),
        ],
        n_in=5,
        flops=6 * pixels * taps * channels,
        nbytes=6 << 20,
        near=(0, 1, 2, 3, 4),
        room=12,
    )(feat_near, cot_near, down_near, bias_near, up_near)
    from_above, from_corner, from_left, raw_other = lax.optimization_barrier(
        (from_above, from_corner, from_left, raw_other)
    )
    pieces = half_cols + half_rows
    rim_grads, feat_rim, cot_rim, rim_act, rim_masked, other_a, other_b, bias_sum = call(
        rim_body,
        (
            vm((pieces, channels), BF16),
            vm((pieces, taps), BF16),
            vm((pieces, taps), BF16),
            vm((pieces, channels), BF16),
            vm((pieces, channels), BF16),
            vm((taps // 2 + SIDE, channels), BF16),
            vm((taps // 2, channels), BF16),
            vm((8, channels), F32),
        ),
        scratch=[
            pltpu.VMEM((tile_cols + 8, channels), F32),
            pltpu.VMEM((3, tile_rows + 8, channels), F32),
        ],
        n_in=12,
        flops=1 << 26,
        nbytes=3 << 20,
        near=tuple(range(12)),
        room=8,
    )(
        feat_patch, cot_patch, feat_firsts, cot_firsts, from_above, from_left, from_corner,
        raw_other, raw_bias, up_mat, down_near, bias_near,
    )
    got_a = turned(other_a, "narrow", 1)
    got_b = turned(other_b, "narrow", 1)
    mine_a, mine_b = call(
        mine_body,
        (vm((taps // 2, channels), F32), vm((taps // 2, channels), F32)),
        n_in=8,
        flops=2 * pixels * taps * channels,
        nbytes=3 << 20,
        near=tuple(range(8)),
        room=12,
    )(feat_patch, cot_patch, act, grads, feat_rim, cot_rim, rim_act, rim_masked)
    from_right = turned(rim_grads[half_cols:], "narrow", -1)
    got_a, mine_a, mine_b = lax.optimization_barrier((got_a, mine_a, mine_b))
    low = jnp.concatenate([rim_grads[:half_cols], from_right[:8]], axis=0)
    from_below = turned(low, "wide", -1)

    bits = lax.axis_size("wide").bit_length() - 1
    order_a = [1, 0, *range(2, bits)] if bits > 1 else list(range(bits))
    order_b = [0, 2, 1, *range(3, bits)] if bits > 2 else list(range(bits))
    halvings = 1 if bits <= 3 else 2
    half = taps // 2
    held_a, held_b = mine_a, mine_b
    for step in range(halvings):
        half //= 2
        held_a, send_a, bias_sum = call(
            functools.partial(halve_body, order_a[step]),
            (vm((half, channels), F32), vm((half + SIDE, channels), BF16), vm((8, channels), F32)),
            n_in=3,
            nbytes=half * channels * 12,
            near=(0, 1, 2),
        )(held_a, got_a, bias_sum)
        held_b, send_b = call(
            functools.partial(halve_body, order_b[step]),
            (vm((half, channels), F32), vm((half, channels), BF16)),
            n_in=2,
            nbytes=half * channels * 12,
            near=(0, 1),
        )(held_b, got_b)
        got_a = traded(send_a, order_a[step])
        got_b = traded(send_b, order_b[step])
    feature_grad = call(
        feature_body,
        sds((tile_rows, tile_cols, channels), BF16),
        scratch=[
            pltpu.VMEM((half_rows + 1, half_cols + 8, channels), F32),
            pltpu.VMEM((half_rows + 1, half_cols, 2 * channels), BF16),
            pltpu.VMEM((4 * channels, 2 * channels), BF16),
            pltpu.VMEM((2 * channels, 2 * channels), BF16),
            pltpu.VMEM((8, 2, tile_cols, channels), F32),
        ],
        n_in=6,
        flops=2 * pixels * 6 * 2 * channels * channels,
        nbytes=3 << 20,
        near=(0, 1, 2, 3, 4, 5),
        room=16,
    )(grads, rim_grads, from_right, from_below, cot_near, down_near)
    for step in range(halvings, bits + 1):
        side = SIDE if step < bits else 0
        held_a, bias_sum = call(
            functools.partial(whole_body, half),
            (vm((half + side, channels), BF16), vm((8, channels), F32)),
            n_in=3,
            nbytes=half * channels * 8,
            near=(0, 1, 2),
        )(held_a, got_a, bias_sum)
        held_b = call(
            functools.partial(whole_body, half),
            vm((half, channels), BF16),
            n_in=2,
            nbytes=half * channels * 8,
            near=(0, 1),
        )(held_b, got_b)
        if step < bits:
            got_a = traded(held_a, order_a[step])
            got_b = traded(held_b, order_b[step])
            if step == bits - 1:
                got_b, feature_grad = lax.optimization_barrier((got_b, feature_grad))
    for step in reversed(range(halvings)):
        got_a = traded(held_a, order_a[step])
        got_b = traded(held_b, order_b[step])
        if step:
            half *= 2
            held_a = call(
                functools.partial(place_body, order_a[step]),
                vm((half, channels), BF16),
                n_in=2,
                near=(0, 1),
            )(held_a, got_a)
            held_b = call(
                functools.partial(place_body, order_b[step]),
                vm((half, channels), BF16),
                n_in=2,
                near=(0, 1),
            )(held_b, got_b)
    blocks = (held_a, got_a, held_b, got_b)
    far_blocks = []
    for block in blocks:
        far_blocks.append(turned(block, "narrow", 1))
    size = taps // 4
    down, up, bias_grad = call(
        functools.partial(final_body, (order_a[0], order_b[0])),
        (
            sds((4, size, channels), F32),
            sds((4, size, channels), F32),
            sds((1, channels), F32),
        ),
        n_in=9,
        nbytes=12 * taps * channels,
        near=tuple(range(9)),
        room=8,
    )(*blocks, *far_blocks, bias_sum)
    shape = (3, 3, channels, channels)
    return (feature_grad, down.reshape(shape), up.reshape(shape), bias_grad.reshape(channels))


def solution(mesh):
    return jax.shard_map(
        program,
        mesh=mesh,
        in_specs=(
            P(("groups", "wide"), "narrow", None),
            P(("groups", "wide"), "narrow", None),
            P(),
            P(),
            P(),
        ),
        out_specs=(
            P(("groups", "wide"), "narrow", None),
            P("groups", None, None, None),
            P("groups", None, None, None),
            P("groups"),
        ),
        check_vma=False,
    )
```

```python
import functools

import jax
import jax.numpy as jnp
from jax import lax
from jax.experimental import pallas as pl
from jax.experimental.pallas import tpu as pltpu
from jax.sharding import PartitionSpec as P


F32 = jnp.float32
BF16 = jnp.bfloat16
VM = pl.BlockSpec(memory_space=pltpu.VMEM)
ANY = pl.BlockSpec(memory_space=pl.ANY)
SIDE = 16


def call(body, out_shape, scratch=(), in_specs=None, n_in=0, flops=0, nbytes=0, near=(), far=(), room=4, out_specs=None):
    kernel = pl.pallas_call(
        body,
        out_shape=out_shape,
        in_specs=in_specs if in_specs is not None else [VM] * n_in,
        out_specs=out_specs or jax.tree.map(lambda _: VM, out_shape),
        scratch_shapes=list(scratch),
        compiler_params=pltpu.CompilerParams(vmem_limit_bytes=room << 20),
        cost_estimate=pl.CostEstimate(flops=flops, transcendentals=0, bytes_accessed=nbytes),
    )

    def run(*args):
        placed = [
            pltpu.with_memory_space_constraint(arg, pltpu.VMEM if at in near else pltpu.HBM)
            if at in near or at in far
            else arg
            for at, arg in enumerate(args)
        ]
        return kernel(*placed)

    return run


def vm(shape, dtype):
    return pltpu.VMEM(shape, dtype)


def sds(shape, dtype):
    return jax.ShapeDtypeStruct(shape, dtype)


def edge_body(
    feat, cot, down, up, bias, feat_near, cot_near, down_near, up_near, bias_near,
    rows, cols, wide_strip, sems,
):
    tile_rows, tile_cols, _ = feat.shape
    bulk = [
        pltpu.make_async_copy(feat, feat_near, sems.at[0]),
        pltpu.make_async_copy(cot, cot_near, sems.at[1]),
        pltpu.make_async_copy(down, down_near, sems.at[2]),
        pltpu.make_async_copy(up, up_near, sems.at[3]),
        pltpu.make_async_copy(bias, bias_near, sems.at[4]),
    ]
    for copy in bulk:
        copy.start()
    for which, near in enumerate((feat_near, cot_near)):
        bulk[which].wait()
        rows[which] = near[tile_rows - 1]
        wide_strip[...] = near[:, tile_cols - 16 :, :].astype(F32).reshape(wide_strip.shape)
        cols[which] = wide_strip[pl.ds(15, tile_rows, stride=16), :].astype(BF16)
    for copy in bulk[2:]:
        copy.wait()


def if_any(there, value):
    return jnp.where(there, value, jnp.zeros_like(value))


def own_patches(tile, wide, strip, patch, firsts):
    rows, cols, channels = tile.shape
    half_rows, half_cols = rows // 2, cols // 2
    wide[:, :, 0:8, :] = jnp.zeros((half_rows, 2, 8, channels), F32)
    wide[:, :, 8:, :] = tile[...].astype(F32).reshape(half_rows, 2, cols, channels)
    for col_off in range(3):
        lanes = [pl.ds((3 * row_off + col_off) * channels, channels) for row_off in range(3)]
        taken = pl.ds(7 + col_off, half_cols, stride=2)
        patch[:, :, lanes[1]] = wide[:, 0, taken, :].astype(BF16)
        odd = wide[:, 1, taken, :].astype(BF16)
        patch[:, :, lanes[2]] = odd
        patch[1:, :, lanes[0]] = odd[:-1]
        patch[0, :, lanes[0]] = jnp.zeros((half_cols, channels), BF16)
    strip[...] = tile[:, 0:16, :].astype(F32).reshape(strip.shape)
    for col in range(2):
        firsts[col] = strip[pl.ds(col, rows, stride=16), :].astype(BF16)


def pointwise(pre, act_grad):
    sigm = 1.0 / (1.0 + jnp.exp(-pre))
    return pre * sigm, act_grad * sigm * (1.0 + pre * (1.0 - sigm))


def taps_of(core_is, patch, values):
    if core_is:
        return lax.dot_general(
            patch, values, (((0,), (0,)), ((), ())), preferred_element_type=F32
        )
    channels = values.shape[1]
    rows = lax.dot_general(values, patch, (((0,), (0,)), ((), ())), preferred_element_type=F32)
    return jnp.concatenate(
        [rows[:, tap * channels : (tap + 1) * channels] for tap in range(9)], axis=0
    )


def interior_body(
    feat, cot, down_weight, down_bias, up_weight,
    feat_patch, cot_patch, act, grads, raw_other, raw_bias, feat_firsts, cot_firsts, up_mat,
    wide, strip,
):
    rows, cols, channels = feat.shape
    half_rows, half_cols = rows // 2, cols // 2
    pixels = half_rows * half_cols
    taps = 9 * channels
    own_patches(feat, wide, strip, feat_patch, feat_firsts)
    own_patches(cot, wide, strip, cot_patch, cot_firsts)
    for tap in range(9):
        up_mat[:, pl.ds(tap * channels, channels)] = up_weight[tap // 3, tap % 3]
    down_mat = down_weight[...].reshape(taps, channels)
    bias_row = down_bias[...].reshape(1, channels)
    step = 8
    count = step * half_cols
    total = jnp.zeros((1, channels), F32)
    at = lax.broadcasted_iota(jnp.int32, (count, channels), 0)
    for start in range(0, half_rows, step):
        span = pl.ds(start * half_cols, count)
        feat_rows = feat_patch[start : start + step].reshape(count, taps)
        cot_rows = cot_patch[start : start + step].reshape(count, taps)
        pre = jnp.dot(feat_rows, down_mat, preferred_element_type=F32) + bias_row
        act_grad = lax.dot_general(
            cot_rows, up_mat[...], (((1,), (1,)), ((), ())), preferred_element_type=F32
        )
        inside = lax.rem(at, half_cols) > 0
        if start == 0:
            inside = inside & (at >= half_cols)
        value, grad = pointwise(pre, act_grad)
        act[span, :] = if_any(inside, value).astype(BF16)
        grad = if_any(inside, grad).astype(BF16)
        grads[span, :] = grad
        total = total + jnp.sum(grad.astype(F32), axis=0, keepdims=True)
    raw_bias[...] = jnp.broadcast_to(total, raw_bias.shape)
    core = lax.axis_index("narrow")

    @pl.when(core == 0)
    def _():
        raw_other[...] = taps_of(False, cot_patch[...].reshape(pixels, taps), act[...])

    @pl.when(core != 0)
    def _():
        raw_other[...] = taps_of(True, feat_patch[...].reshape(pixels, taps), grads[...])


def rim_patches(patch, firsts, top, left, out, line, column):
    half_rows, half_cols, taps = patch.shape
    channels = taps // 9
    above = lax.axis_index("wide") > 0
    aside = lax.axis_index("narrow") > 0
    line[0:8, :] = jnp.zeros((8, channels), F32)
    line[8:, :] = if_any(above, top[...].astype(F32))
    column[0, 0:8, :] = line[0:8, :]
    column[0, 8:, :] = if_any(aside, left[...].astype(F32))
    for col in range(2):
        column[1 + col, 0:8, :] = jnp.zeros((8, channels), F32)
        column[1 + col, 8:, :] = firsts[col].astype(F32)
    out[0:half_cols, 3 * channels :] = patch[0, :, 3 * channels :]
    first = lax.broadcasted_iota(jnp.int32, (half_cols, channels), 0) == 0
    for off in range(3):
        out[0:half_cols, off * channels : (off + 1) * channels] = line[
            pl.ds(7 + off, half_cols, stride=2), :
        ].astype(BF16)
        for col_off in range(3):
            lanes = slice((3 * off + col_off) * channels, (3 * off + col_off + 1) * channels)
            out[half_cols:, lanes] = column[
                col_off, pl.ds(7 + off, half_rows, stride=2), :
            ].astype(BF16)
    for off in (1, 2):
        lanes = slice(3 * off * channels, (3 * off + 1) * channels)
        rest = patch[0, :, lanes].astype(F32)
        halo = jnp.broadcast_to(column[0, 7 + off : 8 + off, :], rest.shape)
        out[0:half_cols, lanes] = jnp.where(first, halo, rest).astype(BF16)


def rim_body(
    feat_patch, cot_patch, feat_firsts, cot_firsts, top, left, raw_other, raw_bias,
    up_mat, down_weight, down_bias,
    rim_grads, feat_rim, cot_rim, rim_act, rim_masked, other_a, other_b, bias_part,
    line, column,
):
    _, half_cols, taps = feat_patch.shape
    channels = taps // 9
    half = taps // 2
    rim_patches(
        feat_patch, feat_firsts, top.at[0], left.at[0], feat_rim, line, column
    )
    rim_patches(cot_patch, cot_firsts, top.at[1], left.at[1], cot_rim, line, column)
    pre = jnp.dot(
        feat_rim[...], down_weight[...].reshape(taps, channels), preferred_element_type=F32
    ) + down_bias[...].reshape(1, channels)
    act_grad = lax.dot_general(
        cot_rim[...], up_mat[...], (((1,), (1,)), ((), ())), preferred_element_type=F32
    )
    value, grad = pointwise(pre, act_grad)
    at = lax.broadcasted_iota(jnp.int32, value.shape, 0)
    once = at != half_cols
    core = lax.axis_index("narrow")
    counted = once & ((at > 0) | (core == 0))
    act = if_any(counted, value).astype(BF16)
    masked = if_any(counted, grad).astype(BF16)
    rim_act[...] = act
    rim_masked[...] = masked
    full = grad.astype(BF16).astype(F32)
    rim_grads[...] = jnp.where(once, full, jnp.broadcast_to(full[0:1], full.shape)).astype(BF16)
    total = raw_bias[0:1, :] + jnp.sum(masked.astype(F32), axis=0, keepdims=True)
    coarse = total.astype(BF16)
    fine = (total - coarse.astype(F32)).astype(BF16)
    bias_part[...] = jnp.broadcast_to(coarse.astype(F32) + fine.astype(F32), bias_part.shape)
    put_side(other_a, half, coarse, fine)
    put_pixel(other_a, half + SIDE, top, feat_rim, cot_rim)

    def give(more):
        other_a[0:half, :] = (raw_other[0:half, :] + more[0:half]).astype(BF16)
        other_b[...] = (raw_other[half:, :] + more[half:]).astype(BF16)

    @pl.when(core == 0)
    def _():
        give(taps_of(False, cot_rim[...], act))

    @pl.when(core != 0)
    def _():
        give(taps_of(True, feat_rim[...], masked))


def put_pixel(out, at, top, feat_rim, cot_rim):
    _, cols, channels = top.shape
    core = lax.axis_index("narrow")
    above = lax.axis_index("wide") > 0
    row = lax.broadcasted_iota(jnp.int32, (2 * SIDE, channels), 0)
    block = jnp.zeros((2 * SIDE, channels), F32)
    for which, rim in enumerate((feat_rim, cot_rim)):
        corner = top[which, cols - 16 :, :].astype(F32)[15:16]
        corner = if_any(above & (core == 0), corner)
        block = jnp.where(row == which * SIDE, corner, block)
        for tap in range(1, 9):
            value = rim[0:16, tap * channels : (tap + 1) * channels].astype(F32)[0:1]
            value = if_any(core > 0, value)
            block = jnp.where(row == which * SIDE + tap, value, block)
    out[at : at + 2 * SIDE, :] = block.astype(BF16)


def late_body(
    own, got, mine_a, mine_b, rim_grads, down_weight, down_bias, up_mat,
    out_a, out_b, grads_out, late, feat_row, cot_row,
):
    half, channels = mine_a.shape
    taps = 2 * half
    core = lax.axis_index("narrow")
    span = slice(half + SIDE, half + 3 * SIDE)
    pixel = own[span, :].astype(F32) + got[span, :].astype(F32)
    first = lax.broadcasted_iota(jnp.int32, (SIDE, channels), 0) == 0
    for which, row in enumerate((feat_row, cot_row)):
        for tap in range(9):
            at = which * SIDE + tap
            row[:, tap * channels : (tap + 1) * channels] = if_any(
                first, jnp.broadcast_to(pixel[at : at + 1], (SIDE, channels))
            ).astype(BF16)
    pre = jnp.dot(
        feat_row[...], down_weight[...].reshape(taps, channels), preferred_element_type=F32
    ) + down_bias[...].reshape(1, channels)
    act_grad = lax.dot_general(
        cot_row[...], up_mat[...], (((1,), (1,)), ((), ())), preferred_element_type=F32
    )
    value, grad = pointwise(pre, act_grad)
    act = if_any(first, value).astype(BF16)
    grad = if_any(first, grad).astype(BF16)
    only = grad.astype(F32)[0:1]
    late[...] = jnp.broadcast_to(only, late.shape)
    half_cols = rim_grads.shape[0] // 2
    row = lax.broadcasted_iota(jnp.int32, rim_grads.shape, 0)
    ours = ((row == 0) | (row == half_cols)) & (core > 0)
    grads_out[...] = jnp.where(
        ours, jnp.broadcast_to(only, rim_grads.shape), rim_grads[...].astype(F32)
    ).astype(BF16)

    def add(more):
        out_a[...] = mine_a[...] + more[0:half]
        out_b[...] = mine_b[...] + more[half:]

    @pl.when(core == 0)
    def _():
        add(taps_of(True, feat_row[...], grad))

    @pl.when(core != 0)
    def _():
        add(taps_of(False, cot_row[...], act))


def mine_body(
    feat_patch, cot_patch, act, grads, feat_rim, cot_rim, rim_act, rim_masked, mine_a, mine_b
):
    half_rows, half_cols, taps = feat_patch.shape
    pixels = half_rows * half_cols
    half = taps // 2
    core = lax.axis_index("narrow")

    def keep(which, patch, values, rim_patch, rim_values):
        total = taps_of(which, patch[...].reshape(pixels, taps), values[...])
        total = total + taps_of(which, rim_patch[...], rim_values[...])
        mine_a[...] = total[0:half]
        mine_b[...] = total[half:]

    @pl.when(core == 0)
    def _():
        keep(True, feat_patch, grads, feat_rim, rim_masked)

    @pl.when(core != 0)
    def _():
        keep(False, cot_patch, act, cot_rim, rim_act)


def put_side(out, at, coarse, fine):
    channels = out.shape[1]
    row = lax.broadcasted_iota(jnp.int32, (SIDE, channels), 0)
    block = jnp.where(row == 0, coarse.astype(F32), jnp.where(row == 1, fine.astype(F32), 0.0))
    out[at : at + SIDE, :] = block.astype(BF16)


def take_side(ref, at):
    block = ref[at : at + SIDE, :].astype(F32)
    return block[0:1] + block[1:2]


def bit_of(position):
    return lax.rem(lax.shift_right_logical(lax.axis_index("wide"), jnp.int32(position)), 2)


def joined_bias(bias_in, got, size, out, sent, at, late=None):
    total = bias_in[0:1, :] + take_side(got, size)
    if late is not None:
        total = total + late[0:1, :]
    coarse = total.astype(BF16)
    fine = (total - coarse.astype(F32)).astype(BF16)
    out[...] = jnp.broadcast_to(coarse.astype(F32) + fine.astype(F32), out.shape)
    if sent is not None:
        put_side(sent, at, coarse, fine)


def split(position, held, got, base, size, keep, send):
    half = size // 2
    bit = bit_of(position)
    near = pl.ds(pl.multiple_of(base + bit * half, 16), half)
    away = pl.ds(pl.multiple_of(base + (1 - bit) * half, 16), half)
    send[0:half, :] = (held[away, :] + got[away, :].astype(F32)).astype(BF16)
    keep[...] = held[near, :] + got[near, :].astype(F32)


def halve_body(position, held, got, *rest):
    size = held.shape[0]
    if len(rest) > 3:
        bias_in, *late, keep, send, bias_out = rest
        joined_bias(bias_in, got, size, bias_out, send, size // 2, *late)
    else:
        keep, send = rest
    split(position, held, got, 0, size, keep, send)


def whole_body(size, held, got, *rest):
    send = rest[-2] if len(rest) == 3 else rest[-1]
    send[0:size, :] = (held[0:size, :].astype(F32) + got[0:size, :].astype(F32)).astype(BF16)
    if len(rest) == 3:
        bias_in, _, bias_out = rest
        joined_bias(bias_in, got, size, bias_out, send if send.shape[0] > size else None, size)


def place_body(position, held, got, out):
    place(position, held, got, out, 0)


def place(position, held, got, out, base):
    size = held.shape[0]
    bit = bit_of(position)
    out[pl.ds(pl.multiple_of(base + bit * size, 16), size), :] = held[...]
    out[pl.ds(pl.multiple_of(base + (1 - bit) * size, 16), size), :] = got[...]


def final_body(
    positions, held_a, got_a, held_b, got_b, far_held_a, far_got_a, far_held_b, far_got_b, bias_in,
    down, up, bias_out,
):
    channels = held_a.shape[1]
    core = lax.axis_index("narrow")
    bit_a, bit_b = bit_of(positions[0]), bit_of(positions[1])

    def square(ref):
        block = ref[...].astype(F32).reshape(-1, 8, channels)
        return jnp.sum(block * block, axis=0)

    def pair(one, two, three, four):
        return (square(one) + square(two)) + (square(three) + square(four))

    squares = pair(held_a, got_a, held_b, got_b) + pair(
        far_held_a, far_got_a, far_held_b, far_got_b
    )
    bias = bias_in[0:1, :]
    total = jnp.sum(jnp.sum(squares, axis=0, keepdims=True) + bias * bias, axis=1, keepdims=True)
    clip_level = 0.5 * float(18 * channels * channels + channels) ** 0.5
    factor = jnp.minimum(1.0, clip_level / jnp.sqrt(total))
    factor = jnp.broadcast_to(factor, (1, channels))
    bias_out[...] = bias * factor
    spots = (bit_a, 1 - bit_a, 2 + bit_b, 3 - bit_b)
    for at, (near_ref, far_ref) in enumerate(
        ((held_a, far_held_a), (got_a, far_got_a), (held_b, far_held_b), (got_b, far_got_b))
    ):
        near_block = near_ref[...].astype(F32) * factor
        far_block = far_ref[...].astype(F32) * factor

        @pl.when(core == 0)
        def _():
            down[spots[at]] = near_block
            up[spots[at]] = far_block

        @pl.when(core != 0)
        def _():
            up[spots[at]] = near_block
            down[spots[at]] = far_block


def feature_body(grads, rim_grads, right, below, cot, down_weight, out, wide, pairs, near_mat, low_mat, woven):
    tile_rows, tile_cols, channels = cot.shape
    half_rows, half_cols = tile_rows // 2, tile_cols // 2
    wide[0:half_rows, 0:half_cols, :] = grads[...].astype(F32).reshape(
        half_rows, half_cols, channels
    )
    last = lax.broadcasted_iota(jnp.int32, (half_rows, 8, channels), 1) == 0
    own = rim_grads[half_cols:, :].astype(F32).reshape(half_rows, 1, channels)
    wide[0:half_rows, 0:8, :] = jnp.where(last, own, wide[0:half_rows, 0:8, :])
    wide[0, 0:half_cols, :] = rim_grads[0:half_cols, :].astype(F32)
    aside = lax.axis_index("narrow") < lax.axis_size("narrow") - 1
    under = lax.axis_index("wide") < lax.axis_size("wide") - 1
    rim = if_any(aside, right[...].astype(F32)).reshape(half_rows, 1, channels)
    wide[0:half_rows, half_cols:, :] = jnp.where(last, rim, 0.0)
    wide[half_rows, 0:half_cols, :] = if_any(under, below[0:half_cols, :].astype(F32))
    wide[half_rows, half_cols:, :] = if_any(under & aside, below[half_cols:, :].astype(F32))
    pairs[:, :, 0:channels] = wide[:, 0:half_cols, :].astype(BF16)
    pairs[:, :, channels:] = wide[:, 1 : half_cols + 1, :].astype(BF16)
    zero = jnp.zeros((channels, channels), BF16)
    blocks = [(1, 1, None), (1, 2, 0), (2, 1, None), (2, 2, 0)]
    for at, (row_off, here, next_off) in enumerate(blocks):
        rows = slice(at * channels, (at + 1) * channels)
        near_mat[rows, 0:channels] = down_weight[row_off, here]
        near_mat[rows, channels:] = zero if next_off is None else down_weight[row_off, next_off]
    for at, (here, next_off) in enumerate([(1, None), (2, 0)]):
        rows = slice(at * channels, (at + 1) * channels)
        low_mat[rows, 0:channels] = down_weight[0, here]
        low_mat[rows, channels:] = zero if next_off is None else down_weight[0, next_off]
    step = 8
    dims = (((1,), (1,)), ((), ()))
    for start in range(0, half_rows, step):
        count = step * half_cols
        here = pairs[start : start + step].reshape(count, 2 * channels)
        lower = pairs[start + 1 : start + 1 + step].reshape(count, 2 * channels)
        near = lax.dot_general(here, near_mat[...], dims, preferred_element_type=F32)
        far = lax.dot_general(lower, low_mat[...], dims, preferred_element_type=F32)
        shape = (step, half_cols, channels)
        for row_par in range(2):
            for col_par in range(2):
                lanes = slice((2 * row_par + col_par) * channels, (2 * row_par + col_par + 1) * channels)
                value = near[:, lanes]
                if row_par:
                    value = value + far[:, col_par * channels : (col_par + 1) * channels]
                woven[:, row_par, pl.ds(col_par, half_cols, stride=2), :] = value.reshape(shape)
        span = slice(2 * start, 2 * (start + step))
        total = cot[span].astype(F32) + woven[...].reshape(2 * step, tile_cols, channels)
        out[span] = total.astype(BF16)


def turned(value, axis, steps):
    count = lax.axis_size(axis)
    return lax.ppermute(value, axis, [(at, (at + steps) % count) for at in range(count)])


def traded(value, position):
    count = lax.axis_size("wide")
    return lax.ppermute(value, "wide", [(at, at ^ (1 << position)) for at in range(count)])


def program(features, cotangent, down_weight, down_bias, up_weight):
    tile_rows, tile_cols, channels = features.shape
    half_rows, half_cols = tile_rows // 2, tile_cols // 2
    pixels = half_rows * half_cols
    taps = 9 * channels
    feat_near, cot_near, down_near, up_near, bias_near, rows, cols = call(
        edge_body,
        (
            vm(features.shape, BF16),
            vm(features.shape, BF16),
            vm(down_weight.shape, BF16),
            vm(up_weight.shape, BF16),
            vm((1, channels), F32),
            vm((2, tile_cols, channels), BF16),
            vm((2, tile_rows, channels), BF16),
        ),
        scratch=[
            pltpu.VMEM((tile_rows * 16, channels), F32),
            pltpu.SemaphoreType.DMA((5,)),
        ],
        in_specs=[ANY] * 5,
        nbytes=1 << 19,
        far=(0, 1, 2, 3, 4),
        room=8,
    )(features, cotangent, down_weight, up_weight, down_bias.reshape(1, channels))
    from_above = turned(rows, "wide", 1)
    from_left = turned(cols, "narrow", 1)
    patches = vm((half_rows, half_cols, taps), BF16)
    firsts = vm((2, tile_rows, channels), BF16)
    (
        feat_patch, cot_patch, act, grads, raw_other, raw_bias, feat_firsts, cot_firsts, up_mat
    ) = call(
        interior_body,
        (
            patches,
            patches,
            vm((pixels, channels), BF16),
            vm((pixels, channels), BF16),
            vm((taps, channels), F32),
            vm((8, channels), F32),
            firsts,
            firsts,
            vm((channels, taps), BF16),
        ),
        scratch=[
            pltpu.VMEM((half_rows, 2, tile_cols + 8, channels), F32),
            pltpu.VMEM((tile_rows * 16, channels), F32),
        ],
        n_in=5,
        flops=6 * pixels * taps * channels,
        nbytes=6 << 20,
        near=(0, 1, 2, 3, 4),
        room=12,
    )(feat_near, cot_near, down_near, bias_near, up_near)
    from_above, from_left, raw_other = lax.optimization_barrier(
        (from_above, from_left, raw_other)
    )
    pieces = half_cols + half_rows
    rim_grads, feat_rim, cot_rim, rim_act, rim_masked, other_a, other_b, bias_sum = call(
        rim_body,
        (
            vm((pieces, channels), BF16),
            vm((pieces, taps), BF16),
            vm((pieces, taps), BF16),
            vm((pieces, channels), BF16),
            vm((pieces, channels), BF16),
            vm((taps // 2 + 3 * SIDE, channels), BF16),
            vm((taps // 2, channels), BF16),
            vm((8, channels), F32),
        ),
        scratch=[
            pltpu.VMEM((tile_cols + 8, channels), F32),
            pltpu.VMEM((3, tile_rows + 8, channels), F32),
        ],
        n_in=11,
        flops=1 << 26,
        nbytes=3 << 20,
        near=tuple(range(11)),
        room=8,
    )(
        feat_patch, cot_patch, feat_firsts, cot_firsts, from_above, from_left,
        raw_other, raw_bias, up_mat, down_near, bias_near,
    )
    got_a = turned(other_a, "narrow", 1)
    got_b = turned(other_b, "narrow", 1)
    mine_a, mine_b = call(
        mine_body,
        (vm((taps // 2, channels), F32), vm((taps // 2, channels), F32)),
        n_in=8,
        flops=2 * pixels * taps * channels,
        nbytes=3 << 20,
        near=tuple(range(8)),
        room=12,
    )(feat_patch, cot_patch, act, grads, feat_rim, cot_rim, rim_act, rim_masked)
    got_a, mine_a, mine_b = lax.optimization_barrier((got_a, mine_a, mine_b))
    mine_a, mine_b, rim_grads, late = call(
        late_body,
        (
            vm((taps // 2, channels), F32),
            vm((taps // 2, channels), F32),
            vm((pieces, channels), BF16),
            vm((8, channels), F32),
        ),
        scratch=[pltpu.VMEM((SIDE, taps), BF16), pltpu.VMEM((SIDE, taps), BF16)],
        n_in=8,
        flops=1 << 24,
        nbytes=1 << 20,
        near=tuple(range(8)),
        room=8,
    )(other_a, got_a, mine_a, mine_b, rim_grads, down_near, bias_near, up_mat)
    from_right = turned(rim_grads[half_cols:], "narrow", -1)
    low = jnp.concatenate([rim_grads[:half_cols], from_right[:8]], axis=0)
    from_below = turned(low, "wide", -1)

    bits = lax.axis_size("wide").bit_length() - 1
    order_a = [1, 0, *range(2, bits)] if bits > 1 else list(range(bits))
    order_b = [0, 2, 1, *range(3, bits)] if bits > 2 else list(range(bits))
    halvings = 1 if bits <= 3 else 2
    half = taps // 2
    held_a, held_b = mine_a, mine_b
    for step in range(halvings):
        half //= 2
        held_a, send_a, bias_sum = call(
            functools.partial(halve_body, order_a[step]),
            (vm((half, channels), F32), vm((half + SIDE, channels), BF16), vm((8, channels), F32)),
            n_in=3 if step else 4,
            nbytes=half * channels * 12,
            near=(0, 1, 2) if step else (0, 1, 2, 3),
        )(held_a, got_a, bias_sum, *(() if step else (late,)))
        held_b, send_b = call(
            functools.partial(halve_body, order_b[step]),
            (vm((half, channels), F32), vm((half, channels), BF16)),
            n_in=2,
            nbytes=half * channels * 12,
            near=(0, 1),
        )(held_b, got_b)
        got_a = traded(send_a, order_a[step])
        got_b = traded(send_b, order_b[step])
    feature_grad = call(
        feature_body,
        sds((tile_rows, tile_cols, channels), BF16),
        scratch=[
            pltpu.VMEM((half_rows + 1, half_cols + 8, channels), F32),
            pltpu.VMEM((half_rows + 1, half_cols, 2 * channels), BF16),
            pltpu.VMEM((4 * channels, 2 * channels), BF16),
            pltpu.VMEM((2 * channels, 2 * channels), BF16),
            pltpu.VMEM((8, 2, tile_cols, channels), F32),
        ],
        n_in=6,
        flops=2 * pixels * 6 * 2 * channels * channels,
        nbytes=3 << 20,
        near=(0, 1, 2, 3, 4, 5),
        room=16,
    )(grads, rim_grads, from_right, from_below, cot_near, down_near)
    for step in range(halvings, bits + 1):
        side = SIDE if step < bits else 0
        held_a, bias_sum = call(
            functools.partial(whole_body, half),
            (vm((half + side, channels), BF16), vm((8, channels), F32)),
            n_in=3,
            nbytes=half * channels * 8,
            near=(0, 1, 2),
        )(held_a, got_a, bias_sum)
        held_b = call(
            functools.partial(whole_body, half),
            vm((half, channels), BF16),
            n_in=2,
            nbytes=half * channels * 8,
            near=(0, 1),
        )(held_b, got_b)
        if step < bits:
            got_a = traded(held_a, order_a[step])
            got_b = traded(held_b, order_b[step])
            if step == bits - 1:
                got_b, feature_grad = lax.optimization_barrier((got_b, feature_grad))
    for step in reversed(range(halvings)):
        got_a = traded(held_a, order_a[step])
        got_b = traded(held_b, order_b[step])
        if step:
            half *= 2
            held_a = call(
                functools.partial(place_body, order_a[step]),
                vm((half, channels), BF16),
                n_in=2,
                near=(0, 1),
            )(held_a, got_a)
            held_b = call(
                functools.partial(place_body, order_b[step]),
                vm((half, channels), BF16),
                n_in=2,
                near=(0, 1),
            )(held_b, got_b)
    blocks = (held_a, got_a, held_b, got_b)
    far_blocks = []
    for block in blocks:
        far_blocks.append(turned(block, "narrow", 1))
    size = taps // 4
    down, up, bias_grad = call(
        functools.partial(final_body, (order_a[0], order_b[0])),
        (
            sds((4, size, channels), F32),
            sds((4, size, channels), F32),
            sds((1, channels), F32),
        ),
        n_in=9,
        nbytes=12 * taps * channels,
        near=tuple(range(9)),
        room=8,
    )(*blocks, *far_blocks, bias_sum)
    shape = (3, 3, channels, channels)
    return (feature_grad, down.reshape(shape), up.reshape(shape), bias_grad.reshape(channels))


def solution(mesh):
    return jax.shard_map(
        program,
        mesh=mesh,
        in_specs=(
            P(("groups", "wide"), "narrow", None),
            P(("groups", "wide"), "narrow", None),
            P(),
            P(),
            P(),
        ),
        out_specs=(
            P(("groups", "wide"), "narrow", None),
            P("groups", None, None, None),
            P("groups", None, None, None),
            P("groups"),
        ),
        check_vma=False,
    )
```

```python
import functools

import jax
import jax.numpy as jnp
from jax import lax
from jax.experimental import pallas as pl
from jax.experimental.pallas import tpu as pltpu
from jax.sharding import PartitionSpec as P


F32 = jnp.float32
BF16 = jnp.bfloat16
VM = pl.BlockSpec(memory_space=pltpu.VMEM)
ANY = pl.BlockSpec(memory_space=pl.ANY)
SIDE = 16


def call(body, out_shape, scratch=(), in_specs=None, n_in=0, flops=0, nbytes=0, near=(), far=(), room=4, out_specs=None):
    kernel = pl.pallas_call(
        body,
        out_shape=out_shape,
        in_specs=in_specs if in_specs is not None else [VM] * n_in,
        out_specs=out_specs or jax.tree.map(lambda _: VM, out_shape),
        scratch_shapes=list(scratch),
        compiler_params=pltpu.CompilerParams(vmem_limit_bytes=room << 20),
        cost_estimate=pl.CostEstimate(flops=flops, transcendentals=0, bytes_accessed=nbytes),
    )

    def run(*args):
        placed = [
            pltpu.with_memory_space_constraint(arg, pltpu.VMEM if at in near else pltpu.HBM)
            if at in near or at in far
            else arg
            for at, arg in enumerate(args)
        ]
        return kernel(*placed)

    return run


def vm(shape, dtype):
    return pltpu.VMEM(shape, dtype)


def sds(shape, dtype):
    return jax.ShapeDtypeStruct(shape, dtype)


def edge_body(
    feat, cot, down, up, bias, feat_near, cot_near, down_near, up_near, bias_near,
    rows, cols, wide_strip, sems,
):
    tile_rows, tile_cols, _ = feat.shape
    bulk = [
        pltpu.make_async_copy(feat, feat_near, sems.at[0]),
        pltpu.make_async_copy(cot, cot_near, sems.at[1]),
        pltpu.make_async_copy(down, down_near, sems.at[2]),
        pltpu.make_async_copy(up, up_near, sems.at[3]),
        pltpu.make_async_copy(bias, bias_near, sems.at[4]),
    ]
    for copy in bulk:
        copy.start()
    for which, near in enumerate((feat_near, cot_near)):
        bulk[which].wait()
        rows[which] = near[tile_rows - 1]
        wide_strip[...] = near[:, tile_cols - 16 :, :].astype(F32).reshape(wide_strip.shape)
        cols[which] = wide_strip[pl.ds(15, tile_rows, stride=16), :].astype(BF16)
    for copy in bulk[2:]:
        copy.wait()


def if_any(there, value):
    return jnp.where(there, value, jnp.zeros_like(value))


def own_patches(tile, wide, strip, patch, firsts):
    rows, cols, channels = tile.shape
    half_rows, half_cols = rows // 2, cols // 2
    wide[:, :, 0:8, :] = jnp.zeros((half_rows, 2, 8, channels), F32)
    wide[:, :, 8:, :] = tile[...].astype(F32).reshape(half_rows, 2, cols, channels)
    for col_off in range(3):
        lanes = [pl.ds((3 * row_off + col_off) * channels, channels) for row_off in range(3)]
        taken = pl.ds(7 + col_off, half_cols, stride=2)
        patch[:, :, lanes[1]] = wide[:, 0, taken, :].astype(BF16)
        odd = wide[:, 1, taken, :].astype(BF16)
        patch[:, :, lanes[2]] = odd
        patch[1:, :, lanes[0]] = odd[:-1]
        patch[0, :, lanes[0]] = jnp.zeros((half_cols, channels), BF16)
    strip[...] = tile[:, 0:16, :].astype(F32).reshape(strip.shape)
    for col in range(2):
        firsts[col] = strip[pl.ds(col, rows, stride=16), :].astype(BF16)


def pointwise(pre, act_grad):
    sigm = 1.0 / (1.0 + jnp.exp(-pre))
    return pre * sigm, act_grad * sigm * (1.0 + pre * (1.0 - sigm))


def taps_of(core_is, patch, values):
    if core_is:
        return lax.dot_general(
            patch, values, (((0,), (0,)), ((), ())), preferred_element_type=F32
        )
    channels = values.shape[1]
    rows = lax.dot_general(values, patch, (((0,), (0,)), ((), ())), preferred_element_type=F32)
    return jnp.concatenate(
        [rows[:, tap * channels : (tap + 1) * channels] for tap in range(9)], axis=0
    )


def interior_body(
    feat, cot, down_weight, down_bias, up_weight,
    feat_patch, cot_patch, act, grads, raw_other, raw_bias, feat_firsts, cot_firsts, up_mat,
    wide, strip,
):
    rows, cols, channels = feat.shape
    half_rows, half_cols = rows // 2, cols // 2
    pixels = half_rows * half_cols
    taps = 9 * channels
    own_patches(feat, wide, strip, feat_patch, feat_firsts)
    own_patches(cot, wide, strip, cot_patch, cot_firsts)
    for tap in range(9):
        up_mat[:, pl.ds(tap * channels, channels)] = up_weight[tap // 3, tap % 3]
    down_mat = down_weight[...].reshape(taps, channels)
    bias_row = down_bias[...].reshape(1, channels)
    step = 8
    count = step * half_cols
    total = jnp.zeros((1, channels), F32)
    at = lax.broadcasted_iota(jnp.int32, (count, channels), 0)
    for start in range(0, half_rows, step):
        span = pl.ds(start * half_cols, count)
        feat_rows = feat_patch[start : start + step].reshape(count, taps)
        cot_rows = cot_patch[start : start + step].reshape(count, taps)
        pre = jnp.dot(feat_rows, down_mat, preferred_element_type=F32) + bias_row
        act_grad = lax.dot_general(
            cot_rows, up_mat[...], (((1,), (1,)), ((), ())), preferred_element_type=F32
        )
        inside = lax.rem(at, half_cols) > 0
        if start == 0:
            inside = inside & (at >= half_cols)
        value, grad = pointwise(pre, act_grad)
        act[span, :] = if_any(inside, value).astype(BF16)
        grad = if_any(inside, grad).astype(BF16)
        grads[span, :] = grad
        total = total + jnp.sum(grad.astype(F32), axis=0, keepdims=True)
    raw_bias[...] = jnp.broadcast_to(total, raw_bias.shape)
    core = lax.axis_index("narrow")

    @pl.when(core == 0)
    def _():
        raw_other[...] = taps_of(False, cot_patch[...].reshape(pixels, taps), act[...])

    @pl.when(core != 0)
    def _():
        raw_other[...] = taps_of(True, feat_patch[...].reshape(pixels, taps), grads[...])


def rim_patches(patch, firsts, top, left, out, line, column):
    half_rows, half_cols, taps = patch.shape
    channels = taps // 9
    above = lax.axis_index("wide") > 0
    aside = lax.axis_index("narrow") > 0
    line[0:8, :] = jnp.zeros((8, channels), F32)
    line[8:, :] = if_any(above, top[...].astype(F32))
    column[0, 0:8, :] = line[0:8, :]
    column[0, 8:, :] = if_any(aside, left[...].astype(F32))
    for col in range(2):
        column[1 + col, 0:8, :] = jnp.zeros((8, channels), F32)
        column[1 + col, 8:, :] = firsts[col].astype(F32)
    out[0:half_cols, 3 * channels :] = patch[0, :, 3 * channels :]
    first = lax.broadcasted_iota(jnp.int32, (half_cols, channels), 0) == 0
    for off in range(3):
        out[0:half_cols, off * channels : (off + 1) * channels] = line[
            pl.ds(7 + off, half_cols, stride=2), :
        ].astype(BF16)
        for col_off in range(3):
            lanes = slice((3 * off + col_off) * channels, (3 * off + col_off + 1) * channels)
            out[half_cols:, lanes] = column[
                col_off, pl.ds(7 + off, half_rows, stride=2), :
            ].astype(BF16)
    for off in (1, 2):
        lanes = slice(3 * off * channels, (3 * off + 1) * channels)
        rest = patch[0, :, lanes].astype(F32)
        halo = jnp.broadcast_to(column[0, 7 + off : 8 + off, :], rest.shape)
        out[0:half_cols, lanes] = jnp.where(first, halo, rest).astype(BF16)


def rim_body(
    feat_patch, cot_patch, feat_firsts, cot_firsts, top, left, raw_other, raw_bias,
    up_mat, down_weight, down_bias,
    rim_grads, feat_rim, cot_rim, rim_act, rim_masked, other_a, other_b, bias_part,
    line, column,
):
    _, half_cols, taps = feat_patch.shape
    channels = taps // 9
    half = taps // 2
    rim_patches(
        feat_patch, feat_firsts, top.at[0], left.at[0], feat_rim, line, column
    )
    rim_patches(cot_patch, cot_firsts, top.at[1], left.at[1], cot_rim, line, column)
    pre = jnp.dot(
        feat_rim[...], down_weight[...].reshape(taps, channels), preferred_element_type=F32
    ) + down_bias[...].reshape(1, channels)
    act_grad = lax.dot_general(
        cot_rim[...], up_mat[...], (((1,), (1,)), ((), ())), preferred_element_type=F32
    )
    value, grad = pointwise(pre, act_grad)
    at = lax.broadcasted_iota(jnp.int32, value.shape, 0)
    once = at != half_cols
    core = lax.axis_index("narrow")
    counted = once & ((at > 0) | (core == 0))
    act = if_any(counted, value).astype(BF16)
    masked = if_any(counted, grad).astype(BF16)
    rim_act[...] = act
    rim_masked[...] = masked
    full = grad.astype(BF16).astype(F32)
    rim_grads[...] = jnp.where(once, full, jnp.broadcast_to(full[0:1], full.shape)).astype(BF16)
    total = raw_bias[0:1, :] + jnp.sum(masked.astype(F32), axis=0, keepdims=True)
    coarse = total.astype(BF16)
    fine = (total - coarse.astype(F32)).astype(BF16)
    bias_part[...] = jnp.broadcast_to(coarse.astype(F32) + fine.astype(F32), bias_part.shape)
    put_side(other_a, half, coarse, fine)
    put_pixel(other_a, half + SIDE, top, feat_rim, cot_rim)

    def give(more):
        other_a[0:half, :] = (raw_other[0:half, :] + more[0:half]).astype(BF16)
        other_b[...] = (raw_other[half:, :] + more[half:]).astype(BF16)

    @pl.when(core == 0)
    def _():
        give(taps_of(False, cot_rim[...], act))

    @pl.when(core != 0)
    def _():
        give(taps_of(True, feat_rim[...], masked))


def put_pixel(out, at, top, feat_rim, cot_rim):
    _, cols, channels = top.shape
    core = lax.axis_index("narrow")
    above = lax.axis_index("wide") > 0
    row = lax.broadcasted_iota(jnp.int32, (2 * SIDE, channels), 0)
    block = jnp.zeros((2 * SIDE, channels), F32)
    for which, rim in enumerate((feat_rim, cot_rim)):
        corner = top[which, cols - 16 :, :].astype(F32)[15:16]
        corner = if_any(above & (core == 0), corner)
        block = jnp.where(row == which * SIDE, corner, block)
        for tap in range(1, 9):
            value = rim[0:16, tap * channels : (tap + 1) * channels].astype(F32)[0:1]
            value = if_any(core > 0, value)
            block = jnp.where(row == which * SIDE + tap, value, block)
    out[at : at + 2 * SIDE, :] = block.astype(BF16)


def late_body(
    own, got, mine_a, mine_b, rim_grads, down_weight, down_bias, up_mat,
    out_a, out_b, grads_out, late, feat_row, cot_row,
):
    half, channels = mine_a.shape
    taps = 2 * half
    core = lax.axis_index("narrow")
    span = slice(half + SIDE, half + 3 * SIDE)
    pixel = own[span, :].astype(F32) + got[span, :].astype(F32)
    first = lax.broadcasted_iota(jnp.int32, (SIDE, channels), 0) == 0
    for which, row in enumerate((feat_row, cot_row)):
        for tap in range(9):
            at = which * SIDE + tap
            row[:, tap * channels : (tap + 1) * channels] = if_any(
                first, jnp.broadcast_to(pixel[at : at + 1], (SIDE, channels))
            ).astype(BF16)
    pre = jnp.dot(
        feat_row[...], down_weight[...].reshape(taps, channels), preferred_element_type=F32
    ) + down_bias[...].reshape(1, channels)
    act_grad = lax.dot_general(
        cot_row[...], up_mat[...], (((1,), (1,)), ((), ())), preferred_element_type=F32
    )
    value, grad = pointwise(pre, act_grad)
    act = if_any(first, value).astype(BF16)
    grad = if_any(first, grad).astype(BF16)
    only = grad.astype(F32)[0:1]
    late[...] = jnp.broadcast_to(only, late.shape)
    half_cols = rim_grads.shape[0] // 2
    row = lax.broadcasted_iota(jnp.int32, rim_grads.shape, 0)
    ours = ((row == 0) | (row == half_cols)) & (core > 0)
    grads_out[...] = jnp.where(
        ours, jnp.broadcast_to(only, rim_grads.shape), rim_grads[...].astype(F32)
    ).astype(BF16)

    def add(more):
        out_a[...] = mine_a[...] + more[0:half]
        out_b[...] = mine_b[...] + more[half:]

    @pl.when(core == 0)
    def _():
        add(taps_of(True, feat_row[...], grad))

    @pl.when(core != 0)
    def _():
        add(taps_of(False, cot_row[...], act))


def mine_body(
    feat_patch, cot_patch, act, grads, feat_rim, cot_rim, rim_act, rim_masked, mine_a, mine_b
):
    half_rows, half_cols, taps = feat_patch.shape
    pixels = half_rows * half_cols
    half = taps // 2
    core = lax.axis_index("narrow")

    def keep(which, patch, values, rim_patch, rim_values):
        total = taps_of(which, patch[...].reshape(pixels, taps), values[...])
        total = total + taps_of(which, rim_patch[...], rim_values[...])
        mine_a[...] = total[0:half]
        mine_b[...] = total[half:]

    @pl.when(core == 0)
    def _():
        keep(True, feat_patch, grads, feat_rim, rim_masked)

    @pl.when(core != 0)
    def _():
        keep(False, cot_patch, act, cot_rim, rim_act)


def put_side(out, at, coarse, fine):
    channels = out.shape[1]
    row = lax.broadcasted_iota(jnp.int32, (SIDE, channels), 0)
    block = jnp.where(row == 0, coarse.astype(F32), jnp.where(row == 1, fine.astype(F32), 0.0))
    out[at : at + SIDE, :] = block.astype(BF16)


def take_side(ref, at):
    block = ref[at : at + SIDE, :].astype(F32)
    return block[0:1] + block[1:2]


def bit_of(position):
    return lax.rem(lax.shift_right_logical(lax.axis_index("wide"), jnp.int32(position)), 2)


def joined_bias(bias_in, got, size, out, sent, at, late=None):
    total = bias_in[0:1, :] + take_side(got, size)
    if late is not None:
        total = total + late[0:1, :]
    coarse = total.astype(BF16)
    fine = (total - coarse.astype(F32)).astype(BF16)
    out[...] = jnp.broadcast_to(coarse.astype(F32) + fine.astype(F32), out.shape)
    if sent is not None:
        put_side(sent, at, coarse, fine)


def split(position, held, got, base, size, keep, send):
    half = size // 2
    bit = bit_of(position)
    near = pl.ds(pl.multiple_of(base + bit * half, 16), half)
    away = pl.ds(pl.multiple_of(base + (1 - bit) * half, 16), half)
    send[0:half, :] = (held[away, :] + got[away, :].astype(F32)).astype(BF16)
    keep[...] = held[near, :] + got[near, :].astype(F32)


def halve_body(position, held, got, *rest):
    size = held.shape[0]
    if len(rest) > 3:
        bias_in, *late, keep, send, bias_out = rest
        joined_bias(bias_in, got, size, bias_out, send, size // 2, *late)
    else:
        keep, send = rest
    split(position, held, got, 0, size, keep, send)


def whole_body(size, held, got, *rest):
    send = rest[-2] if len(rest) == 3 else rest[-1]
    send[0:size, :] = (held[0:size, :].astype(F32) + got[0:size, :].astype(F32)).astype(BF16)
    if len(rest) == 3:
        bias_in, _, bias_out = rest
        joined_bias(bias_in, got, size, bias_out, send if send.shape[0] > size else None, size)


def place_body(position, held, got, out):
    place(position, held, got, out, 0)


def place(position, held, got, out, base):
    size = held.shape[0]
    bit = bit_of(position)
    out[pl.ds(pl.multiple_of(base + bit * size, 16), size), :] = held[...]
    out[pl.ds(pl.multiple_of(base + (1 - bit) * size, 16), size), :] = got[...]


def final_body(
    positions, held_a, got_a, held_b, got_b, far_held_a, far_got_a, far_held_b, far_got_b, bias_in,
    down, up, bias_out,
):
    channels = held_a.shape[1]
    core = lax.axis_index("narrow")
    bit_a, bit_b = bit_of(positions[0]), bit_of(positions[1])

    def square(ref):
        total = jnp.zeros((32, channels), F32)
        for at in range(0, ref.shape[0], 32):
            block = ref[at : at + 32, :].astype(F32)
            total = total + block * block
        return total

    def pair(one, two, three, four):
        return (square(one) + square(two)) + (square(three) + square(four))

    squares = pair(held_a, got_a, held_b, got_b) + pair(
        far_held_a, far_got_a, far_held_b, far_got_b
    )
    bias = bias_in[0:1, :]
    total = jnp.sum(jnp.sum(squares, axis=0, keepdims=True) + bias * bias, axis=1, keepdims=True)
    clip_level = 0.5 * float(18 * channels * channels + channels) ** 0.5
    factor = jnp.minimum(1.0, clip_level / jnp.sqrt(total))
    factor = jnp.broadcast_to(factor, (1, channels))
    bias_out[...] = bias * factor
    spots = (bit_a, 1 - bit_a, 2 + bit_b, 3 - bit_b)

    def write(near_out, far_out):
        near = (held_a, got_a, held_b, got_b)
        far = (far_held_a, far_got_a, far_held_b, far_got_b)
        for out, refs in ((near_out, near), (far_out, far)):
            for spot, ref in zip(spots, refs):
                for at in range(0, ref.shape[0], 32):
                    out[spot, at : at + 32, :] = ref[at : at + 32, :].astype(F32) * factor

    @pl.when(core == 0)
    def _():
        write(down, up)

    @pl.when(core != 0)
    def _():
        write(up, down)


def feature_body(grads, rim_grads, right, below, cot, down_weight, out, wide, pairs, near_mat, low_mat, woven):
    tile_rows, tile_cols, channels = cot.shape
    half_rows, half_cols = tile_rows // 2, tile_cols // 2
    wide[0:half_rows, 0:half_cols, :] = grads[...].astype(F32).reshape(
        half_rows, half_cols, channels
    )
    last = lax.broadcasted_iota(jnp.int32, (half_rows, 8, channels), 1) == 0
    own = rim_grads[half_cols:, :].astype(F32).reshape(half_rows, 1, channels)
    wide[0:half_rows, 0:8, :] = jnp.where(last, own, wide[0:half_rows, 0:8, :])
    wide[0, 0:half_cols, :] = rim_grads[0:half_cols, :].astype(F32)
    aside = lax.axis_index("narrow") < lax.axis_size("narrow") - 1
    under = lax.axis_index("wide") < lax.axis_size("wide") - 1
    rim = if_any(aside, right[...].astype(F32)).reshape(half_rows, 1, channels)
    wide[0:half_rows, half_cols:, :] = jnp.where(last, rim, 0.0)
    wide[half_rows, 0:half_cols, :] = if_any(under, below[0:half_cols, :].astype(F32))
    wide[half_rows, half_cols:, :] = if_any(under & aside, below[half_cols:, :].astype(F32))
    pairs[:, :, 0:channels] = wide[:, 0:half_cols, :].astype(BF16)
    pairs[:, :, channels:] = wide[:, 1 : half_cols + 1, :].astype(BF16)
    zero = jnp.zeros((channels, channels), BF16)
    blocks = [(1, 1, None), (1, 2, 0), (2, 1, None), (2, 2, 0)]
    for at, (row_off, here, next_off) in enumerate(blocks):
        rows = slice(at * channels, (at + 1) * channels)
        near_mat[rows, 0:channels] = down_weight[row_off, here]
        near_mat[rows, channels:] = zero if next_off is None else down_weight[row_off, next_off]
    for at, (here, next_off) in enumerate([(1, None), (2, 0)]):
        rows = slice(at * channels, (at + 1) * channels)
        low_mat[rows, 0:channels] = down_weight[0, here]
        low_mat[rows, channels:] = zero if next_off is None else down_weight[0, next_off]
    step = 8
    dims = (((1,), (1,)), ((), ()))
    for start in range(0, half_rows, step):
        count = step * half_cols
        here = pairs[start : start + step].reshape(count, 2 * channels)
        lower = pairs[start + 1 : start + 1 + step].reshape(count, 2 * channels)
        near = lax.dot_general(here, near_mat[...], dims, preferred_element_type=F32)
        far = lax.dot_general(lower, low_mat[...], dims, preferred_element_type=F32)
        shape = (step, half_cols, channels)
        for row_par in range(2):
            for col_par in range(2):
                lanes = slice((2 * row_par + col_par) * channels, (2 * row_par + col_par + 1) * channels)
                value = near[:, lanes]
                if row_par:
                    value = value + far[:, col_par * channels : (col_par + 1) * channels]
                woven[:, row_par, pl.ds(col_par, half_cols, stride=2), :] = value.reshape(shape)
        span = slice(2 * start, 2 * (start + step))
        total = cot[span].astype(F32) + woven[...].reshape(2 * step, tile_cols, channels)
        out[span] = total.astype(BF16)


def turned(value, axis, steps):
    count = lax.axis_size(axis)
    return lax.ppermute(value, axis, [(at, (at + steps) % count) for at in range(count)])


def traded(value, position):
    count = lax.axis_size("wide")
    return lax.ppermute(value, "wide", [(at, at ^ (1 << position)) for at in range(count)])


def program(features, cotangent, down_weight, down_bias, up_weight):
    tile_rows, tile_cols, channels = features.shape
    half_rows, half_cols = tile_rows // 2, tile_cols // 2
    pixels = half_rows * half_cols
    taps = 9 * channels
    feat_near, cot_near, down_near, up_near, bias_near, rows, cols = call(
        edge_body,
        (
            vm(features.shape, BF16),
            vm(features.shape, BF16),
            vm(down_weight.shape, BF16),
            vm(up_weight.shape, BF16),
            vm((1, channels), F32),
            vm((2, tile_cols, channels), BF16),
            vm((2, tile_rows, channels), BF16),
        ),
        scratch=[
            pltpu.VMEM((tile_rows * 16, channels), F32),
            pltpu.SemaphoreType.DMA((5,)),
        ],
        in_specs=[ANY] * 5,
        nbytes=1 << 19,
        far=(0, 1, 2, 3, 4),
        room=8,
    )(features, cotangent, down_weight, up_weight, down_bias.reshape(1, channels))
    from_above = turned(rows, "wide", 1)
    from_left = turned(cols, "narrow", 1)
    patches = vm((half_rows, half_cols, taps), BF16)
    firsts = vm((2, tile_rows, channels), BF16)
    (
        feat_patch, cot_patch, act, grads, raw_other, raw_bias, feat_firsts, cot_firsts, up_mat
    ) = call(
        interior_body,
        (
            patches,
            patches,
            vm((pixels, channels), BF16),
            vm((pixels, channels), BF16),
            vm((taps, channels), F32),
            vm((8, channels), F32),
            firsts,
            firsts,
            vm((channels, taps), BF16),
        ),
        scratch=[
            pltpu.VMEM((half_rows, 2, tile_cols + 8, channels), F32),
            pltpu.VMEM((tile_rows * 16, channels), F32),
        ],
        n_in=5,
        flops=6 * pixels * taps * channels,
        nbytes=6 << 20,
        near=(0, 1, 2, 3, 4),
        room=12,
    )(feat_near, cot_near, down_near, bias_near, up_near)
    from_above, from_left, raw_other = lax.optimization_barrier(
        (from_above, from_left, raw_other)
    )
    pieces = half_cols + half_rows
    rim_grads, feat_rim, cot_rim, rim_act, rim_masked, other_a, other_b, bias_sum = call(
        rim_body,
        (
            vm((pieces, channels), BF16),
            vm((pieces, taps), BF16),
            vm((pieces, taps), BF16),
            vm((pieces, channels), BF16),
            vm((pieces, channels), BF16),
            vm((taps // 2 + 3 * SIDE, channels), BF16),
            vm((taps // 2, channels), BF16),
            vm((8, channels), F32),
        ),
        scratch=[
            pltpu.VMEM((tile_cols + 8, channels), F32),
            pltpu.VMEM((3, tile_rows + 8, channels), F32),
        ],
        n_in=11,
        flops=1 << 26,
        nbytes=3 << 20,
        near=tuple(range(11)),
        room=8,
    )(
        feat_patch, cot_patch, feat_firsts, cot_firsts, from_above, from_left,
        raw_other, raw_bias, up_mat, down_near, bias_near,
    )
    got_a = turned(other_a, "narrow", 1)
    got_b = turned(other_b, "narrow", 1)
    mine_a, mine_b = call(
        mine_body,
        (vm((taps // 2, channels), F32), vm((taps // 2, channels), F32)),
        n_in=8,
        flops=2 * pixels * taps * channels,
        nbytes=3 << 20,
        near=tuple(range(8)),
        room=12,
    )(feat_patch, cot_patch, act, grads, feat_rim, cot_rim, rim_act, rim_masked)
    got_a, mine_a, mine_b = lax.optimization_barrier((got_a, mine_a, mine_b))
    mine_a, mine_b, rim_grads, late = call(
        late_body,
        (
            vm((taps // 2, channels), F32),
            vm((taps // 2, channels), F32),
            vm((pieces, channels), BF16),
            vm((8, channels), F32),
        ),
        scratch=[pltpu.VMEM((SIDE, taps), BF16), pltpu.VMEM((SIDE, taps), BF16)],
        n_in=8,
        flops=1 << 24,
        nbytes=1 << 20,
        near=tuple(range(8)),
        room=8,
    )(other_a, got_a, mine_a, mine_b, rim_grads, down_near, bias_near, up_mat)
    from_right = turned(rim_grads[half_cols:], "narrow", -1)
    low = jnp.concatenate([rim_grads[:half_cols], from_right[:8]], axis=0)
    from_below = turned(low, "wide", -1)

    bits = lax.axis_size("wide").bit_length() - 1
    order_a = [1, 0, *range(2, bits)] if bits > 1 else list(range(bits))
    order_b = [0, 2, 1, *range(3, bits)] if bits > 2 else list(range(bits))
    halvings = 1 if bits <= 3 else 2
    half = taps // 2
    held_a, held_b = mine_a, mine_b
    for step in range(halvings):
        half //= 2
        held_a, send_a, bias_sum = call(
            functools.partial(halve_body, order_a[step]),
            (vm((half, channels), F32), vm((half + SIDE, channels), BF16), vm((8, channels), F32)),
            n_in=3 if step else 4,
            nbytes=half * channels * 12,
            near=(0, 1, 2) if step else (0, 1, 2, 3),
        )(held_a, got_a, bias_sum, *(() if step else (late,)))
        held_b, send_b = call(
            functools.partial(halve_body, order_b[step]),
            (vm((half, channels), F32), vm((half, channels), BF16)),
            n_in=2,
            nbytes=half * channels * 12,
            near=(0, 1),
        )(held_b, got_b)
        got_a = traded(send_a, order_a[step])
        got_b = traded(send_b, order_b[step])
    feature_grad = call(
        feature_body,
        sds((tile_rows, tile_cols, channels), BF16),
        scratch=[
            pltpu.VMEM((half_rows + 1, half_cols + 8, channels), F32),
            pltpu.VMEM((half_rows + 1, half_cols, 2 * channels), BF16),
            pltpu.VMEM((4 * channels, 2 * channels), BF16),
            pltpu.VMEM((2 * channels, 2 * channels), BF16),
            pltpu.VMEM((8, 2, tile_cols, channels), F32),
        ],
        n_in=6,
        flops=2 * pixels * 6 * 2 * channels * channels,
        nbytes=3 << 20,
        near=(0, 1, 2, 3, 4, 5),
        room=16,
    )(grads, rim_grads, from_right, from_below, cot_near, down_near)
    for step in range(halvings, bits + 1):
        side = SIDE if step < bits else 0
        held_a, bias_sum = call(
            functools.partial(whole_body, half),
            (vm((half + side, channels), BF16), vm((8, channels), F32)),
            n_in=3,
            nbytes=half * channels * 8,
            near=(0, 1, 2),
        )(held_a, got_a, bias_sum)
        held_b = call(
            functools.partial(whole_body, half),
            vm((half, channels), BF16),
            n_in=2,
            nbytes=half * channels * 8,
            near=(0, 1),
        )(held_b, got_b)
        if step < bits:
            got_a = traded(held_a, order_a[step])
            got_b = traded(held_b, order_b[step])
            if step == bits - 1:
                got_b, feature_grad = lax.optimization_barrier((got_b, feature_grad))
    for step in reversed(range(halvings)):
        got_a = traded(held_a, order_a[step])
        got_b = traded(held_b, order_b[step])
        if step:
            half *= 2
            held_a = call(
                functools.partial(place_body, order_a[step]),
                vm((half, channels), BF16),
                n_in=2,
                near=(0, 1),
            )(held_a, got_a)
            held_b = call(
                functools.partial(place_body, order_b[step]),
                vm((half, channels), BF16),
                n_in=2,
                near=(0, 1),
            )(held_b, got_b)
    blocks = (held_a, got_a, held_b, got_b)
    far_blocks = []
    for block in blocks:
        far_blocks.append(turned(block, "narrow", 1))
    size = taps // 4
    down, up, bias_grad = call(
        functools.partial(final_body, (order_a[0], order_b[0])),
        (
            sds((4, size, channels), F32),
            sds((4, size, channels), F32),
            sds((1, channels), F32),
        ),
        n_in=9,
        nbytes=12 * taps * channels,
        near=tuple(range(9)),
        room=8,
    )(*blocks, *far_blocks, bias_sum)
    shape = (3, 3, channels, channels)
    return (feature_grad, down.reshape(shape), up.reshape(shape), bias_grad.reshape(channels))


def solution(mesh):
    return jax.shard_map(
        program,
        mesh=mesh,
        in_specs=(
            P(("groups", "wide"), "narrow", None),
            P(("groups", "wide"), "narrow", None),
            P(),
            P(),
            P(),
        ),
        out_specs=(
            P(("groups", "wide"), "narrow", None),
            P("groups", None, None, None),
            P("groups", None, None, None),
            P("groups"),
        ),
        check_vma=False,
    )
```

```python
import functools

import jax
import jax.numpy as jnp
from jax import lax
from jax.experimental import pallas as pl
from jax.experimental.pallas import tpu as pltpu
from jax.sharding import PartitionSpec as P


F32 = jnp.float32
BF16 = jnp.bfloat16
VM = pl.BlockSpec(memory_space=pltpu.VMEM)
ANY = pl.BlockSpec(memory_space=pl.ANY)
SIDE = 16


def call(body, out_shape, scratch=(), in_specs=None, n_in=0, flops=0, nbytes=0, near=(), far=(), room=4, out_specs=None):
    kernel = pl.pallas_call(
        body,
        out_shape=out_shape,
        in_specs=in_specs if in_specs is not None else [VM] * n_in,
        out_specs=out_specs or jax.tree.map(lambda _: VM, out_shape),
        scratch_shapes=list(scratch),
        compiler_params=pltpu.CompilerParams(vmem_limit_bytes=room << 20),
        cost_estimate=pl.CostEstimate(flops=flops, transcendentals=0, bytes_accessed=nbytes),
    )

    def run(*args):
        placed = [
            pltpu.with_memory_space_constraint(arg, pltpu.VMEM if at in near else pltpu.HBM)
            if at in near or at in far
            else arg
            for at, arg in enumerate(args)
        ]
        return kernel(*placed)

    return run


def vm(shape, dtype):
    return pltpu.VMEM(shape, dtype)


def sds(shape, dtype):
    return jax.ShapeDtypeStruct(shape, dtype)


def edge_body(
    feat, cot, down, up, bias, feat_near, cot_near, down_near, up_near, bias_near,
    rows, cols, wide_strip, sems,
):
    tile_rows, tile_cols, _ = feat.shape
    bulk = [
        pltpu.make_async_copy(feat, feat_near, sems.at[0]),
        pltpu.make_async_copy(cot, cot_near, sems.at[1]),
        pltpu.make_async_copy(down, down_near, sems.at[2]),
        pltpu.make_async_copy(up, up_near, sems.at[3]),
        pltpu.make_async_copy(bias, bias_near, sems.at[4]),
    ]
    for copy in bulk:
        copy.start()
    for which, near in enumerate((feat_near, cot_near)):
        bulk[which].wait()
        rows[which] = near[tile_rows - 1]
        wide_strip[...] = near[:, tile_cols - 16 :, :].astype(F32).reshape(wide_strip.shape)
        cols[which] = wide_strip[pl.ds(15, tile_rows, stride=16), :].astype(BF16)
    for copy in bulk[2:]:
        copy.wait()


def if_any(there, value):
    return jnp.where(there, value, jnp.zeros_like(value))


def own_patches(tile, wide, strip, patch, firsts):
    rows, cols, channels = tile.shape
    half_rows, half_cols = rows // 2, cols // 2
    wide[:, :, 0:8, :] = jnp.zeros((half_rows, 2, 8, channels), F32)
    wide[:, :, 8:, :] = tile[...].astype(F32).reshape(half_rows, 2, cols, channels)
    for col_off in range(3):
        lanes = [pl.ds((3 * row_off + col_off) * channels, channels) for row_off in range(3)]
        taken = pl.ds(7 + col_off, half_cols, stride=2)
        patch[:, :, lanes[1]] = wide[:, 0, taken, :].astype(BF16)
        odd = wide[:, 1, taken, :].astype(BF16)
        patch[:, :, lanes[2]] = odd
        patch[1:, :, lanes[0]] = odd[:-1]
        patch[0, :, lanes[0]] = jnp.zeros((half_cols, channels), BF16)
    strip[...] = tile[:, 0:16, :].astype(F32).reshape(strip.shape)
    for col in range(2):
        firsts[col] = strip[pl.ds(col, rows, stride=16), :].astype(BF16)


def pointwise(pre, act_grad):
    sigm = 1.0 / (1.0 + jnp.exp(-pre))
    return pre * sigm, act_grad * sigm * (1.0 + pre * (1.0 - sigm))


def taps_of(core_is, patch, values):
    if core_is:
        return lax.dot_general(
            patch, values, (((0,), (0,)), ((), ())), preferred_element_type=F32
        )
    channels = values.shape[1]
    rows = lax.dot_general(values, patch, (((0,), (0,)), ((), ())), preferred_element_type=F32)
    return jnp.concatenate(
        [rows[:, tap * channels : (tap + 1) * channels] for tap in range(9)], axis=0
    )


def interior_body(
    feat, cot, down_weight, down_bias, up_weight,
    feat_patch, cot_patch, act, grads, raw_other, raw_bias, feat_firsts, cot_firsts, up_mat,
    wide, strip,
):
    rows, cols, channels = feat.shape
    half_rows, half_cols = rows // 2, cols // 2
    pixels = half_rows * half_cols
    taps = 9 * channels
    own_patches(feat, wide, strip, feat_patch, feat_firsts)
    own_patches(cot, wide, strip, cot_patch, cot_firsts)
    for tap in range(9):
        up_mat[:, pl.ds(tap * channels, channels)] = up_weight[tap // 3, tap % 3]
    down_mat = down_weight[...].reshape(taps, channels)
    bias_row = down_bias[...].reshape(1, channels)
    step = 8
    count = step * half_cols
    total = jnp.zeros((1, channels), F32)
    at = lax.broadcasted_iota(jnp.int32, (count, channels), 0)
    for start in range(0, half_rows, step):
        span = pl.ds(start * half_cols, count)
        feat_rows = feat_patch[start : start + step].reshape(count, taps)
        cot_rows = cot_patch[start : start + step].reshape(count, taps)
        pre = jnp.dot(feat_rows, down_mat, preferred_element_type=F32) + bias_row
        act_grad = lax.dot_general(
            cot_rows, up_mat[...], (((1,), (1,)), ((), ())), preferred_element_type=F32
        )
        inside = lax.rem(at, half_cols) > 0
        if start == 0:
            inside = inside & (at >= half_cols)
        value, grad = pointwise(pre, act_grad)
        act[span, :] = if_any(inside, value).astype(BF16)
        grad = if_any(inside, grad).astype(BF16)
        grads[span, :] = grad
        total = total + jnp.sum(grad.astype(F32), axis=0, keepdims=True)
    raw_bias[...] = jnp.broadcast_to(total, raw_bias.shape)
    core = lax.axis_index("narrow")

    @pl.when(core == 0)
    def _():
        raw_other[...] = taps_of(False, cot_patch[...].reshape(pixels, taps), act[...])

    @pl.when(core != 0)
    def _():
        raw_other[...] = taps_of(True, feat_patch[...].reshape(pixels, taps), grads[...])


def rim_patches(patch, firsts, top, left, out, line, column):
    half_rows, half_cols, taps = patch.shape
    channels = taps // 9
    above = lax.axis_index("wide") > 0
    aside = lax.axis_index("narrow") > 0
    line[0:8, :] = jnp.zeros((8, channels), F32)
    line[8:, :] = if_any(above, top[...].astype(F32))
    column[0, 0:8, :] = line[0:8, :]
    column[0, 8:, :] = if_any(aside, left[...].astype(F32))
    for col in range(2):
        column[1 + col, 0:8, :] = jnp.zeros((8, channels), F32)
        column[1 + col, 8:, :] = firsts[col].astype(F32)
    out[0:half_cols, 3 * channels :] = patch[0, :, 3 * channels :]
    first = lax.broadcasted_iota(jnp.int32, (half_cols, channels), 0) == 0
    for off in range(3):
        out[0:half_cols, off * channels : (off + 1) * channels] = line[
            pl.ds(7 + off, half_cols, stride=2), :
        ].astype(BF16)
        for col_off in range(3):
            lanes = slice((3 * off + col_off) * channels, (3 * off + col_off + 1) * channels)
            out[half_cols:, lanes] = column[
                col_off, pl.ds(7 + off, half_rows, stride=2), :
            ].astype(BF16)
    for off in (1, 2):
        lanes = slice(3 * off * channels, (3 * off + 1) * channels)
        rest = patch[0, :, lanes].astype(F32)
        halo = jnp.broadcast_to(column[0, 7 + off : 8 + off, :], rest.shape)
        out[0:half_cols, lanes] = jnp.where(first, halo, rest).astype(BF16)


def rim_body(
    feat_patch, cot_patch, feat_firsts, cot_firsts, top, left, raw_other, raw_bias,
    up_mat, down_weight, down_bias,
    rim_grads, feat_rim, cot_rim, rim_act, rim_masked, other_a, other_b, bias_part,
    line, column,
):
    _, half_cols, taps = feat_patch.shape
    channels = taps // 9
    half = taps // 2
    rim_patches(
        feat_patch, feat_firsts, top.at[0], left.at[0], feat_rim, line, column
    )
    rim_patches(cot_patch, cot_firsts, top.at[1], left.at[1], cot_rim, line, column)
    pre = jnp.dot(
        feat_rim[...], down_weight[...].reshape(taps, channels), preferred_element_type=F32
    ) + down_bias[...].reshape(1, channels)
    act_grad = lax.dot_general(
        cot_rim[...], up_mat[...], (((1,), (1,)), ((), ())), preferred_element_type=F32
    )
    value, grad = pointwise(pre, act_grad)
    at = lax.broadcasted_iota(jnp.int32, value.shape, 0)
    once = at != half_cols
    core = lax.axis_index("narrow")
    counted = once & ((at > 0) | (core == 0))
    act = if_any(counted, value).astype(BF16)
    masked = if_any(counted, grad).astype(BF16)
    rim_act[...] = act
    rim_masked[...] = masked
    full = grad.astype(BF16).astype(F32)
    rim_grads[...] = jnp.where(once, full, jnp.broadcast_to(full[0:1], full.shape)).astype(BF16)
    total = raw_bias[0:1, :] + jnp.sum(masked.astype(F32), axis=0, keepdims=True)
    coarse = total.astype(BF16)
    fine = (total - coarse.astype(F32)).astype(BF16)
    bias_part[...] = jnp.broadcast_to(coarse.astype(F32) + fine.astype(F32), bias_part.shape)
    put_side(other_a, half, coarse, fine)
    put_pixel(other_a, half + SIDE, top, feat_rim, cot_rim)

    def give(more):
        other_a[0:half, :] = (raw_other[0:half, :] + more[0:half]).astype(BF16)
        other_b[...] = (raw_other[half:, :] + more[half:]).astype(BF16)

    @pl.when(core == 0)
    def _():
        give(taps_of(False, cot_rim[...], act))

    @pl.when(core != 0)
    def _():
        give(taps_of(True, feat_rim[...], masked))


def put_pixel(out, at, top, feat_rim, cot_rim):
    _, cols, channels = top.shape
    core = lax.axis_index("narrow")
    above = lax.axis_index("wide") > 0
    row = lax.broadcasted_iota(jnp.int32, (2 * SIDE, channels), 0)
    block = jnp.zeros((2 * SIDE, channels), F32)
    for which, rim in enumerate((feat_rim, cot_rim)):
        corner = top[which, cols - 16 :, :].astype(F32)[15:16]
        corner = if_any(above & (core == 0), corner)
        block = jnp.where(row == which * SIDE, corner, block)
        for tap in range(1, 9):
            value = rim[0:16, tap * channels : (tap + 1) * channels].astype(F32)[0:1]
            value = if_any(core > 0, value)
            block = jnp.where(row == which * SIDE + tap, value, block)
    out[at : at + 2 * SIDE, :] = block.astype(BF16)


def late_body(
    position, own, got, mine_a, mine_b, rim_grads, down_weight, down_bias, up_mat, bias_in,
    keep, send, out_b, grads_out, bias_out, feat_row, cot_row, held,
):
    half, channels = mine_a.shape
    taps = 2 * half
    core = lax.axis_index("narrow")
    span = slice(half + SIDE, half + 3 * SIDE)
    pixel = own[span, :].astype(F32) + got[span, :].astype(F32)
    first = lax.broadcasted_iota(jnp.int32, (SIDE, channels), 0) == 0
    for which, row in enumerate((feat_row, cot_row)):
        for tap in range(9):
            at = which * SIDE + tap
            row[:, tap * channels : (tap + 1) * channels] = if_any(
                first, jnp.broadcast_to(pixel[at : at + 1], (SIDE, channels))
            ).astype(BF16)
    pre = jnp.dot(
        feat_row[...], down_weight[...].reshape(taps, channels), preferred_element_type=F32
    ) + down_bias[...].reshape(1, channels)
    act_grad = lax.dot_general(
        cot_row[...], up_mat[...], (((1,), (1,)), ((), ())), preferred_element_type=F32
    )
    value, grad = pointwise(pre, act_grad)
    act = if_any(first, value).astype(BF16)
    grad = if_any(first, grad).astype(BF16)
    only = grad.astype(F32)[0:1]
    joined_bias(bias_in, got, half, bias_out, send, half // 2, only)
    half_cols = rim_grads.shape[0] // 2
    row = lax.broadcasted_iota(jnp.int32, rim_grads.shape, 0)
    ours = ((row == 0) | (row == half_cols)) & (core > 0)
    grads_out[...] = jnp.where(
        ours, jnp.broadcast_to(only, rim_grads.shape), rim_grads[...].astype(F32)
    ).astype(BF16)

    def add(more):
        held[...] = mine_a[...] + more[0:half]
        out_b[...] = mine_b[...] + more[half:]

    @pl.when(core == 0)
    def _():
        add(taps_of(True, feat_row[...], grad))

    @pl.when(core != 0)
    def _():
        add(taps_of(False, cot_row[...], act))

    split(position, held, got, 0, half, keep, send)


def mine_body(
    feat_patch, cot_patch, act, grads, feat_rim, cot_rim, rim_act, rim_masked, mine_a, mine_b
):
    half_rows, half_cols, taps = feat_patch.shape
    pixels = half_rows * half_cols
    half = taps // 2
    core = lax.axis_index("narrow")

    def keep(which, patch, values, rim_patch, rim_values):
        total = taps_of(which, patch[...].reshape(pixels, taps), values[...])
        total = total + taps_of(which, rim_patch[...], rim_values[...])
        mine_a[...] = total[0:half]
        mine_b[...] = total[half:]

    @pl.when(core == 0)
    def _():
        keep(True, feat_patch, grads, feat_rim, rim_masked)

    @pl.when(core != 0)
    def _():
        keep(False, cot_patch, act, cot_rim, rim_act)


def put_side(out, at, coarse, fine):
    channels = out.shape[1]
    row = lax.broadcasted_iota(jnp.int32, (SIDE, channels), 0)
    block = jnp.where(row == 0, coarse.astype(F32), jnp.where(row == 1, fine.astype(F32), 0.0))
    out[at : at + SIDE, :] = block.astype(BF16)


def take_side(ref, at):
    block = ref[at : at + SIDE, :].astype(F32)
    return block[0:1] + block[1:2]


def bit_of(position):
    return lax.rem(lax.shift_right_logical(lax.axis_index("wide"), jnp.int32(position)), 2)


def joined_bias(bias_in, got, size, out, sent, at, late=None):
    total = bias_in[0:1, :] + take_side(got, size)
    if late is not None:
        total = total + late[0:1, :]
    coarse = total.astype(BF16)
    fine = (total - coarse.astype(F32)).astype(BF16)
    out[...] = jnp.broadcast_to(coarse.astype(F32) + fine.astype(F32), out.shape)
    if sent is not None:
        put_side(sent, at, coarse, fine)


def split(position, held, got, base, size, keep, send):
    half = size // 2
    bit = bit_of(position)
    near = pl.ds(pl.multiple_of(base + bit * half, 16), half)
    away = pl.ds(pl.multiple_of(base + (1 - bit) * half, 16), half)
    send[0:half, :] = (held[away, :] + got[away, :].astype(F32)).astype(BF16)
    keep[...] = held[near, :] + got[near, :].astype(F32)


def halve_body(position, held, got, *rest):
    size = held.shape[0]
    if len(rest) > 3:
        bias_in, keep, send, bias_out = rest
        joined_bias(bias_in, got, size, bias_out, send, size // 2)
    else:
        keep, send = rest
    split(position, held, got, 0, size, keep, send)


def whole_body(size, held, got, *rest):
    send = rest[-2] if len(rest) == 3 else rest[-1]
    send[0:size, :] = (held[0:size, :].astype(F32) + got[0:size, :].astype(F32)).astype(BF16)
    if len(rest) == 3:
        bias_in, _, bias_out = rest
        joined_bias(bias_in, got, size, bias_out, send if send.shape[0] > size else None, size)


def place_body(position, held, got, out):
    place(position, held, got, out, 0)


def place(position, held, got, out, base):
    size = held.shape[0]
    bit = bit_of(position)
    out[pl.ds(pl.multiple_of(base + bit * size, 16), size), :] = held[...]
    out[pl.ds(pl.multiple_of(base + (1 - bit) * size, 16), size), :] = got[...]


def final_body(
    positions, held_a, got_a, held_b, got_b, far_held_a, far_got_a, far_held_b, far_got_b, bias_in,
    down, up, bias_out,
):
    channels = held_a.shape[1]
    core = lax.axis_index("narrow")
    bit_a, bit_b = bit_of(positions[0]), bit_of(positions[1])

    def square(ref):
        total = jnp.zeros((32, channels), F32)
        for at in range(0, ref.shape[0], 32):
            block = ref[at : at + 32, :].astype(F32)
            total = total + block * block
        return total

    def pair(one, two, three, four):
        return (square(one) + square(two)) + (square(three) + square(four))

    squares = pair(held_a, got_a, held_b, got_b) + pair(
        far_held_a, far_got_a, far_held_b, far_got_b
    )
    bias = bias_in[0:1, :]
    total = jnp.sum(jnp.sum(squares, axis=0, keepdims=True) + bias * bias, axis=1, keepdims=True)
    clip_level = 0.5 * float(18 * channels * channels + channels) ** 0.5
    factor = jnp.minimum(1.0, clip_level / jnp.sqrt(total))
    factor = jnp.broadcast_to(factor, (1, channels))
    bias_out[...] = bias * factor
    spots = (bit_a, 1 - bit_a, 2 + bit_b, 3 - bit_b)

    def write(near_out, far_out):
        near = (held_a, got_a, held_b, got_b)
        far = (far_held_a, far_got_a, far_held_b, far_got_b)
        for out, refs in ((near_out, near), (far_out, far)):
            for spot, ref in zip(spots, refs):
                for at in range(0, ref.shape[0], 32):
                    out[spot, at : at + 32, :] = ref[at : at + 32, :].astype(F32) * factor

    @pl.when(core == 0)
    def _():
        write(down, up)

    @pl.when(core != 0)
    def _():
        write(up, down)


def feature_body(grads, rim_grads, right, below, cot, down_weight, out, wide, pairs, near_mat, low_mat, woven):
    tile_rows, tile_cols, channels = cot.shape
    half_rows, half_cols = tile_rows // 2, tile_cols // 2
    wide[0:half_rows, 0:half_cols, :] = grads[...].astype(F32).reshape(
        half_rows, half_cols, channels
    )
    last = lax.broadcasted_iota(jnp.int32, (half_rows, 8, channels), 1) == 0
    own = rim_grads[half_cols:, :].astype(F32).reshape(half_rows, 1, channels)
    wide[0:half_rows, 0:8, :] = jnp.where(last, own, wide[0:half_rows, 0:8, :])
    wide[0, 0:half_cols, :] = rim_grads[0:half_cols, :].astype(F32)
    aside = lax.axis_index("narrow") < lax.axis_size("narrow") - 1
    under = lax.axis_index("wide") < lax.axis_size("wide") - 1
    rim = if_any(aside, right[...].astype(F32)).reshape(half_rows, 1, channels)
    wide[0:half_rows, half_cols:, :] = jnp.where(last, rim, 0.0)
    wide[half_rows, 0:half_cols, :] = if_any(under, below[0:half_cols, :].astype(F32))
    wide[half_rows, half_cols:, :] = if_any(under & aside, below[half_cols:, :].astype(F32))
    pairs[:, :, 0:channels] = wide[:, 0:half_cols, :].astype(BF16)
    pairs[:, :, channels:] = wide[:, 1 : half_cols + 1, :].astype(BF16)
    zero = jnp.zeros((channels, channels), BF16)
    blocks = [(1, 1, None), (1, 2, 0), (2, 1, None), (2, 2, 0)]
    for at, (row_off, here, next_off) in enumerate(blocks):
        rows = slice(at * channels, (at + 1) * channels)
        near_mat[rows, 0:channels] = down_weight[row_off, here]
        near_mat[rows, channels:] = zero if next_off is None else down_weight[row_off, next_off]
    for at, (here, next_off) in enumerate([(1, None), (2, 0)]):
        rows = slice(at * channels, (at + 1) * channels)
        low_mat[rows, 0:channels] = down_weight[0, here]
        low_mat[rows, channels:] = zero if next_off is None else down_weight[0, next_off]
    step = 8
    dims = (((1,), (1,)), ((), ()))
    for start in range(0, half_rows, step):
        count = step * half_cols
        here = pairs[start : start + step].reshape(count, 2 * channels)
        lower = pairs[start + 1 : start + 1 + step].reshape(count, 2 * channels)
        near = lax.dot_general(here, near_mat[...], dims, preferred_element_type=F32)
        far = lax.dot_general(lower, low_mat[...], dims, preferred_element_type=F32)
        shape = (step, half_cols, channels)
        for row_par in range(2):
            for col_par in range(2):
                lanes = slice((2 * row_par + col_par) * channels, (2 * row_par + col_par + 1) * channels)
                value = near[:, lanes]
                if row_par:
                    value = value + far[:, col_par * channels : (col_par + 1) * channels]
                woven[:, row_par, pl.ds(col_par, half_cols, stride=2), :] = value.reshape(shape)
        span = slice(2 * start, 2 * (start + step))
        total = cot[span].astype(F32) + woven[...].reshape(2 * step, tile_cols, channels)
        out[span] = total.astype(BF16)


def turned(value, axis, steps):
    count = lax.axis_size(axis)
    return lax.ppermute(value, axis, [(at, (at + steps) % count) for at in range(count)])


def traded(value, position):
    count = lax.axis_size("wide")
    return lax.ppermute(value, "wide", [(at, at ^ (1 << position)) for at in range(count)])


def program(features, cotangent, down_weight, down_bias, up_weight):
    tile_rows, tile_cols, channels = features.shape
    half_rows, half_cols = tile_rows // 2, tile_cols // 2
    pixels = half_rows * half_cols
    taps = 9 * channels
    feat_near, cot_near, down_near, up_near, bias_near, rows, cols = call(
        edge_body,
        (
            vm(features.shape, BF16),
            vm(features.shape, BF16),
            vm(down_weight.shape, BF16),
            vm(up_weight.shape, BF16),
            vm((1, channels), F32),
            vm((2, tile_cols, channels), BF16),
            vm((2, tile_rows, channels), BF16),
        ),
        scratch=[
            pltpu.VMEM((tile_rows * 16, channels), F32),
            pltpu.SemaphoreType.DMA((5,)),
        ],
        in_specs=[ANY] * 5,
        nbytes=1 << 19,
        far=(0, 1, 2, 3, 4),
        room=8,
    )(features, cotangent, down_weight, up_weight, down_bias.reshape(1, channels))
    from_above = turned(rows, "wide", 1)
    from_left = turned(cols, "narrow", 1)
    patches = vm((half_rows, half_cols, taps), BF16)
    firsts = vm((2, tile_rows, channels), BF16)
    (
        feat_patch, cot_patch, act, grads, raw_other, raw_bias, feat_firsts, cot_firsts, up_mat
    ) = call(
        interior_body,
        (
            patches,
            patches,
            vm((pixels, channels), BF16),
            vm((pixels, channels), BF16),
            vm((taps, channels), F32),
            vm((8, channels), F32),
            firsts,
            firsts,
            vm((channels, taps), BF16),
        ),
        scratch=[
            pltpu.VMEM((half_rows, 2, tile_cols + 8, channels), F32),
            pltpu.VMEM((tile_rows * 16, channels), F32),
        ],
        n_in=5,
        flops=6 * pixels * taps * channels,
        nbytes=6 << 20,
        near=(0, 1, 2, 3, 4),
        room=12,
    )(feat_near, cot_near, down_near, bias_near, up_near)
    from_above, from_left, raw_other = lax.optimization_barrier(
        (from_above, from_left, raw_other)
    )
    pieces = half_cols + half_rows
    rim_grads, feat_rim, cot_rim, rim_act, rim_masked, other_a, other_b, bias_sum = call(
        rim_body,
        (
            vm((pieces, channels), BF16),
            vm((pieces, taps), BF16),
            vm((pieces, taps), BF16),
            vm((pieces, channels), BF16),
            vm((pieces, channels), BF16),
            vm((taps // 2 + 3 * SIDE, channels), BF16),
            vm((taps // 2, channels), BF16),
            vm((8, channels), F32),
        ),
        scratch=[
            pltpu.VMEM((tile_cols + 8, channels), F32),
            pltpu.VMEM((3, tile_rows + 8, channels), F32),
        ],
        n_in=11,
        flops=1 << 26,
        nbytes=3 << 20,
        near=tuple(range(11)),
        room=8,
    )(
        feat_patch, cot_patch, feat_firsts, cot_firsts, from_above, from_left,
        raw_other, raw_bias, up_mat, down_near, bias_near,
    )
    got_a = turned(other_a, "narrow", 1)
    got_b = turned(other_b, "narrow", 1)
    mine_a, mine_b = call(
        mine_body,
        (vm((taps // 2, channels), F32), vm((taps // 2, channels), F32)),
        n_in=8,
        flops=2 * pixels * taps * channels,
        nbytes=3 << 20,
        near=tuple(range(8)),
        room=12,
    )(feat_patch, cot_patch, act, grads, feat_rim, cot_rim, rim_act, rim_masked)
    got_a, mine_a, mine_b = lax.optimization_barrier((got_a, mine_a, mine_b))
    bits = lax.axis_size("wide").bit_length() - 1
    order_a = [1, 0, *range(2, bits)] if bits > 1 else list(range(bits))
    order_b = [0, 2, 1, *range(3, bits)] if bits > 2 else list(range(bits))
    half = taps // 4
    held_a, send_a, mine_b, rim_grads, bias_sum = call(
        functools.partial(late_body, order_a[0]),
        (
            vm((half, channels), F32),
            vm((half + SIDE, channels), BF16),
            vm((taps // 2, channels), F32),
            vm((pieces, channels), BF16),
            vm((8, channels), F32),
        ),
        scratch=[
            pltpu.VMEM((SIDE, taps), BF16),
            pltpu.VMEM((SIDE, taps), BF16),
            pltpu.VMEM((taps // 2, channels), F32),
        ],
        n_in=9,
        flops=1 << 24,
        nbytes=1 << 20,
        near=tuple(range(9)),
        room=8,
    )(other_a, got_a, mine_a, mine_b, rim_grads, down_near, bias_near, up_mat, bias_sum)
    from_right = turned(rim_grads[half_cols:], "narrow", -1)
    low = jnp.concatenate([rim_grads[:half_cols], from_right[:8]], axis=0)
    from_below = turned(low, "wide", -1)

    halvings = 1 if bits <= 3 else 2
    half = taps // 2
    held_b = mine_b
    for step in range(halvings):
        half //= 2
        if step:
            held_a, send_a, bias_sum = call(
                functools.partial(halve_body, order_a[step]),
                (
                    vm((half, channels), F32),
                    vm((half + SIDE, channels), BF16),
                    vm((8, channels), F32),
                ),
                n_in=3,
                nbytes=half * channels * 12,
                near=(0, 1, 2),
            )(held_a, got_a, bias_sum)
        held_b, send_b = call(
            functools.partial(halve_body, order_b[step]),
            (vm((half, channels), F32), vm((half, channels), BF16)),
            n_in=2,
            nbytes=half * channels * 12,
            near=(0, 1),
        )(held_b, got_b)
        got_a = traded(send_a, order_a[step])
        got_b = traded(send_b, order_b[step])
    feature_grad = call(
        feature_body,
        sds((tile_rows, tile_cols, channels), BF16),
        scratch=[
            pltpu.VMEM((half_rows + 1, half_cols + 8, channels), F32),
            pltpu.VMEM((half_rows + 1, half_cols, 2 * channels), BF16),
            pltpu.VMEM((4 * channels, 2 * channels), BF16),
            pltpu.VMEM((2 * channels, 2 * channels), BF16),
            pltpu.VMEM((8, 2, tile_cols, channels), F32),
        ],
        n_in=6,
        flops=2 * pixels * 6 * 2 * channels * channels,
        nbytes=3 << 20,
        near=(0, 1, 2, 3, 4, 5),
        room=16,
    )(grads, rim_grads, from_right, from_below, cot_near, down_near)
    for step in range(halvings, bits + 1):
        side = SIDE if step < bits else 0
        held_a, bias_sum = call(
            functools.partial(whole_body, half),
            (vm((half + side, channels), BF16), vm((8, channels), F32)),
            n_in=3,
            nbytes=half * channels * 8,
            near=(0, 1, 2),
        )(held_a, got_a, bias_sum)
        held_b = call(
            functools.partial(whole_body, half),
            vm((half, channels), BF16),
            n_in=2,
            nbytes=half * channels * 8,
            near=(0, 1),
        )(held_b, got_b)
        if step < bits:
            got_a = traded(held_a, order_a[step])
            got_b = traded(held_b, order_b[step])
            if step == bits - 1:
                got_b, feature_grad = lax.optimization_barrier((got_b, feature_grad))
    for step in reversed(range(halvings)):
        got_a = traded(held_a, order_a[step])
        got_b = traded(held_b, order_b[step])
        if step:
            half *= 2
            held_a = call(
                functools.partial(place_body, order_a[step]),
                vm((half, channels), BF16),
                n_in=2,
                near=(0, 1),
            )(held_a, got_a)
            held_b = call(
                functools.partial(place_body, order_b[step]),
                vm((half, channels), BF16),
                n_in=2,
                near=(0, 1),
            )(held_b, got_b)
    blocks = (held_a, got_a, held_b, got_b)
    far_blocks = []
    for block in blocks:
        far_blocks.append(turned(block, "narrow", 1))
    size = taps // 4
    down, up, bias_grad = call(
        functools.partial(final_body, (order_a[0], order_b[0])),
        (
            sds((4, size, channels), F32),
            sds((4, size, channels), F32),
            sds((1, channels), F32),
        ),
        n_in=9,
        nbytes=12 * taps * channels,
        near=tuple(range(9)),
        room=8,
    )(*blocks, *far_blocks, bias_sum)
    shape = (3, 3, channels, channels)
    return (feature_grad, down.reshape(shape), up.reshape(shape), bias_grad.reshape(channels))


def solution(mesh):
    return jax.shard_map(
        program,
        mesh=mesh,
        in_specs=(
            P(("groups", "wide"), "narrow", None),
            P(("groups", "wide"), "narrow", None),
            P(),
            P(),
            P(),
        ),
        out_specs=(
            P(("groups", "wide"), "narrow", None),
            P("groups", None, None, None),
            P("groups", None, None, None),
            P("groups"),
        ),
        check_vma=False,
    )
```

```python
import functools

import jax
import jax.numpy as jnp
from jax import lax
from jax.experimental import pallas as pl
from jax.experimental.pallas import tpu as pltpu
from jax.sharding import PartitionSpec as P


F32 = jnp.float32
BF16 = jnp.bfloat16
VM = pl.BlockSpec(memory_space=pltpu.VMEM)
ANY = pl.BlockSpec(memory_space=pl.ANY)
SIDE = 16


def call(body, out_shape, scratch=(), in_specs=None, n_in=0, flops=0, nbytes=0, near=(), far=(), room=4, out_specs=None):
    kernel = pl.pallas_call(
        body,
        out_shape=out_shape,
        in_specs=in_specs if in_specs is not None else [VM] * n_in,
        out_specs=out_specs or jax.tree.map(lambda _: VM, out_shape),
        scratch_shapes=list(scratch),
        compiler_params=pltpu.CompilerParams(vmem_limit_bytes=room << 20),
        cost_estimate=pl.CostEstimate(flops=flops, transcendentals=0, bytes_accessed=nbytes),
    )

    def run(*args):
        placed = [
            pltpu.with_memory_space_constraint(arg, pltpu.VMEM if at in near else pltpu.HBM)
            if at in near or at in far
            else arg
            for at, arg in enumerate(args)
        ]
        return kernel(*placed)

    return run


def vm(shape, dtype):
    return pltpu.VMEM(shape, dtype)


def sds(shape, dtype):
    return jax.ShapeDtypeStruct(shape, dtype)


def edge_body(
    feat, cot, down, up, bias, feat_near, cot_near, down_near, up_near, bias_near,
    rows, cols, wide_strip, sems,
):
    tile_rows, tile_cols, _ = feat.shape
    bulk = [
        pltpu.make_async_copy(feat, feat_near, sems.at[0]),
        pltpu.make_async_copy(cot, cot_near, sems.at[1]),
        pltpu.make_async_copy(down, down_near, sems.at[2]),
        pltpu.make_async_copy(up, up_near, sems.at[3]),
        pltpu.make_async_copy(bias, bias_near, sems.at[4]),
    ]
    for copy in bulk:
        copy.start()
    for which, near in enumerate((feat_near, cot_near)):
        bulk[which].wait()
        rows[which] = near[tile_rows - 1]
        wide_strip[...] = near[:, tile_cols - 16 :, :].astype(F32)[:, 8:, :].reshape(wide_strip.shape)
        cols[which] = wide_strip[pl.ds(7, tile_rows, stride=8), :].astype(BF16)
    for copy in bulk[2:]:
        copy.wait()


def if_any(there, value):
    return jnp.where(there, value, jnp.zeros_like(value))


def own_patches(tile, wide, strip, patch, firsts):
    rows, cols, channels = tile.shape
    half_rows, half_cols = rows // 2, cols // 2
    wide[:, :, 0:8, :] = jnp.zeros((half_rows, 2, 8, channels), F32)
    wide[:, :, 8:, :] = tile[...].astype(F32).reshape(half_rows, 2, cols, channels)
    for col_off in range(3):
        lanes = [pl.ds((3 * row_off + col_off) * channels, channels) for row_off in range(3)]
        taken = pl.ds(7 + col_off, half_cols, stride=2)
        patch[:, :, lanes[1]] = wide[:, 0, taken, :].astype(BF16)
        odd = wide[:, 1, taken, :].astype(BF16)
        patch[:, :, lanes[2]] = odd
        patch[1:, :, lanes[0]] = odd[:-1]
        patch[0, :, lanes[0]] = jnp.zeros((half_cols, channels), BF16)
    strip[...] = tile[:, 0:16, :].astype(F32).reshape(strip.shape)
    for col in range(2):
        firsts[col] = strip[pl.ds(col, rows, stride=16), :].astype(BF16)


def pointwise(pre, act_grad):
    sigm = 1.0 / (1.0 + jnp.exp(-pre))
    return pre * sigm, act_grad * sigm * (1.0 + pre * (1.0 - sigm))


def taps_of(core_is, patch, values):
    if core_is:
        return lax.dot_general(
            patch, values, (((0,), (0,)), ((), ())), preferred_element_type=F32
        )
    channels = values.shape[1]
    rows = lax.dot_general(values, patch, (((0,), (0,)), ((), ())), preferred_element_type=F32)
    return jnp.concatenate(
        [rows[:, tap * channels : (tap + 1) * channels] for tap in range(9)], axis=0
    )


def interior_body(
    feat, cot, down_weight, down_bias, up_weight,
    feat_patch, cot_patch, act, grads, raw_other, raw_bias, feat_firsts, cot_firsts, up_mat,
    wide, strip,
):
    rows, cols, channels = feat.shape
    half_rows, half_cols = rows // 2, cols // 2
    pixels = half_rows * half_cols
    taps = 9 * channels
    own_patches(feat, wide, strip, feat_patch, feat_firsts)
    own_patches(cot, wide, strip, cot_patch, cot_firsts)
    for tap in range(9):
        up_mat[:, pl.ds(tap * channels, channels)] = up_weight[tap // 3, tap % 3]
    down_mat = down_weight[...].reshape(taps, channels)
    bias_row = down_bias[...].reshape(1, channels)
    step = 8
    count = step * half_cols
    total = jnp.zeros((1, channels), F32)
    at = lax.broadcasted_iota(jnp.int32, (count, channels), 0)
    for start in range(0, half_rows, step):
        span = pl.ds(start * half_cols, count)
        feat_rows = feat_patch[start : start + step].reshape(count, taps)
        cot_rows = cot_patch[start : start + step].reshape(count, taps)
        pre = jnp.dot(feat_rows, down_mat, preferred_element_type=F32) + bias_row
        act_grad = lax.dot_general(
            cot_rows, up_mat[...], (((1,), (1,)), ((), ())), preferred_element_type=F32
        )
        inside = lax.rem(at, half_cols) > 0
        if start == 0:
            inside = inside & (at >= half_cols)
        value, grad = pointwise(pre, act_grad)
        act[span, :] = if_any(inside, value).astype(BF16)
        grad = if_any(inside, grad).astype(BF16)
        grads[span, :] = grad
        total = total + jnp.sum(grad.astype(F32), axis=0, keepdims=True)
    raw_bias[...] = jnp.broadcast_to(total, raw_bias.shape)
    core = lax.axis_index("narrow")

    @pl.when(core == 0)
    def _():
        raw_other[...] = taps_of(False, cot_patch[...].reshape(pixels, taps), act[...])

    @pl.when(core != 0)
    def _():
        raw_other[...] = taps_of(True, feat_patch[...].reshape(pixels, taps), grads[...])


def rim_patches(patch, firsts, top, left, out, line, column):
    half_rows, half_cols, taps = patch.shape
    channels = taps // 9
    above = lax.axis_index("wide") > 0
    aside = lax.axis_index("narrow") > 0
    line[0:8, :] = jnp.zeros((8, channels), F32)
    line[8:, :] = if_any(above, top[...].astype(F32))
    column[0, 0:8, :] = line[0:8, :]
    column[0, 8:, :] = if_any(aside, left[...].astype(F32))
    for col in range(2):
        column[1 + col, 0:8, :] = jnp.zeros((8, channels), F32)
        column[1 + col, 8:, :] = firsts[col].astype(F32)
    out[0:half_cols, 3 * channels :] = patch[0, :, 3 * channels :]
    first = lax.broadcasted_iota(jnp.int32, (half_cols, channels), 0) == 0
    for off in range(3):
        out[0:half_cols, off * channels : (off + 1) * channels] = line[
            pl.ds(7 + off, half_cols, stride=2), :
        ].astype(BF16)
        for col_off in range(3):
            lanes = slice((3 * off + col_off) * channels, (3 * off + col_off + 1) * channels)
            out[half_cols:, lanes] = column[
                col_off, pl.ds(7 + off, half_rows, stride=2), :
            ].astype(BF16)
    for off in (1, 2):
        lanes = slice(3 * off * channels, (3 * off + 1) * channels)
        rest = patch[0, :, lanes].astype(F32)
        halo = jnp.broadcast_to(column[0, 7 + off : 8 + off, :], rest.shape)
        out[0:half_cols, lanes] = jnp.where(first, halo, rest).astype(BF16)


def rim_body(
    feat_patch, cot_patch, feat_firsts, cot_firsts, top, left, raw_other, raw_bias,
    up_mat, down_weight, down_bias,
    rim_grads, feat_rim, cot_rim, rim_act, rim_masked, other_a, other_b, bias_part,
    line, column,
):
    _, half_cols, taps = feat_patch.shape
    channels = taps // 9
    half = taps // 2
    rim_patches(
        feat_patch, feat_firsts, top.at[0], left.at[0], feat_rim, line, column
    )
    rim_patches(cot_patch, cot_firsts, top.at[1], left.at[1], cot_rim, line, column)
    pre = jnp.dot(
        feat_rim[...], down_weight[...].reshape(taps, channels), preferred_element_type=F32
    ) + down_bias[...].reshape(1, channels)
    act_grad = lax.dot_general(
        cot_rim[...], up_mat[...], (((1,), (1,)), ((), ())), preferred_element_type=F32
    )
    value, grad = pointwise(pre, act_grad)
    at = lax.broadcasted_iota(jnp.int32, value.shape, 0)
    once = at != half_cols
    core = lax.axis_index("narrow")
    counted = once & ((at > 0) | (core == 0))
    act = if_any(counted, value).astype(BF16)
    masked = if_any(counted, grad).astype(BF16)
    rim_act[...] = act
    rim_masked[...] = masked
    full = grad.astype(BF16).astype(F32)
    rim_grads[...] = jnp.where(once, full, jnp.broadcast_to(full[0:1], full.shape)).astype(BF16)
    total = raw_bias[0:1, :] + jnp.sum(masked.astype(F32), axis=0, keepdims=True)
    coarse = total.astype(BF16)
    fine = (total - coarse.astype(F32)).astype(BF16)
    bias_part[...] = jnp.broadcast_to(coarse.astype(F32) + fine.astype(F32), bias_part.shape)
    put_side(other_a, half, coarse, fine)
    put_pixel(other_a, half + SIDE, top, feat_rim, cot_rim)

    def give(more):
        other_a[0:half, :] = (raw_other[0:half, :] + more[0:half]).astype(BF16)
        other_b[...] = (raw_other[half:, :] + more[half:]).astype(BF16)

    @pl.when(core == 0)
    def _():
        give(taps_of(False, cot_rim[...], act))

    @pl.when(core != 0)
    def _():
        give(taps_of(True, feat_rim[...], masked))


def put_pixel(out, at, top, feat_rim, cot_rim):
    _, cols, channels = top.shape
    core = lax.axis_index("narrow")
    above = lax.axis_index("wide") > 0
    row = lax.broadcasted_iota(jnp.int32, (2 * SIDE, channels), 0)
    block = jnp.zeros((2 * SIDE, channels), F32)
    for which, rim in enumerate((feat_rim, cot_rim)):
        corner = top[which, cols - 16 :, :].astype(F32)[15:16]
        corner = if_any(above & (core == 0), corner)
        block = jnp.where(row == which * SIDE, corner, block)
        for tap in range(1, 9):
            value = rim[0:16, tap * channels : (tap + 1) * channels].astype(F32)[0:1]
            value = if_any(core > 0, value)
            block = jnp.where(row == which * SIDE + tap, value, block)
    out[at : at + 2 * SIDE, :] = block.astype(BF16)


def late_body(
    own, got, mine_a, mine_b, rim_grads, down_weight, down_bias, up_mat,
    out_a, out_b, grads_out, late, feat_row, cot_row,
):
    half, channels = mine_a.shape
    taps = 2 * half
    core = lax.axis_index("narrow")
    span = slice(half + SIDE, half + 3 * SIDE)
    pixel = own[span, :].astype(F32) + got[span, :].astype(F32)
    first = lax.broadcasted_iota(jnp.int32, (SIDE, channels), 0) == 0
    for which, row in enumerate((feat_row, cot_row)):
        for tap in range(9):
            at = which * SIDE + tap
            row[:, tap * channels : (tap + 1) * channels] = if_any(
                first, jnp.broadcast_to(pixel[at : at + 1], (SIDE, channels))
            ).astype(BF16)
    pre = jnp.dot(
        feat_row[...], down_weight[...].reshape(taps, channels), preferred_element_type=F32
    ) + down_bias[...].reshape(1, channels)
    act_grad = lax.dot_general(
        cot_row[...], up_mat[...], (((1,), (1,)), ((), ())), preferred_element_type=F32
    )
    value, grad = pointwise(pre, act_grad)
    act = if_any(first, value).astype(BF16)
    grad = if_any(first, grad).astype(BF16)
    only = grad.astype(F32)[0:1]
    late[...] = jnp.broadcast_to(only, late.shape)
    half_cols = rim_grads.shape[0] // 2
    row = lax.broadcasted_iota(jnp.int32, rim_grads.shape, 0)
    ours = ((row == 0) | (row == half_cols)) & (core > 0)
    grads_out[...] = jnp.where(
        ours, jnp.broadcast_to(only, rim_grads.shape), rim_grads[...].astype(F32)
    ).astype(BF16)

    def add(more):
        out_a[...] = mine_a[...] + more[0:half]
        out_b[...] = mine_b[...] + more[half:]

    @pl.when(core == 0)
    def _():
        add(taps_of(True, feat_row[...], grad))

    @pl.when(core != 0)
    def _():
        add(taps_of(False, cot_row[...], act))


def mine_body(
    feat_patch, cot_patch, act, grads, feat_rim, cot_rim, rim_act, rim_masked, mine_a, mine_b
):
    half_rows, half_cols, taps = feat_patch.shape
    pixels = half_rows * half_cols
    half = taps // 2
    core = lax.axis_index("narrow")

    def keep(which, patch, values, rim_patch, rim_values):
        total = taps_of(which, patch[...].reshape(pixels, taps), values[...])
        total = total + taps_of(which, rim_patch[...], rim_values[...])
        mine_a[...] = total[0:half]
        mine_b[...] = total[half:]

    @pl.when(core == 0)
    def _():
        keep(True, feat_patch, grads, feat_rim, rim_masked)

    @pl.when(core != 0)
    def _():
        keep(False, cot_patch, act, cot_rim, rim_act)


def put_side(out, at, coarse, fine):
    channels = out.shape[1]
    row = lax.broadcasted_iota(jnp.int32, (SIDE, channels), 0)
    block = jnp.where(row == 0, coarse.astype(F32), jnp.where(row == 1, fine.astype(F32), 0.0))
    out[at : at + SIDE, :] = block.astype(BF16)


def take_side(ref, at):
    block = ref[at : at + SIDE, :].astype(F32)
    return block[0:1] + block[1:2]


def bit_of(position):
    return lax.rem(lax.shift_right_logical(lax.axis_index("wide"), jnp.int32(position)), 2)


def joined_bias(bias_in, got, size, out, sent, at, late=None):
    total = bias_in[0:1, :] + take_side(got, size)
    if late is not None:
        total = total + late[0:1, :]
    coarse = total.astype(BF16)
    fine = (total - coarse.astype(F32)).astype(BF16)
    out[...] = jnp.broadcast_to(coarse.astype(F32) + fine.astype(F32), out.shape)
    if sent is not None:
        put_side(sent, at, coarse, fine)


def split(position, held, got, base, size, keep, send):
    half = size // 2
    bit = bit_of(position)
    near = pl.ds(pl.multiple_of(base + bit * half, 16), half)
    away = pl.ds(pl.multiple_of(base + (1 - bit) * half, 16), half)
    send[0:half, :] = (held[away, :] + got[away, :].astype(F32)).astype(BF16)
    keep[...] = held[near, :] + got[near, :].astype(F32)


def halve_body(position, held, got, *rest):
    size = held.shape[0]
    if len(rest) > 3:
        bias_in, *late, keep, send, bias_out = rest
        joined_bias(bias_in, got, size, bias_out, send, size // 2, *late)
    else:
        keep, send = rest
    split(position, held, got, 0, size, keep, send)


def whole_body(size, held, got, *rest):
    send = rest[-2] if len(rest) == 3 else rest[-1]
    send[0:size, :] = (held[0:size, :].astype(F32) + got[0:size, :].astype(F32)).astype(BF16)
    if len(rest) == 3:
        bias_in, _, bias_out = rest
        joined_bias(bias_in, got, size, bias_out, send if send.shape[0] > size else None, size)


def place_body(position, held, got, out):
    place(position, held, got, out, 0)


def place(position, held, got, out, base):
    size = held.shape[0]
    bit = bit_of(position)
    out[pl.ds(pl.multiple_of(base + bit * size, 16), size), :] = held[...]
    out[pl.ds(pl.multiple_of(base + (1 - bit) * size, 16), size), :] = got[...]


def final_body(
    positions, held_a, got_a, held_b, got_b, far_held_a, far_got_a, far_held_b, far_got_b, bias_in,
    down, up, bias_out,
):
    channels = held_a.shape[1]
    core = lax.axis_index("narrow")
    bit_a, bit_b = bit_of(positions[0]), bit_of(positions[1])

    def square(ref):
        total = jnp.zeros((32, channels), F32)
        for at in range(0, ref.shape[0], 32):
            block = ref[at : at + 32, :].astype(F32)
            total = total + block * block
        return total

    def pair(one, two, three, four):
        return (square(one) + square(two)) + (square(three) + square(four))

    squares = pair(held_a, got_a, held_b, got_b) + pair(
        far_held_a, far_got_a, far_held_b, far_got_b
    )
    bias = bias_in[0:1, :]
    total = jnp.sum(jnp.sum(squares, axis=0, keepdims=True) + bias * bias, axis=1, keepdims=True)
    clip_level = 0.5 * float(18 * channels * channels + channels) ** 0.5
    factor = jnp.minimum(1.0, clip_level / jnp.sqrt(total))
    factor = jnp.broadcast_to(factor, (1, channels))
    bias_out[...] = bias * factor
    spots = (bit_a, 1 - bit_a, 2 + bit_b, 3 - bit_b)

    def write(near_out, far_out):
        near = (held_a, got_a, held_b, got_b)
        far = (far_held_a, far_got_a, far_held_b, far_got_b)
        for out, refs in ((near_out, near), (far_out, far)):
            for spot, ref in zip(spots, refs):
                for at in range(0, ref.shape[0], 32):
                    out[spot, at : at + 32, :] = ref[at : at + 32, :].astype(F32) * factor

    @pl.when(core == 0)
    def _():
        write(down, up)

    @pl.when(core != 0)
    def _():
        write(up, down)


def feature_body(grads, rim_grads, right, below, cot, down_weight, out, wide, pairs, near_mat, low_mat, woven):
    tile_rows, tile_cols, channels = cot.shape
    half_rows, half_cols = tile_rows // 2, tile_cols // 2
    wide[0:half_rows, 0:half_cols, :] = grads[...].astype(F32).reshape(
        half_rows, half_cols, channels
    )
    last = lax.broadcasted_iota(jnp.int32, (half_rows, 8, channels), 1) == 0
    own = rim_grads[half_cols:, :].astype(F32).reshape(half_rows, 1, channels)
    wide[0:half_rows, 0:8, :] = jnp.where(last, own, wide[0:half_rows, 0:8, :])
    wide[0, 0:half_cols, :] = rim_grads[0:half_cols, :].astype(F32)
    aside = lax.axis_index("narrow") < lax.axis_size("narrow") - 1
    under = lax.axis_index("wide") < lax.axis_size("wide") - 1
    rim = if_any(aside, right[...].astype(F32)).reshape(half_rows, 1, channels)
    wide[0:half_rows, half_cols:, :] = jnp.where(last, rim, 0.0)
    wide[half_rows, 0:half_cols, :] = if_any(under, below[0:half_cols, :].astype(F32))
    wide[half_rows, half_cols:, :] = if_any(under & aside, below[half_cols:, :].astype(F32))
    pairs[:, :, 0:channels] = wide[:, 0:half_cols, :].astype(BF16)
    pairs[:, :, channels:] = wide[:, 1 : half_cols + 1, :].astype(BF16)
    zero = jnp.zeros((channels, channels), BF16)
    blocks = [(1, 1, None), (1, 2, 0), (2, 1, None), (2, 2, 0)]
    for at, (row_off, here, next_off) in enumerate(blocks):
        rows = slice(at * channels, (at + 1) * channels)
        near_mat[rows, 0:channels] = down_weight[row_off, here]
        near_mat[rows, channels:] = zero if next_off is None else down_weight[row_off, next_off]
    for at, (here, next_off) in enumerate([(1, None), (2, 0)]):
        rows = slice(at * channels, (at + 1) * channels)
        low_mat[rows, 0:channels] = down_weight[0, here]
        low_mat[rows, channels:] = zero if next_off is None else down_weight[0, next_off]
    step = 8
    dims = (((1,), (1,)), ((), ()))
    for start in range(0, half_rows, step):
        count = step * half_cols
        here = pairs[start : start + step].reshape(count, 2 * channels)
        lower = pairs[start + 1 : start + 1 + step].reshape(count, 2 * channels)
        near = lax.dot_general(here, near_mat[...], dims, preferred_element_type=F32)
        far = lax.dot_general(lower, low_mat[...], dims, preferred_element_type=F32)
        shape = (step, half_cols, channels)
        for row_par in range(2):
            for col_par in range(2):
                lanes = slice((2 * row_par + col_par) * channels, (2 * row_par + col_par + 1) * channels)
                value = near[:, lanes]
                if row_par:
                    value = value + far[:, col_par * channels : (col_par + 1) * channels]
                woven[:, row_par, pl.ds(col_par, half_cols, stride=2), :] = value.reshape(shape)
        span = slice(2 * start, 2 * (start + step))
        total = cot[span].astype(F32) + woven[...].reshape(2 * step, tile_cols, channels)
        out[span] = total.astype(BF16)


def turned(value, axis, steps):
    count = lax.axis_size(axis)
    return lax.ppermute(value, axis, [(at, (at + steps) % count) for at in range(count)])


def traded(value, position):
    count = lax.axis_size("wide")
    return lax.ppermute(value, "wide", [(at, at ^ (1 << position)) for at in range(count)])


def program(features, cotangent, down_weight, down_bias, up_weight):
    tile_rows, tile_cols, channels = features.shape
    half_rows, half_cols = tile_rows // 2, tile_cols // 2
    pixels = half_rows * half_cols
    taps = 9 * channels
    feat_near, cot_near, down_near, up_near, bias_near, rows, cols = call(
        edge_body,
        (
            vm(features.shape, BF16),
            vm(features.shape, BF16),
            vm(down_weight.shape, BF16),
            vm(up_weight.shape, BF16),
            vm((1, channels), F32),
            vm((2, tile_cols, channels), BF16),
            vm((2, tile_rows, channels), BF16),
        ),
        scratch=[
            pltpu.VMEM((tile_rows * 8, channels), F32),
            pltpu.SemaphoreType.DMA((5,)),
        ],
        in_specs=[ANY] * 5,
        nbytes=1 << 19,
        far=(0, 1, 2, 3, 4),
        room=8,
    )(features, cotangent, down_weight, up_weight, down_bias.reshape(1, channels))
    from_above = turned(rows, "wide", 1)
    from_left = turned(cols, "narrow", 1)
    patches = vm((half_rows, half_cols, taps), BF16)
    firsts = vm((2, tile_rows, channels), BF16)
    (
        feat_patch, cot_patch, act, grads, raw_other, raw_bias, feat_firsts, cot_firsts, up_mat
    ) = call(
        interior_body,
        (
            patches,
            patches,
            vm((pixels, channels), BF16),
            vm((pixels, channels), BF16),
            vm((taps, channels), F32),
            vm((8, channels), F32),
            firsts,
            firsts,
            vm((channels, taps), BF16),
        ),
        scratch=[
            pltpu.VMEM((half_rows, 2, tile_cols + 8, channels), F32),
            pltpu.VMEM((tile_rows * 16, channels), F32),
        ],
        n_in=5,
        flops=6 * pixels * taps * channels,
        nbytes=6 << 20,
        near=(0, 1, 2, 3, 4),
        room=12,
    )(feat_near, cot_near, down_near, bias_near, up_near)
    from_above, from_left, raw_other = lax.optimization_barrier(
        (from_above, from_left, raw_other)
    )
    pieces = half_cols + half_rows
    rim_grads, feat_rim, cot_rim, rim_act, rim_masked, other_a, other_b, bias_sum = call(
        rim_body,
        (
            vm((pieces, channels), BF16),
            vm((pieces, taps), BF16),
            vm((pieces, taps), BF16),
            vm((pieces, channels), BF16),
            vm((pieces, channels), BF16),
            vm((taps // 2 + 3 * SIDE, channels), BF16),
            vm((taps // 2, channels), BF16),
            vm((8, channels), F32),
        ),
        scratch=[
            pltpu.VMEM((tile_cols + 8, channels), F32),
            pltpu.VMEM((3, tile_rows + 8, channels), F32),
        ],
        n_in=11,
        flops=1 << 26,
        nbytes=3 << 20,
        near=tuple(range(11)),
        room=8,
    )(
        feat_patch, cot_patch, feat_firsts, cot_firsts, from_above, from_left,
        raw_other, raw_bias, up_mat, down_near, bias_near,
    )
    got_a = turned(other_a, "narrow", 1)
    mine_a, mine_b = call(
        mine_body,
        (vm((taps // 2, channels), F32), vm((taps // 2, channels), F32)),
        n_in=8,
        flops=2 * pixels * taps * channels,
        nbytes=3 << 20,
        near=tuple(range(8)),
        room=12,
    )(feat_patch, cot_patch, act, grads, feat_rim, cot_rim, rim_act, rim_masked)
    other_b, mine_a = lax.optimization_barrier((other_b, mine_a))
    got_b = turned(other_b, "narrow", 1)
    got_a, mine_a, mine_b = lax.optimization_barrier((got_a, mine_a, mine_b))
    mine_a, mine_b, rim_grads, late = call(
        late_body,
        (
            vm((taps // 2, channels), F32),
            vm((taps // 2, channels), F32),
            vm((pieces, channels), BF16),
            vm((8, channels), F32),
        ),
        scratch=[pltpu.VMEM((SIDE, taps), BF16), pltpu.VMEM((SIDE, taps), BF16)],
        n_in=8,
        flops=1 << 24,
        nbytes=1 << 20,
        near=tuple(range(8)),
        room=8,
    )(other_a, got_a, mine_a, mine_b, rim_grads, down_near, bias_near, up_mat)
    from_right = turned(rim_grads[half_cols:], "narrow", -1)
    low = jnp.concatenate([rim_grads[:half_cols], from_right[:8]], axis=0)
    from_below = turned(low, "wide", -1)

    bits = lax.axis_size("wide").bit_length() - 1
    order_a = [1, 0, *range(2, bits)] if bits > 1 else list(range(bits))
    order_b = [0, 2, 1, *range(3, bits)] if bits > 2 else list(range(bits))
    halvings = 1 if bits <= 3 else 2
    half = taps // 2
    held_a, held_b = mine_a, mine_b
    for step in range(halvings):
        half //= 2
        held_a, send_a, bias_sum = call(
            functools.partial(halve_body, order_a[step]),
            (vm((half, channels), F32), vm((half + SIDE, channels), BF16), vm((8, channels), F32)),
            n_in=3 if step else 4,
            nbytes=half * channels * 12,
            near=(0, 1, 2) if step else (0, 1, 2, 3),
        )(held_a, got_a, bias_sum, *(() if step else (late,)))
        held_b, send_b = call(
            functools.partial(halve_body, order_b[step]),
            (vm((half, channels), F32), vm((half, channels), BF16)),
            n_in=2,
            nbytes=half * channels * 12,
            near=(0, 1),
        )(held_b, got_b)
        got_a = traded(send_a, order_a[step])
        got_b = traded(send_b, order_b[step])
    feature_grad = call(
        feature_body,
        sds((tile_rows, tile_cols, channels), BF16),
        scratch=[
            pltpu.VMEM((half_rows + 1, half_cols + 8, channels), F32),
            pltpu.VMEM((half_rows + 1, half_cols, 2 * channels), BF16),
            pltpu.VMEM((4 * channels, 2 * channels), BF16),
            pltpu.VMEM((2 * channels, 2 * channels), BF16),
            pltpu.VMEM((8, 2, tile_cols, channels), F32),
        ],
        n_in=6,
        flops=2 * pixels * 6 * 2 * channels * channels,
        nbytes=3 << 20,
        near=(0, 1, 2, 3, 4, 5),
        room=16,
    )(grads, rim_grads, from_right, from_below, cot_near, down_near)
    for step in range(halvings, bits + 1):
        side = SIDE if step < bits else 0
        held_a, bias_sum = call(
            functools.partial(whole_body, half),
            (vm((half + side, channels), BF16), vm((8, channels), F32)),
            n_in=3,
            nbytes=half * channels * 8,
            near=(0, 1, 2),
        )(held_a, got_a, bias_sum)
        held_b = call(
            functools.partial(whole_body, half),
            vm((half, channels), BF16),
            n_in=2,
            nbytes=half * channels * 8,
            near=(0, 1),
        )(held_b, got_b)
        if step < bits:
            got_a = traded(held_a, order_a[step])
            got_b = traded(held_b, order_b[step])
            if step == bits - 1:
                got_b, feature_grad = lax.optimization_barrier((got_b, feature_grad))
    for step in reversed(range(halvings)):
        got_a = traded(held_a, order_a[step])
        got_b = traded(held_b, order_b[step])
        if step:
            half *= 2
            held_a = call(
                functools.partial(place_body, order_a[step]),
                vm((half, channels), BF16),
                n_in=2,
                near=(0, 1),
            )(held_a, got_a)
            held_b = call(
                functools.partial(place_body, order_b[step]),
                vm((half, channels), BF16),
                n_in=2,
                near=(0, 1),
            )(held_b, got_b)
    blocks = (held_a, got_a, held_b, got_b)
    far_blocks = []
    for block in blocks:
        far_blocks.append(turned(block, "narrow", 1))
    size = taps // 4
    down, up, bias_grad = call(
        functools.partial(final_body, (order_a[0], order_b[0])),
        (
            sds((4, size, channels), F32),
            sds((4, size, channels), F32),
            sds((1, channels), F32),
        ),
        n_in=9,
        nbytes=12 * taps * channels,
        near=tuple(range(9)),
        room=8,
    )(*blocks, *far_blocks, bias_sum)
    shape = (3, 3, channels, channels)
    return (feature_grad, down.reshape(shape), up.reshape(shape), bias_grad.reshape(channels))


def solution(mesh):
    return jax.shard_map(
        program,
        mesh=mesh,
        in_specs=(
            P(("groups", "wide"), "narrow", None),
            P(("groups", "wide"), "narrow", None),
            P(),
            P(),
            P(),
        ),
        out_specs=(
            P(("groups", "wide"), "narrow", None),
            P("groups", None, None, None),
            P("groups", None, None, None),
            P("groups"),
        ),
        check_vma=False,
    )
```
